32 devices in a mesh: groups: 2 (over y), ctx: 16 (over z, x, core).
Axes of the slice: x: 2, y: 2, z: 4, core: 2. Of those that a mesh axis runs over, the one named last changes fastest.
Arguments:
- normed_input: bfloat16 [2048, 8192], P(('groups', 'ctx')), parts along dimension 0, may hold values from -5 to 5
- query_base: bfloat16 [2048, 4096], P(('groups', 'ctx')), parts along dimension 0, may hold values from -6 to 6
- key_base: bfloat16 [2048, 512], P(('groups', 'ctx')), parts along dimension 0, may hold values from -6 to 6
- value_base: bfloat16 [2048, 512], P(('groups', 'ctx')), parts along dimension 0, may hold values from -4 to 4
- adapter_pool: bfloat16 [16, 2686976], P('ctx'), may hold values from -1 to 1
- stretch_adapter: int32 [4], P('groups'), parts along dimension 0, may hold values from 0 to 15
- adapter_owner: int32 [16], replicated, may hold values from 0 to 15, each once
Outputs:
- attended: bfloat16 [2048, 4096], P(('groups', 'ctx')), parts along dimension 0
- out_delta: bfloat16 [2048, 8192], P(('groups', 'ctx')), parts along dimension 0
The draws below stay inside these ranges and needn't reach their ends.
There are 2 independent parts, one for each index of `groups`. The reference program is written for one: setup_inputs(seed, part) draws one part's arguments, and reference() takes and returns one part's arrays. A program takes and returns all parts, laid end to end along the dimension named above; an argument that names none is the same for every part. Nothing has to cross between parts.
All inputs are finite; a program needn't handle non-finite values.
Results may differ from the reference program's by a relative error of at most 0.018.
Values may be sent and summed in bfloat16 or wider, within the bound.
A program may use at most 192 MiB of HBM per device.

```python
import math
import jax
import jax.numpy as jnp
import numpy as np
from jax import lax

D = 8192
QH = 32
KEYVALUE_HEADS = 4
HEAD_SIZE = 128
ADAPTER_RANK = 64
BLOCK_TOKENS = 512
SEQ = 1024
NCHUNK = 2
ADAPTERS = 16
QKV_POOL = 1900544
POOL = 2686976


def draw_query_base(key, part):
    return jnp.clip(jax.random.normal(jax.random.fold_in(key, 11), (SEQ, QH * HEAD_SIZE), jnp.float32), -4.0, 4.0).astype(jnp.bfloat16)


def draw_key_base(key, part):
    return jnp.clip(jax.random.normal(jax.random.fold_in(key, 13), (SEQ, KEYVALUE_HEADS * HEAD_SIZE), jnp.float32), -4.0, 4.0).astype(jnp.bfloat16)


def draw_adapter_pool(key, part):
    raw_values = jnp.clip(jax.random.normal(jax.random.fold_in(key, 17), (ADAPTERS, POOL), jnp.float32), -4.0, 4.0)
    column = jnp.arange(POOL)
    bound_one = 3 * ADAPTER_RANK * D
    bound_two = bound_one + ADAPTER_RANK * QH * HEAD_SIZE
    bound_three = bound_two + 2 * ADAPTER_RANK * KEYVALUE_HEADS * HEAD_SIZE
    bound_four = bound_three + ADAPTER_RANK * QH * HEAD_SIZE
    in_keyval = (column - bound_two) % (2 * KEYVALUE_HEADS * HEAD_SIZE)
    column_scale = jnp.where(column < bound_one, D ** (-0.5), jnp.where(column < bound_two, 0.01, jnp.where(column < bound_three, jnp.where(in_keyval < KEYVALUE_HEADS * HEAD_SIZE, 0.01, 0.06), jnp.where(column < bound_four, (QH * HEAD_SIZE) ** (-0.5), 0.25))))
    return (raw_values * column_scale.astype(jnp.float32)[None, :]).astype(jnp.bfloat16)


def block_levels(stream_key, extent, split, low, top_value):
    gain = 1.0
    for dim, parts in split:
        draws = jax.random.uniform(jax.random.fold_in(jax.random.fold_in(stream_key, 6), dim), (parts,), jnp.float32, low / len(split), top_value / len(split))
        gain = gain * jnp.repeat(jnp.exp(draws), extent[dim] // parts).reshape((-1,) + (1,) * (len(extent) - 1 - dim))
    return gain


def rank_bounds(amount, lean):
    portions = [(1 << 20) // math.isqrt(standing ** lean) + 1 for standing in range(1, amount + 1)]
    spread = 1 + sum(portions) // (1 << 30)
    return np.cumsum(np.array([max(1, weight // spread) for weight in portions]))


def ranked(stream_key, shape, amount, slope):
    table = rank_bounds(amount, slope)
    ticket = jax.random.randint(jax.random.fold_in(stream_key, 1), shape, 0, int(table[amount - 1]))
    rank = jnp.searchsorted(jnp.asarray(table, jnp.int32), ticket, side="right")
    return jax.random.permutation(jax.random.fold_in(stream_key, 2), amount)[rank].astype(jnp.int32)


def scatter_about(rng, shape, spread, reach, shards=(), kind=jnp.bfloat16):
    values = jax.random.normal(rng, shape, jnp.float32) * spread
    if len(shards) > 0:
        values = block_levels(rng, shape, shards, -0.22, 0.18) * values
    return jnp.clip(values, min=-reach, max=reach).astype(kind)


def setup_inputs(seed: int = 0, part: int = 0) -> dict:
    arg_keys = jax.random.split(jax.random.key(seed), 8)
    own_keys = jax.random.split(jax.random.fold_in(arg_keys[7], part), 8)
    return {
        "normed_input": scatter_about(own_keys[0], (SEQ, D), 1.0, 5.0, ((0, 16),)),
        "query_base": draw_query_base(jax.random.fold_in(jax.random.fold_in(arg_keys[7], part), 71), part),
        "key_base": draw_key_base(jax.random.fold_in(jax.random.fold_in(arg_keys[7], part), 71), part),
        "value_base": scatter_about(own_keys[3], (SEQ, KEYVALUE_HEADS * HEAD_SIZE), 1.0, 4.0, ((0, 16),)),
        "adapter_pool": draw_adapter_pool(jax.random.fold_in(arg_keys[7], 71), part),
        "stretch_adapter": ranked(own_keys[5], (NCHUNK,), ADAPTERS, 2),
        "adapter_owner": jax.random.permutation(arg_keys[6], ADAPTERS).astype(jnp.int32),
    }


adapter_scale = 2.0
rope_base = 500000.0
mask_floor = -1.0e30


def rotate(delta, token_positions, heads):
    half_dim = HEAD_SIZE // 2
    frequency = rope_base ** (-(jnp.arange(half_dim, dtype=jnp.float32) * 2.0) / HEAD_SIZE)
    angle = token_positions.astype(jnp.float32)[:, None] * frequency[None, :]
    cosine = jnp.cos(angle)[:, None, :]
    sine_part = jnp.sin(angle)[:, None, :]
    shaped = delta.reshape(delta.shape[0], heads, HEAD_SIZE)
    first_half = shaped[..., :half_dim]
    second_half = shaped[..., half_dim:]
    joined = jnp.concatenate([first_half * cosine - second_half * sine_part, second_half * cosine + first_half * sine_part], -1)
    return joined.reshape(delta.shape[0], heads * HEAD_SIZE)


def adapter_inputs(hidden_state_rows, query_row_block, key_row_block, value_row_block, projection_piece, token_positions):
    split_one = D * 3 * ADAPTER_RANK
    split_two = split_one + ADAPTER_RANK * QH * HEAD_SIZE
    down_qkv = projection_piece[:split_one].reshape(D, 3 * ADAPTER_RANK)
    query_up_weight = projection_piece[split_one:split_two].reshape(ADAPTER_RANK, QH * HEAD_SIZE)
    keyvalue_up_weight = projection_piece[split_two:].reshape(ADAPTER_RANK, 2 * KEYVALUE_HEADS * HEAD_SIZE)
    narrow_product = jnp.dot(hidden_state_rows, down_qkv, preferred_element_type=jnp.float32).astype(jnp.bfloat16)
    query_correction = adapter_scale * jnp.dot(narrow_product[:, :ADAPTER_RANK], query_up_weight, preferred_element_type=jnp.float32)
    key_correction = adapter_scale * jnp.dot(narrow_product[:, ADAPTER_RANK:2 * ADAPTER_RANK], keyvalue_up_weight[:, :KEYVALUE_HEADS * HEAD_SIZE], preferred_element_type=jnp.float32)
    value_correction = adapter_scale * jnp.dot(narrow_product[:, 2 * ADAPTER_RANK:], keyvalue_up_weight[:, KEYVALUE_HEADS * HEAD_SIZE:], preferred_element_type=jnp.float32)
    queries = (query_row_block.astype(jnp.float32) + rotate(query_correction, token_positions, QH)).astype(jnp.bfloat16)
    new_keys = (key_row_block.astype(jnp.float32) + rotate(key_correction, token_positions, KEYVALUE_HEADS)).astype(jnp.bfloat16)
    new_values = (value_row_block.astype(jnp.float32) + value_correction).astype(jnp.bfloat16)
    return queries, new_keys, new_values


def output_delta(attended_rows, out_part):
    down_out = out_part[:QH * HEAD_SIZE * ADAPTER_RANK].reshape(QH * HEAD_SIZE, ADAPTER_RANK)
    raised_output = out_part[QH * HEAD_SIZE * ADAPTER_RANK:].reshape(ADAPTER_RANK, D)
    narrow_product = jnp.dot(attended_rows, down_out, preferred_element_type=jnp.float32).astype(jnp.bfloat16)
    return (adapter_scale * jnp.dot(narrow_product, raised_output, preferred_element_type=jnp.float32)).astype(jnp.bfloat16)


def reference(normed_input, query_base, key_base, value_base, adapter_pool, stretch_adapter, adapter_owner):
    adapter_ids = jnp.arange(ADAPTERS, dtype=jnp.int32)
    slots = jnp.sum(jnp.where(stretch_adapter[:, None] == adapter_ids[None, :], adapter_owner[None, :], 0), axis=1).astype(jnp.int32)

    def one_stretch(stretch_index):
        starting_row = stretch_index * BLOCK_TOKENS
        token_positions = starting_row + jnp.arange(BLOCK_TOKENS, dtype=jnp.int32)
        pool_row = lax.dynamic_index_in_dim(adapter_pool, slots[stretch_index], 0, keepdims=False)
        return adapter_inputs(lax.dynamic_slice_in_dim(normed_input, starting_row, BLOCK_TOKENS, 0),
                           lax.dynamic_slice_in_dim(query_base, starting_row, BLOCK_TOKENS, 0),
                           lax.dynamic_slice_in_dim(key_base, starting_row, BLOCK_TOKENS, 0),
                           lax.dynamic_slice_in_dim(value_base, starting_row, BLOCK_TOKENS, 0),
                           pool_row[:QKV_POOL], token_positions)

    stretch_list = jnp.arange(NCHUNK, dtype=jnp.int32)
    queries, all_keys, all_values = lax.map(one_stretch, stretch_list)
    queries = queries.reshape(SEQ, QH * HEAD_SIZE)
    key_heads = all_keys.reshape(SEQ, KEYVALUE_HEADS, HEAD_SIZE).astype(jnp.float32)
    value_heads = all_values.reshape(SEQ, KEYVALUE_HEADS, HEAD_SIZE).astype(jnp.float32)
    group_size = QH // KEYVALUE_HEADS
    block_rows = min(512, SEQ)
    key_pos = jnp.arange(SEQ, dtype=jnp.int32)

    def attend(block_index):
        starting_row = block_index * block_rows
        block_q = lax.dynamic_slice_in_dim(queries, starting_row, block_rows, 0)
        head_q = block_q.reshape(block_rows, KEYVALUE_HEADS, group_size, HEAD_SIZE).transpose(1, 2, 0, 3).reshape(KEYVALUE_HEADS, group_size * block_rows, HEAD_SIZE)
        query_pos = jnp.tile(starting_row + jnp.arange(block_rows, dtype=jnp.int32), group_size)
        scores = jnp.einsum("hqd,khd->hqk", head_q.astype(jnp.float32), key_heads) * (HEAD_SIZE ** -0.5)
        allowed = (query_pos[:, None] >= key_pos[None, :])[None]
        row_max = jnp.max(jnp.where(allowed, scores, mask_floor), axis=-1)
        weights = jnp.where(allowed, jnp.exp(scores - row_max[..., None]), 0.0)
        total = jnp.sum(weights, axis=-1)
        rounded = lax.optimization_barrier(weights.astype(jnp.bfloat16))
        summed = jnp.einsum("hqk,khd->hqd", rounded.astype(jnp.float32), value_heads)
        result = summed / total[..., None]
        return result.reshape(KEYVALUE_HEADS, group_size, block_rows, HEAD_SIZE).transpose(2, 0, 1, 3).reshape(block_rows, QH * HEAD_SIZE).astype(jnp.bfloat16)

    attended = lax.map(attend, jnp.arange(SEQ // block_rows, dtype=jnp.int32)).reshape(SEQ, QH * HEAD_SIZE)

    def out_stretch(stretch_index):
        starting_row = stretch_index * BLOCK_TOKENS
        pool_row = lax.dynamic_index_in_dim(adapter_pool, slots[stretch_index], 0, keepdims=False)
        return output_delta(lax.dynamic_slice_in_dim(attended, starting_row, BLOCK_TOKENS, 0), pool_row[QKV_POOL:])

    out_delta = lax.map(out_stretch, stretch_list).reshape(SEQ, D)
    return attended, out_delta
```

```python
from functools import partial
import math

import jax
import jax.numpy as jnp
from jax import lax
from jax.experimental import pallas as pl
from jax.experimental.pallas import tpu as pltpu
from jax.sharding import PartitionSpec as P

D = 8192
QH = 32
KEYVALUE_HEADS = 4
HEAD_SIZE = 128
ADAPTER_RANK = 64
BLOCK_TOKENS = 512
QKV_POOL = 1900544


adapter_scale = 2.0
rope_base = 500000.0
mask_floor = -1e30


LANES = 128
MESH = pl.DeviceIdType.MESH
ON_CHIP = pl.BlockSpec(memory_space=pltpu.VMEM)
ANYWHERE = pl.BlockSpec(memory_space=pl.ANY)
SCALARS = pl.BlockSpec(memory_space=pltpu.SMEM)


def remote(src, dst, send_sem, recv_sem, group, ctx):
    return pltpu.make_async_remote_copy(
        src_ref=src,
        dst_ref=dst,
        send_sem=send_sem,
        recv_sem=recv_sem,
        device_id=(group, ctx),
        device_id_type=MESH,
    )


def place_adapter_kernel(
    groups, cubes, cube, down_size,
    owner_ref, stretch_ref, x_ref, pool_ref,
    x_out, down_out, rest_out,
    down_flat, rest_flat, down_source, rest_source,
    down_rows, rest_rows, down_send, rest_send, down_land, rest_land,
    stretch_land, table,
    s_flat, s_cube, r_cube, s_far, r_far, s_tree, r_tree, s_own, s_row, r_row, s_table,
):
    group = lax.axis_index("groups")
    ctx = lax.axis_index("ctx")
    inner = ctx % cube
    outer = ctx // cube
    home = group * cubes + outer
    kinds = groups * cubes
    width = x_out.shape[2] // groups
    down_piece = down_flat.shape[2]
    rest_piece = rest_flat.shape[2]

    def read_piece(row, k):
        piece = (rest_piece, down_piece)[row]
        start = (group * cube + (inner ^ k)) * piece + (down_size, 0)[row]
        return pltpu.make_async_copy(
            pool_ref.at[:, pl.ds(pl.multiple_of(start, LANES), piece)],
            (rest_flat, down_flat)[row].at[k],
            s_flat.at[row, k],
        )

    for row in range(2):
        for k in reversed(range(cube)):
            read_piece(row, k).start()

    barrier = pltpu.get_barrier_semaphore()
    for k in range(1, cube):
        pl.semaphore_signal(
            barrier, inc=1, device_id=(group, outer * cube + (inner ^ k)), device_id_type=MESH
        )
    for k in range(1, kinds):
        there = home ^ k
        pl.semaphore_signal(
            barrier,
            inc=1,
            device_id=(there // cubes, (there % cubes) * cube + inner),
            device_id_type=MESH,
        )
    pl.semaphore_wait(barrier, cube - 1 + kinds - 1)
    row_copies = []
    for step in range(1, groups):
        copy = remote(
            stretch_ref, stretch_land.at[step], s_row.at[step], r_row.at[step], group ^ step, ctx
        )
        copy.start()
        row_copies.append(copy)

    def columns(part, owner):
        return pl.ds(pl.multiple_of((part * cube + owner) * width, width), width)

    def cube_copy(row, k):
        peer = inner ^ k
        return remote(
            (rest_source, down_source)[row].at[k], (rest_rows, down_rows)[row].at[inner],
            s_cube.at[row, k], r_cube.at[row, k], group, outer * cube + peer,
        )

    def dense(row, k):
        flat = (rest_flat, down_flat)[row][k].astype(jnp.float32)
        return flat.reshape(-1, LANES).astype(jnp.bfloat16)

    def x_copy(part, k):
        peer = inner ^ k
        return remote(
            x_ref.at[:, columns(part, peer)],
            x_out.at[inner, :, pl.ds(part * width, width)],
            s_cube.at[2 + part, k], r_cube.at[2 + part, k],
            group, outer * cube + peer,
        )

    for row, (source, rows) in enumerate(((rest_source, rest_rows), (down_source, down_rows))):

        def spread(step, carry, row=row, source=source):
            k = cube - 1 - step
            read_piece(row, k).wait()
            source[k] = dense(row, k)
            cube_copy(row, k).start()
            return carry

        lax.fori_loop(0, cube - 1, spread, 0)
        read_piece(row, 0).wait()
        rows[inner] = dense(row, 0)

    to_table = [pltpu.make_async_copy(stretch_ref, table.at[0], s_table.at[0])]
    to_table[0].start()
    for step, copy in zip(range(1, groups), row_copies):
        copy.wait_recv()
        move = pltpu.make_async_copy(stretch_land.at[step], table.at[step], s_table.at[step])
        move.start()
        to_table.append(move)
    for move in to_table:
        move.wait()

    def slot_of(k):
        return owner_ref[table[k // cubes, 0, outer ^ (k % cubes)]]

    def chosen(part):
        return (part * cubes + lax.div(slot_of(0), cube)) ^ home

    owns = []
    for part in range(groups):
        own = pltpu.make_async_copy(
            x_ref.at[:, columns(part, inner)],
            x_out.at[inner, :, pl.ds(part * width, width)],
            s_own.at[part],
        )
        own.start()
        owns.append(own)

    far = []
    for row, (rows, outgoing, landing) in enumerate(
        ((rest_rows, rest_send, rest_land), (down_rows, down_send, down_land))
    ):
        for k in range(1, cube):
            cube_copy(row, k).wait_recv()
        coming = []
        for k in range(1, kinds):
            there = home ^ k
            outgoing[k] = rows[lax.rem(slot_of(k), cube)]
            copy = remote(
                outgoing.at[k], landing.at[k], s_far.at[row, k], r_far.at[row, k],
                there // cubes, (there % cubes) * cube + inner,
            )
            copy.start()
            coming.append(copy)
        landing[0] = rows[lax.rem(slot_of(0), cube)]
        far.append(coming)

    for copy in far[0]:
        copy.wait_recv()
    for part in range(groups):
        rest_out[part, inner] = rest_land[chosen(part)]
    tree = {}
    have = [[0] for _ in range(groups)]
    levels = cube.bit_length() - 1
    orders = []
    for part in range(groups):
        order = [1 << level for level in reversed(range(levels))]
        if part % 2:
            order[:2] = order[1::-1]
        orders.append(order)
    for stage in range(levels):
        for part in range(groups):
            bit = orders[part][stage]
            before = orders[part][stage - 1] if stage else 0
            for k in have[part]:
                if k & before:
                    tree[k, part].wait_recv()
            new = []
            for k in have[part]:
                slot = rest_out.at[part, inner ^ k]
                copy = remote(
                    slot, slot, s_tree.at[part, k ^ bit], r_tree.at[part, k ^ bit],
                    group, outer * cube + (inner ^ bit),
                )
                copy.start()
                tree[k ^ bit, part] = copy
                new.append(k ^ bit)
            have[part] = have[part] + new
        if stage == 0:
            for part in range(groups):
                for k in reversed(range(1, cube)):
                    x_copy(part, k).start()

    for copy in far[1]:
        copy.wait_recv()
    for part in range(groups):
        down_out[part] = down_land[chosen(part)]
    for (k, part), copy in tree.items():
        if k & orders[part][-1]:
            copy.wait_recv()
    for own in owns:
        own.wait()
    for part in range(groups):
        for k in range(1, cube):
            x_copy(part, k).wait_recv()
            x_copy(part, k).wait_send()
    for row in range(2):
        for k in range(1, cube):
            cube_copy(row, k).wait_send()
    for copy in row_copies + far[0] + far[1] + list(tree.values()):
        copy.wait_send()


def place_adapter(groups, cubes, cube, down_size, owner, stretch_row, x, pool):
    kinds = groups * cubes
    tokens, depth = x.shape
    down_piece = down_size // (groups * cube)
    rest_piece = (pool.shape[1] - down_size) // (groups * cube)
    down_shape = (down_piece // LANES, LANES)
    rest_shape = (rest_piece // LANES, LANES)
    bf16 = jnp.bfloat16
    dma = pltpu.SemaphoreType.DMA
    return pl.pallas_call(
        partial(place_adapter_kernel, groups, cubes, cube, down_size),
        out_shape=(
            jax.ShapeDtypeStruct((cube, tokens, depth // cube), bf16),
            jax.ShapeDtypeStruct((groups,) + down_shape, bf16),
            jax.ShapeDtypeStruct((groups, cube) + rest_shape, bf16),
        ),
        in_specs=[SCALARS, ON_CHIP, ON_CHIP, pl.BlockSpec(memory_space=pl.ANY)],
        out_specs=(ON_CHIP, ON_CHIP, ON_CHIP),
        scratch_shapes=[
            pltpu.VMEM((cube, 1, down_piece), bf16),
            pltpu.VMEM((cube, 1, rest_piece), bf16),
            pltpu.VMEM((cube,) + down_shape, bf16),
            pltpu.VMEM((cube,) + rest_shape, bf16),
            pltpu.VMEM((cube,) + down_shape, bf16),
            pltpu.VMEM((cube,) + rest_shape, bf16),
            pltpu.VMEM((kinds,) + down_shape, bf16),
            pltpu.VMEM((kinds,) + rest_shape, bf16),
            pltpu.VMEM((kinds,) + down_shape, bf16),
            pltpu.VMEM((kinds,) + rest_shape, bf16),
            pltpu.VMEM((groups,) + stretch_row.shape, jnp.int32),
            pltpu.SMEM((groups,) + stretch_row.shape, jnp.int32),
            dma((2, cube)),
            dma((2 + groups, cube)),
            dma((2 + groups, cube)),
            dma((2, kinds)),
            dma((2, kinds)),
            dma((groups, cube)),
            dma((groups, cube)),
            dma((groups,)),
            dma((groups,)),
            dma((groups,)),
            dma((groups,)),
        ],
        compiler_params=pltpu.CompilerParams(
            collective_id=0, has_side_effects=True, vmem_limit_bytes=60 * 1024 * 1024
        ),
    )(owner, stretch_row, x, pool)


def keyval_kernel(
    cube, count,
    x_any, w_ref, rest_any, query_ref, key_ref, value_ref, cos_ref, sin_ref,
    query_out, out_ref,
    x_ref, up_ref, s_in, wide, total, outgoing, landing, s_sem, r_sem, s_all, r_all,
):
    group = lax.axis_index("groups")
    ctx = lax.axis_index("ctx")
    inner = ctx % cube
    outer = ctx // cube
    levels = count.bit_length() - 1
    x_in = pltpu.make_async_copy(x_any, x_ref, s_in.at[0])
    x_in.start()
    up_in = pltpu.make_async_copy(
        rest_any.at[pl.ds(0, up_ref.shape[0])], up_ref, s_in.at[1]
    )
    up_in.start()
    barrier = pltpu.get_barrier_semaphore()
    apart = list(range(1, cube)) + [1 << n for n in range(levels) if 1 << n >= cube]
    for k in apart:
        pl.semaphore_signal(barrier, inc=1, device_id=(group, ctx ^ k), device_id_type=MESH)
    _, tokens, depth = x_ref.shape
    x_in.wait()
    product = jnp.dot(
        x_ref[...].reshape(cube * tokens, depth), w_ref[...], preferred_element_type=jnp.float32
    ).reshape(cube, tokens, w_ref.shape[1])
    total[...] = product
    outgoing[...] = product.astype(jnp.bfloat16)
    pl.semaphore_wait(barrier, len(apart))
    copies = []
    for k in range(1, cube):
        peer = inner ^ k
        copy = remote(
            outgoing.at[peer], landing.at[k], s_sem.at[k], r_sem.at[k], group, outer * cube + peer
        )
        copy.start()
        copies.append(copy)
    up_in.wait()
    wide[...] = up_ref[...].astype(jnp.float32)
    result = total[inner]
    for k, copy in zip(range(1, cube), copies):
        copy.wait_recv()
        result = result + landing[k].astype(jnp.float32)
    low = result.astype(jnp.bfloat16)
    half = HEAD_SIZE // 2
    query_rows = ADAPTER_RANK * QH
    kinds = 2 * KEYVALUE_HEADS
    for j in range(2 * KEYVALUE_HEADS):
        first = ADAPTER_RANK * (1 if j < KEYVALUE_HEADS else 2)
        delta = adapter_scale * jnp.dot(
            low[:, first : first + ADAPTER_RANK],
            wide[pl.ds(query_rows + j, ADAPTER_RANK, stride=kinds), :].astype(jnp.bfloat16),
            preferred_element_type=jnp.float32
        )
        base_ref = key_ref if j < KEYVALUE_HEADS else value_ref
        head = j % KEYVALUE_HEADS
        if j < KEYVALUE_HEADS:
            swapped = jnp.concatenate([delta[:, half:], delta[:, :half]], axis=1)
            delta = delta * cos_ref[...] + swapped * sin_ref[...]
        base = base_ref[:, head * HEAD_SIZE : (head + 1) * HEAD_SIZE].astype(jnp.float32)
        out_ref[ctx, :, j * HEAD_SIZE : (j + 1) * HEAD_SIZE] = (base + delta).astype(jnp.bfloat16)

    def query_head(head):
        up = wide[pl.ds(head, ADAPTER_RANK, stride=QH), :].astype(jnp.bfloat16)
        delta = adapter_scale * jnp.dot(
            low[:, :ADAPTER_RANK], up, preferred_element_type=jnp.float32
        )
        swapped = jnp.concatenate([delta[:, half:], delta[:, :half]], axis=1)
        delta = delta * cos_ref[...] + swapped * sin_ref[...]
        base = query_ref[:, head * HEAD_SIZE : (head + 1) * HEAD_SIZE].astype(jnp.float32)
        shared = QH // KEYVALUE_HEADS
        query_out[
            head // shared, (head % shared) * tokens : (head % shared + 1) * tokens, :
        ] = (base + delta).astype(jnp.bfloat16)

    kv_width = KEYVALUE_HEADS * HEAD_SIZE
    far_first = [1 << level for level in reversed(range(levels))]
    orders = (far_first, [2] + [bit for bit in far_first if bit != 2])
    have = [[0], [0]]
    moved = {}
    done = 0
    for stage in range(levels):
        for part in range(2):
            bit = orders[part][stage]
            before = orders[part][stage - 1] if stage else 0
            new = []
            for k in have[part]:
                if k & before:
                    moved[k, part].wait_recv()
                slot = out_ref.at[ctx ^ k, :, pl.ds(part * kv_width, kv_width)]
                copy = remote(
                    slot, slot, s_all.at[part, k ^ bit], r_all.at[part, k ^ bit], group, ctx ^ bit
                )
                copy.start()
                moved[k ^ bit, part] = copy
                new.append(k ^ bit)
            have[part] = have[part] + new
        until = QH * (stage + 1) // levels
        for head in range(done, until):
            query_head(head)
        done = until
    for (k, part), copy in moved.items():
        if k & orders[part][-1]:
            copy.wait_recv()
    for copy in copies + list(moved.values()):
        copy.wait_send()


def keyval(cube, count, x, w, rest, query_rows, key_rows, value_rows, cosine, sine):
    _, tokens, _ = x.shape
    shape = (cube, tokens, w.shape[1])
    up_rows = ADAPTER_RANK * (QH + 2 * KEYVALUE_HEADS)
    dma = pltpu.SemaphoreType.DMA
    return pl.pallas_call(
        partial(keyval_kernel, cube, count),
        out_shape=(
            jax.ShapeDtypeStruct(
                (KEYVALUE_HEADS, QH // KEYVALUE_HEADS * tokens, HEAD_SIZE), jnp.bfloat16
            ),
            jax.ShapeDtypeStruct(
                (count, tokens, 2 * KEYVALUE_HEADS * HEAD_SIZE), jnp.bfloat16
            ),
        ),
        in_specs=[ANYWHERE, ON_CHIP, ANYWHERE] + [ON_CHIP] * 5,
        out_specs=(ON_CHIP, ON_CHIP),
        scratch_shapes=[
            pltpu.VMEM(x.shape, jnp.bfloat16),
            pltpu.VMEM((up_rows, LANES), jnp.bfloat16),
            dma((2,)),
            pltpu.VMEM((up_rows, LANES), jnp.float32),
            pltpu.VMEM(shape, jnp.float32),
            pltpu.VMEM(shape, jnp.bfloat16),
            pltpu.VMEM(shape, jnp.bfloat16),
            dma((cube,)),
            dma((cube,)),
            dma((2, count)),
            dma((2, count)),
        ],
        compiler_params=pltpu.CompilerParams(
            collective_id=1, has_side_effects=True, vmem_limit_bytes=40 * 1024 * 1024
        ),
    )(x, w, rest, query_rows, key_rows, value_rows, cosine, sine)


def attend_kernel(
    step_keys, queries, kv_ref, rest_any,
    attended_ref, delta_ref,
    rest_ref, s_in, wide, permuted, run_max, run_sum, run_acc,
):
    tokens = attended_ref.shape[0]
    ctx = lax.axis_index("ctx")
    heads = QH // KEYVALUE_HEADS
    rows = heads * tokens
    half = HEAD_SIZE // 2
    query_rows = ADAPTER_RANK * QH
    raise_start = QH * half
    rest_in = pltpu.make_async_copy(
        rest_any.at[pl.ds(query_rows + 2 * ADAPTER_RANK * KEYVALUE_HEADS, rest_ref.shape[0])],
        rest_ref,
        s_in,
    )
    rest_in.start()
    first = ctx * tokens
    steps = (first + tokens + step_keys - 1) // step_keys
    row = lax.broadcasted_iota(jnp.int32, (rows, step_keys), 0)
    query_pos = first + lax.rem(row, tokens)
    key_off = lax.broadcasted_iota(jnp.int32, (rows, step_keys), 1)
    source = lax.broadcasted_iota(jnp.int32, (HEAD_SIZE, HEAD_SIZE), 0)
    target = lax.broadcasted_iota(jnp.int32, (HEAD_SIZE, HEAD_SIZE), 1)
    wanted = jnp.where(target < half, 2 * target, 2 * (target - half) + 1)
    shuffle = jnp.where(source == wanted, 1.0, 0.0).astype(jnp.bfloat16)
    for group in range(KEYVALUE_HEADS):
        run_max[...] = jnp.full_like(run_max, mask_floor)
        run_sum[...] = jnp.zeros_like(run_sum)
        run_acc[...] = jnp.zeros_like(run_acc)
        key_cols = slice(group * HEAD_SIZE, (group + 1) * HEAD_SIZE)
        value_first = (KEYVALUE_HEADS + group) * HEAD_SIZE

        def advance(step, carry):
            start = pl.multiple_of(step * step_keys, step_keys)
            keys = kv_ref[pl.ds(start, step_keys), key_cols]
            values = kv_ref[pl.ds(start, step_keys), value_first : value_first + HEAD_SIZE]
            scores = lax.dot_general(
                queries[group], keys, (((1,), (1,)), ((), ())),
                preferred_element_type=jnp.float32,
            ) * HEAD_SIZE ** (-0.5)
            scores = jnp.where(query_pos >= key_off + start, scores, mask_floor)
            new_max = jnp.maximum(run_max[...], jnp.max(scores, axis=1, keepdims=True))
            weights = jnp.exp(scores - new_max)
            rescale = jnp.exp(run_max[...] - new_max)
            run_sum[...] = run_sum[...] * rescale + jnp.sum(weights, axis=1, keepdims=True)
            run_acc[...] = run_acc[...] * rescale + jnp.dot(
                weights.astype(jnp.bfloat16), values, preferred_element_type=jnp.float32
            )
            run_max[...] = new_max
            return carry

        lax.fori_loop(0, steps, advance, 0)
        result = (run_acc[...] / run_sum[...]).astype(jnp.bfloat16)
        mixed = jnp.dot(result, shuffle, preferred_element_type=jnp.float32).astype(jnp.bfloat16)
        for j in range(heads):
            head = group * heads + j
            cols = slice(head * HEAD_SIZE, (head + 1) * HEAD_SIZE)
            attended_ref[:, cols] = result[j * tokens : (j + 1) * tokens]
            permuted[:, cols] = mixed[j * tokens : (j + 1) * tokens]
    rest_in.wait()
    wide[...] = rest_ref[raise_start:, :].astype(jnp.float32)
    narrow = jnp.zeros((tokens, ADAPTER_RANK), jnp.float32)
    for head in range(QH):
        block = rest_ref[head * half : (head + 1) * half, :]
        weight = jnp.concatenate([block[:, :half], block[:, half:]], axis=0)
        narrow = narrow + jnp.dot(
            permuted[:, head * HEAD_SIZE : (head + 1) * HEAD_SIZE],
            weight,
            preferred_element_type=jnp.float32,
        )
    narrow = narrow.astype(jnp.bfloat16)
    blocks = D // LANES
    for j in range(blocks):
        up = wide[pl.ds(j, ADAPTER_RANK, stride=blocks), :].astype(jnp.bfloat16)
        delta_ref[:, j * LANES : (j + 1) * LANES] = (
            adapter_scale * jnp.dot(narrow, up, preferred_element_type=jnp.float32)
        ).astype(jnp.bfloat16)


def attend(queries, kv, rest):
    rows = queries.shape[1]
    tokens = rows // (QH // KEYVALUE_HEADS)
    out_rows = ADAPTER_RANK * (QH * HEAD_SIZE + D) // LANES
    return pl.pallas_call(
        partial(attend_kernel, math.gcd(kv.shape[0], 1024)),
        out_shape=(
            jax.ShapeDtypeStruct((tokens, QH * HEAD_SIZE), jnp.bfloat16),
            jax.ShapeDtypeStruct((tokens, D), jnp.bfloat16),
        ),
        in_specs=[ON_CHIP, ON_CHIP, ANYWHERE],
        out_specs=(ON_CHIP, ON_CHIP),
        scratch_shapes=[
            pltpu.VMEM((out_rows, LANES), jnp.bfloat16),
            pltpu.SemaphoreType.DMA,
            pltpu.VMEM((ADAPTER_RANK * D // LANES, LANES), jnp.float32),
            pltpu.VMEM((tokens, QH * HEAD_SIZE), jnp.bfloat16),
            pltpu.VMEM((rows, 1), jnp.float32),
            pltpu.VMEM((rows, 1), jnp.float32),
            pltpu.VMEM((rows, HEAD_SIZE), jnp.float32),
        ],
        compiler_params=pltpu.CompilerParams(vmem_limit_bytes=56 * 1024 * 1024),
    )(queries, kv, rest)


PLANE = 4
DOWN_CHUNKS = 8
INNER_CHUNKS = 2
EARLY_CHUNKS = 4
OUT_CHUNKS = 2
FAR, NEAR, MID, BACK, CROSS, WIDE, PAIR, PAIR2 = range(8)


def section_rows():
    down = 3 * ADAPTER_RANK * D // LANES
    inner = ADAPTER_RANK * (QH + 2 * KEYVALUE_HEADS) * HEAD_SIZE // LANES
    outer = ADAPTER_RANK * (QH * HEAD_SIZE + D) // LANES
    return down, inner, outer


def item_table(slices):
    items = []
    first = 0
    for rows, chunks in zip(section_rows(), (DOWN_CHUNKS, 1, OUT_CHUNKS)):
        piece = rows // slices
        for chunk in range(chunks):
            items.append((first + chunk * (piece // chunks), piece, piece // chunks))
        first += rows
    return items


def fused_kernel(
    items,
    owner_ref, stretch_ref, x_any, pool_any, query_ref, key_ref, value_ref, cos_ref, sin_ref,
    attended_ref, delta_ref,
    flat, source, held, first_out, second_out, far_in, near_in, mid_in, cross_out, final,
    acts, spread_w, packed_a, packed_b, weights, total, low_out, low_in, wide_in, wide_out, queries, kv, permuted,
    run_max, run_sum, run_acc, row_out, row_in, table,
    s_flat, s_plane, r_plane, s_move, r_move, s_acts, r_acts, s_own, s_row, r_row, s_table,
    s_low, r_low, s_keys, r_keys,
):
    group = lax.axis_index("groups")
    ctx = lax.axis_index("ctx")
    lane = ctx % PLANE
    level = ctx // PLANE
    half_of = level // 2
    is_end = (level == 0) | (level == 3)
    is_inner = (level == 1) | (level == 2)
    tokens = x_any.shape[0]
    count = len(items)
    down_items = list(range(DOWN_CHUNKS))
    in_item = DOWN_CHUNKS
    end_items = down_items[:-INNER_CHUNKS]
    inner_items = down_items[-INNER_CHUNKS:]
    order = down_items[:EARLY_CHUNKS] + [in_item] + down_items[EARLY_CHUNKS:]
    out_items = list(range(DOWN_CHUNKS + 1, count))

    def read_piece(i, k):
        first, piece, rows = items[i]
        begin = (first + (group * PLANE + (lane ^ k)) * piece) * LANES
        return pltpu.make_async_copy(
            pool_any.at[:, pl.ds(pl.multiple_of(begin, LANES), rows * LANES)],
            flat[i].at[k],
            s_flat.at[i, k],
        )

    for i in range(count):
        for k in reversed(range(PLANE)):
            read_piece(i, k).start()

    def dense(i, k):
        return flat[i][k].astype(jnp.float32).reshape(-1, LANES).astype(jnp.bfloat16)

    def prepare(i):
        def step(n, carry):
            k = PLANE - 1 - n
            read_piece(i, k).wait()
            source[i][k] = dense(i, k)
            return carry

        lax.fori_loop(0, PLANE - 1, step, 0)
        read_piece(i, 0).wait()
        held[i][lane] = dense(i, 0)

    barrier = pltpu.get_barrier_semaphore()
    greeted = (1, 2, 3, 4, 5, 6, 7, 12)
    for k in greeted:
        pl.semaphore_signal(barrier, inc=1, device_id=(group, ctx ^ k), device_id_type=MESH)
    pl.semaphore_signal(barrier, inc=1, device_id=(group ^ 1, ctx), device_id_type=MESH)
    mine_row = lax.broadcasted_iota(jnp.int32, row_out.shape, 1)
    row_out[...] = jnp.where(mine_row == 0, stretch_ref[0], stretch_ref[1])
    for i in order[:2]:
        prepare(i)
    pl.semaphore_wait(barrier, len(greeted) + 1)

    row_copy = remote(row_out, row_in, s_row, r_row, group ^ 1, ctx)
    row_copy.start()
    own_row = pltpu.make_async_copy(row_out, table.at[0], s_table.at[0])
    own_row.start()

    def plane_copy(i, k):
        return remote(
            source[i].at[k], held[i].at[lane], s_plane.at[i, k], r_plane.at[i, k], group, ctx ^ k
        )

    def scatter(i):
        for k in reversed(range(1, PLANE)):
            plane_copy(i, k).start()

    def slot(which, part):
        return owner_ref[table[which, 0, part]]

    def mine(which, part, where):
        return lax.div(slot(which, part), PLANE) == where

    def own_candidate(i, which, part):
        return held[i][lax.rem(slot(which, part), PLANE)]

    def move(i, kind):
        if kind == FAR:
            src, dst, there = first_out[i], far_in[i], (group, ctx ^ PLANE)
        elif kind == NEAR:
            src, dst, there = second_out[i], near_in[i], (group, ctx ^ PLANE)
        elif kind == MID:
            src, dst, there = first_out[i], mid_in[i], (group, ctx ^ (3 * PLANE))
        elif kind == BACK:
            src, dst, there = second_out[i], far_in[i], (group, ctx ^ PLANE)
        elif kind == CROSS:
            place = final[i].at[group] if i < in_item else final[i].at[lane, group]
            src, dst, there = cross_out[i], place, (group ^ 1, ctx)
        elif kind == WIDE:
            src = dst = final[i].at[lane]
            there = (group, ctx ^ 2)
        elif kind == PAIR:
            src = dst = final[i].at[lane]
            there = (group, ctx ^ 1)
        else:
            src = dst = final[i].at[lane ^ 2]
            there = (group, ctx ^ 1)
        return remote(src, dst, s_move.at[i, kind], r_move.at[i, kind], *there)

    def landed(i):
        for k in range(1, PLANE):
            plane_copy(i, k).wait_recv()

    def end_send(i):
        landed(i)
        for which in range(2):
            first_out[i][which] = own_candidate(i, which, 1 - half_of)
        move(i, FAR).start()
        if i not in end_items:
            for which in range(2):
                second_out[i][which] = own_candidate(i, which, half_of)
            move(i, NEAR).start()

    def settle(i, other_value, own_value):
        cross_out[i][...] = other_value
        move(i, CROSS).start()
        if i < in_item:
            final[i][group] = own_value
        else:
            final[i][lane, group] = own_value

    def end_settle(i):
        move(i, BACK).wait_recv()

        def value(which):
            return jnp.where(
                mine(which, half_of, level), own_candidate(i, which, half_of), far_in[i][which]
            )

        settle(i, value(1), value(0))

    def inner_across(i):
        landed(i)
        move(i, FAR).wait_recv()
        for which in range(2):
            first_out[i][which] = jnp.where(
                mine(which, 1 - half_of, level),
                own_candidate(i, which, 1 - half_of),
                far_in[i][which],
            )
        move(i, MID).start()

    def inner_back(i):
        move(i, MID).wait_recv()
        for which in range(2):
            second_out[i][which] = jnp.where(
                mine(which, half_of, level),
                own_candidate(i, which, half_of),
                mid_in[i][which],
            )
        if i not in inner_items:
            move(i, BACK).start()

    def inner_settle(i):
        move(i, NEAR).wait_recv()

        def value(which):
            return jnp.where(
                mine(which, half_of, level ^ 1), near_in[i][which], second_out[i][which]
            )

        settle(i, value(1), value(0))

    def gather_wide(i):
        move(i, CROSS).wait_recv()
        move(i, WIDE).start()
        move(i, PAIR).start()

    def gather_pair(i):
        move(i, WIDE).wait_recv()
        move(i, PAIR2).start()

    def gathered(i):
        move(i, PAIR).wait_recv()
        move(i, PAIR2).wait_recv()

    strip = D // (2 * PLANE)
    inner_width = strip * INNER_CHUNKS // DOWN_CHUNKS
    end_width = strip - inner_width

    def acts_copy(part, k, to_end):
        width = end_width if to_end else inner_width
        begin = (part * PLANE + (lane ^ (k % PLANE))) * strip + (0 if to_end else end_width)
        src = x_any.at[:, pl.ds(pl.multiple_of(begin, LANES), width)]
        dst = acts.at[part, k // PLANE * PLANE + lane, :, pl.ds(0, width)]
        if k == 0:
            return pltpu.make_async_copy(src, dst, s_own.at[part])
        return remote(src, dst, s_acts.at[part, k], r_acts.at[part, k], group, ctx ^ k)

    def acts_send(ks):
        @pl.when(is_end)
        def _():
            for k in ks:
                for part in range(2):
                    acts_copy(part, k, k < PLANE).start()

        @pl.when(is_inner)
        def _():
            for k in ks:
                for part in range(2):
                    acts_copy(part, k, k >= PLANE).start()

    def acts_landed(to_end):
        for part in range(2):
            acts_copy(part, 0, to_end).wait()
            for k in range(1, 2 * PLANE):
                acts_copy(part, k, to_end).wait_recv()

    def convert(i):
        move(i, CROSS).wait_recv()
        pairs = 2 * final[i].shape[1] // 3
        third = pairs // 2
        half = LANES // 2
        row = (i - (inner_items[0] if i in inner_items else 0)) * pairs
        for part in range(2):
            spread_w[...] = final[i][part].astype(jnp.float32)
            first = spread_w[pl.ds(0, third, stride=3), :]
            second = spread_w[pl.ds(1, third, stride=3), :]
            last = spread_w[pl.ds(2, third, stride=3), :]
            packed_a[pl.ds(0, third, stride=2), :] = first
            packed_b[pl.ds(0, third, stride=2), :] = second
            packed_a[pl.ds(1, third, stride=2), :] = jnp.concatenate(
                [second[:, half:], last[:, :half]], axis=1
            )
            packed_b[pl.ds(1, third, stride=2), :] = jnp.concatenate(
                [last[:, half:], last[:, :half]], axis=1
            )
            weights[part, row : row + pairs, 0:LANES] = packed_a[...].astype(jnp.bfloat16)
            weights[part, row : row + pairs, LANES : 2 * LANES] = packed_b[...].astype(jnp.bfloat16)

    def product(width):
        sum_now = None
        for part in range(2):
            chunk = acts[part, :, :, 0:width].reshape(2 * PLANE * tokens, width)
            term = jnp.dot(chunk, weights[part, 0:width, :], preferred_element_type=jnp.float32)
            sum_now = term if sum_now is None else sum_now + term
        total[...] = sum_now.reshape(2 * PLANE, tokens, 2 * LANES)

    acts_send((0, 4, 5))
    scatter(order[0])
    scatter(order[1])
    for i in order[2:]:
        prepare(i)
        scatter(i)
    acts_send((1, 2, 3, 6, 7))
    row_copy.wait_recv()
    own_row.wait()
    other_row = pltpu.make_async_copy(row_in, table.at[1], s_table.at[1])
    other_row.start()
    other_row.wait()
    for i in out_items:
        prepare(i)
        scatter(i)
    lag = 5

    @pl.when(is_end)
    def _():
        for n in range(len(order) + lag):
            if n < len(order):
                end_send(order[n])
            if n >= lag and order[n - lag] not in inner_items:
                end_settle(order[n - lag])
            if n > lag and order[n - lag - 1] in end_items:
                convert(order[n - lag - 1])
        acts_landed(True)
        product(end_width)

    @pl.when(is_inner)
    def _():
        for n in range(len(order) + 3):
            if n < len(order):
                inner_across(order[n])
            if 0 <= n - 1 < len(order):
                inner_back(order[n - 1])
            if 0 <= n - 2 < len(order) and order[n - 2] not in end_items:
                inner_settle(order[n - 2])
            if 0 <= n - 3 < len(order) and order[n - 3] in inner_items:
                convert(order[n - 3])
        acts_landed(False)
        product(inner_width)

    def low_copy(k):
        return remote(
            low_out.at[k // PLANE * PLANE + (lane ^ (k % PLANE))], low_in.at[k],
            s_low.at[k], r_low.at[k], group, ctx ^ k,
        )

    low_out[...] = total[...].astype(jnp.bfloat16)
    for k in reversed(range(1, 2 * PLANE)):
        low_copy(k).start()

    gather_wide(in_item)

    @pl.when(is_end)
    def _():
        end_send(out_items[0])

    result = total[lane]
    gather_pair(in_item)
    for k in range(1, 2 * PLANE):
        low_copy(k).wait_recv()
        result = result + low_in[k].astype(jnp.float32)
    low = result.astype(jnp.bfloat16)
    gathered(in_item)
    in_rows = items[in_item][2]
    for part in range(2):
        for owner in range(PLANE):
            j = part * PLANE + owner
            wide_in[j * in_rows : (j + 1) * in_rows, :] = final[in_item][owner, part].astype(
                jnp.float32
            )

    half = HEAD_SIZE // 2
    query_rows = ADAPTER_RANK * QH
    kinds = 2 * KEYVALUE_HEADS
    for j in range(kinds):
        first = ADAPTER_RANK * (1 if j < KEYVALUE_HEADS else 2)
        delta = adapter_scale * jnp.dot(
            low[:, first : first + ADAPTER_RANK],
            wide_in[pl.ds(query_rows + j, ADAPTER_RANK, stride=kinds), :].astype(jnp.bfloat16),
            preferred_element_type=jnp.float32
        )
        base_ref = key_ref if j < KEYVALUE_HEADS else value_ref
        head = j % KEYVALUE_HEADS
        if j < KEYVALUE_HEADS:
            swapped = jnp.concatenate([delta[:, half:], delta[:, :half]], axis=1)
            delta = delta * cos_ref[...] + swapped * sin_ref[...]
        base = base_ref[:, head * HEAD_SIZE : (head + 1) * HEAD_SIZE].astype(jnp.float32)
        kv[ctx, :, j * HEAD_SIZE : (j + 1) * HEAD_SIZE] = (base + delta).astype(jnp.bfloat16)

    def query_head(head):
        up = wide_in[pl.ds(head, ADAPTER_RANK, stride=QH), :].astype(jnp.bfloat16)
        delta = adapter_scale * jnp.dot(
            low[:, :ADAPTER_RANK], up, preferred_element_type=jnp.float32
        )
        swapped = jnp.concatenate([delta[:, half:], delta[:, :half]], axis=1)
        delta = delta * cos_ref[...] + swapped * sin_ref[...]
        base = query_ref[:, head * HEAD_SIZE : (head + 1) * HEAD_SIZE].astype(jnp.float32)
        shared = QH // KEYVALUE_HEADS
        queries[
            head // shared, (head % shared) * tokens : (head % shared + 1) * tokens, :
        ] = (base + delta).astype(jnp.bfloat16)

    def keys_copy(n, kind):
        place = kv.at[ctx - PLANE * n]
        if kind == 0:
            return remote(
                place, place, s_keys.at[n, 0], r_keys.at[n + 1, 0], group, ctx + PLANE
            )
        if kind == 3:
            place = kv.at[(ctx ^ 2) - PLANE * n]
        return remote(
            place, place, s_keys.at[n, kind], r_keys.at[n, kind], group, ctx ^ (2 if kind == 1 else 1)
        )

    def keys_kick(n):
        @pl.when(level >= n)
        def _():
            if n > 0:
                place = kv.at[ctx - PLANE * n]
                pltpu.make_async_remote_copy(
                    src_ref=place, dst_ref=place, send_sem=s_keys.at[n - 1, 0],
                    recv_sem=r_keys.at[n, 0], device_id=(group, ctx - PLANE), device_id_type=MESH,
                ).wait_recv()
            if n < 3:

                @pl.when(level < 3)
                def _():
                    keys_copy(n, 0).start()

            keys_copy(n, 1).start()
            keys_copy(n, 2).start()

    def keys_relay(n):
        @pl.when(level >= n)
        def _():
            keys_copy(n, 1).wait_recv()
            keys_copy(n, 3).start()

    def keys_drain(n):
        @pl.when(level >= n)
        def _():
            if n < 3:

                @pl.when(level < 3)
                def _():
                    keys_copy(n, 0).wait_send()

            for kind in (1, 2, 3):
                keys_copy(n, kind).wait_send()

    heads = QH // KEYVALUE_HEADS
    rows = heads * tokens
    keys_count = PLANE * tokens
    source_lane = lax.broadcasted_iota(jnp.int32, (HEAD_SIZE, HEAD_SIZE), 0)
    target_lane = lax.broadcasted_iota(jnp.int32, (HEAD_SIZE, HEAD_SIZE), 1)
    wanted = jnp.where(target_lane < half, 2 * target_lane, 2 * (target_lane - half) + 1)
    shuffle = jnp.where(source_lane == wanted, 1.0, 0.0).astype(jnp.bfloat16)
    factor = HEAD_SIZE ** (-0.5) * math.log2(math.e)

    def attend_block(n):
        @pl.when(level >= n)
        def _():
            keys_copy(n, 2).wait_recv()
            keys_copy(n, 3).wait_recv()
            first = PLANE * (level - n)
            for head in range(KEYVALUE_HEADS):
                keys = kv[pl.ds(first, PLANE), :, head * HEAD_SIZE : (head + 1) * HEAD_SIZE]
                value_first = (KEYVALUE_HEADS + head) * HEAD_SIZE
                values = kv[pl.ds(first, PLANE), :, value_first : value_first + HEAD_SIZE]
                keys = keys.reshape(keys_count, HEAD_SIZE)
                values = values.reshape(keys_count, HEAD_SIZE)
                scores = lax.dot_general(
                    queries[head], keys, (((1,), (1,)), ((), ())), preferred_element_type=jnp.float32
                )
                if n == 0:
                    query_pos = lane * tokens + lax.rem(
                        lax.broadcasted_iota(jnp.int32, (rows, keys_count), 0), tokens
                    )
                    key_pos = lax.broadcasted_iota(jnp.int32, (rows, keys_count), 1)
                    scores = jnp.where(query_pos >= key_pos, scores, mask_floor)
                top = jnp.max(scores, axis=1, keepdims=True)
                if n > 0:
                    top = jnp.maximum(top, run_max[head])
                weights = jnp.exp2((scores - top) * factor)
                norm = jnp.sum(weights, axis=1, keepdims=True)
                summed = jnp.dot(
                    weights.astype(jnp.bfloat16), values, preferred_element_type=jnp.float32
                )
                if n > 0:
                    rescale = jnp.exp2((run_max[head] - top) * factor)
                    norm = norm + run_sum[head] * rescale
                    summed = summed + run_acc[head] * rescale
                run_max[head] = top
                run_sum[head] = norm
                run_acc[head] = summed

    keys_kick(0)

    @pl.when(is_end)
    def _():
        end_send(out_items[1])

    @pl.when(is_inner)
    def _():
        inner_across(out_items[0])

    for head in range(QH // 2):
        query_head(head)
    keys_relay(0)
    keys_kick(1)
    for head in range(QH // 2, QH):
        query_head(head)
    keys_relay(1)
    attend_block(0)
    keys_kick(2)

    @pl.when(is_inner)
    def _():
        inner_back(out_items[0])
        inner_across(out_items[1])

    keys_relay(2)
    attend_block(1)
    keys_kick(3)

    @pl.when(is_end)
    def _():
        end_settle(out_items[0])

    @pl.when(is_inner)
    def _():
        inner_settle(out_items[0])
        inner_back(out_items[1])

    keys_relay(3)
    attend_block(2)
    gather_wide(out_items[0])

    @pl.when(is_end)
    def _():
        end_settle(out_items[1])

    @pl.when(is_inner)
    def _():
        inner_settle(out_items[1])

    gather_pair(out_items[0])
    attend_block(3)
    gather_wide(out_items[1])
    for head in range(KEYVALUE_HEADS):
        attended = (run_acc[head] / run_sum[head]).astype(jnp.bfloat16)
        mixed = jnp.dot(attended, shuffle, preferred_element_type=jnp.float32).astype(jnp.bfloat16)
        for j in range(heads):
            place = slice((head * heads + j) * HEAD_SIZE, (head * heads + j + 1) * HEAD_SIZE)
            attended_ref[:, place] = attended[j * tokens : (j + 1) * tokens]
            permuted[:, place] = mixed[j * tokens : (j + 1) * tokens]
    gather_pair(out_items[1])
    gathered(out_items[0])
    gathered(out_items[1])

    unit = items[out_items[0]][2]
    raise_start = QH * half

    def out_unit(n):
        j, chunk = n // OUT_CHUNKS, n % OUT_CHUNKS
        return final[out_items[chunk]].at[j % PLANE, j // PLANE]

    units = 2 * PLANE * OUT_CHUNKS
    for n in range(units):
        low_row = max(n * unit, raise_start)
        high_row = (n + 1) * unit
        if high_row > low_row:
            wide_out[low_row - raise_start : high_row - raise_start, :] = out_unit(n)[
                low_row - n * unit : unit, :
            ].astype(jnp.float32)
    narrow = jnp.zeros((tokens, ADAPTER_RANK), jnp.float32)
    for head in range(QH):
        begin = head * half
        block = out_unit(begin // unit)[begin % unit : begin % unit + half, :]
        weight = jnp.concatenate([block[:, :half], block[:, half:]], axis=0)
        narrow = narrow + jnp.dot(
            permuted[:, head * HEAD_SIZE : (head + 1) * HEAD_SIZE],
            weight,
            preferred_element_type=jnp.float32,
        )
    narrow = narrow.astype(jnp.bfloat16)
    blocks = D // LANES
    for j in range(blocks):
        up = wide_out[pl.ds(j, ADAPTER_RANK, stride=blocks), :].astype(jnp.bfloat16)
        delta_ref[:, j * LANES : (j + 1) * LANES] = (
            adapter_scale * jnp.dot(narrow, up, preferred_element_type=jnp.float32)
        ).astype(jnp.bfloat16)

    row_copy.wait_send()
    for i in range(count):
        for k in range(1, PLANE):
            plane_copy(i, k).wait_send()
        if i >= in_item:
            for kind in (CROSS, WIDE, PAIR, PAIR2):
                move(i, kind).wait_send()
    for k in range(1, 2 * PLANE):
        low_copy(k).wait_send()
    for n in range(4):
        keys_drain(n)

    @pl.when(is_end)
    def _():
        for i in range(count):
            move(i, FAR).wait_send()
            if i not in end_items:
                move(i, NEAR).wait_send()
            if i in end_items:
                move(i, CROSS).wait_send()
        for k in range(1, 2 * PLANE):
            for part in range(2):
                acts_copy(part, k, k < PLANE).wait_send()

    @pl.when(is_inner)
    def _():
        for i in range(count):
            move(i, MID).wait_send()
            if i not in inner_items:
                move(i, BACK).wait_send()
            if i in inner_items:
                move(i, CROSS).wait_send()
        for k in range(1, 2 * PLANE):
            for part in range(2):
                acts_copy(part, k, k >= PLANE).wait_send()


def fused(owner, stretch, x, pool, query_rows, key_rows, value_rows, cosine, sine):
    items = item_table(2 * PLANE)
    tokens = x.shape[0]
    bf16 = jnp.bfloat16
    f32 = jnp.float32
    dma = pltpu.SemaphoreType.DMA
    vmem = pltpu.VMEM
    count = len(items)
    sizes = [rows for _, _, rows in items]

    def each(*lead):
        return [vmem(lead + (rows, LANES), bf16) for rows in sizes]

    down_rows, in_rows, out_rows = section_rows()
    final = [
        vmem(((2,) if i < DOWN_CHUNKS else (PLANE, 2)) + (rows, LANES), bf16)
        for i, rows in enumerate(sizes)
    ]
    end_width = D // (2 * PLANE) * (DOWN_CHUNKS - INNER_CHUNKS) // DOWN_CHUNKS
    heads = QH // KEYVALUE_HEADS
    kv_columns = 2 * KEYVALUE_HEADS * HEAD_SIZE
    devices = 4 * PLANE
    scratch = [
        [vmem((PLANE, 1, rows * LANES), bf16) for rows in sizes],
        each(PLANE),
        each(PLANE),
        each(2),
        each(2),
        each(2),
        each(2),
        each(2),
        each(),
        final,
        vmem((2, 2 * PLANE, tokens, end_width), bf16),
        vmem((sizes[0], LANES), f32),
        vmem((2 * sizes[0] // 3, LANES), f32),
        vmem((2 * sizes[0] // 3, LANES), f32),
        vmem((2, end_width, 2 * LANES), bf16),
        vmem((2 * PLANE, tokens, 2 * LANES), f32),
        vmem((2 * PLANE, tokens, 2 * LANES), bf16),
        vmem((2 * PLANE, tokens, 2 * LANES), bf16),
        vmem((in_rows, LANES), f32),
        vmem((ADAPTER_RANK * D // LANES, LANES), f32),
        vmem((KEYVALUE_HEADS, heads * tokens, HEAD_SIZE), bf16),
        vmem((devices, tokens, kv_columns), bf16),
        vmem((tokens, QH * HEAD_SIZE), bf16),
        vmem((KEYVALUE_HEADS, heads * tokens, 1), f32),
        vmem((KEYVALUE_HEADS, heads * tokens, 1), f32),
        vmem((KEYVALUE_HEADS, heads * tokens, HEAD_SIZE), f32),
        vmem((1, LANES), jnp.int32),
        vmem((1, LANES), jnp.int32),
        pltpu.SMEM((2, 1, LANES), jnp.int32),
        dma((count, PLANE)),
        dma((count, PLANE)),
        dma((count, PLANE)),
        dma((count, 8)),
        dma((count, 8)),
        dma((2, 2 * PLANE)),
        dma((2, 2 * PLANE)),
        dma((2,)),
        dma,
        dma,
        dma((2,)),
        dma((2 * PLANE,)),
        dma((2 * PLANE,)),
        dma((4, 4)),
        dma((4, 4)),
    ]
    return pl.pallas_call(
        partial(fused_kernel, items),
        out_shape=(
            jax.ShapeDtypeStruct((tokens, QH * HEAD_SIZE), bf16),
            jax.ShapeDtypeStruct((tokens, D), bf16),
        ),
        in_specs=[SCALARS, SCALARS, ANYWHERE, ANYWHERE] + [ON_CHIP] * 5,
        out_specs=(ON_CHIP, ON_CHIP),
        scratch_shapes=scratch,
        compiler_params=pltpu.CompilerParams(
            collective_id=2, has_side_effects=True, vmem_limit_bytes=60 * 1024 * 1024
        ),
    )(owner, stretch, x, pool, query_rows, key_rows, value_rows, cosine, sine)


def shards(
    normed_input, query_base, key_base, value_base, adapter_pool, stretch_adapter, adapter_owner
):
    cycle_size = lax.axis_size("ctx")
    my_index = lax.axis_index("ctx")
    tok_rows = normed_input.shape[0]
    token_positions = my_index * tok_rows + jnp.arange(tok_rows, dtype=jnp.int32)
    groups = lax.axis_size("groups")
    cube = BLOCK_TOKENS // tok_rows
    cubes = cycle_size // cube
    down_size = 3 * ADAPTER_RANK * D
    half_dim = HEAD_SIZE // 2
    frequency = rope_base ** (-(jnp.arange(half_dim, dtype=jnp.float32) * 2.0) / HEAD_SIZE)
    angle = token_positions.astype(jnp.float32)[:, None] * frequency[None, :]
    cosine = jnp.cos(angle)
    sine = jnp.sin(angle)
    cosine = jnp.concatenate([cosine, cosine], axis=1)
    sine = jnp.concatenate([-sine, sine], axis=1)
    if groups == 2 and cube == 2 * PLANE and cubes == 2:
        return fused(
            adapter_owner, stretch_adapter, normed_input, adapter_pool,
            query_base, key_base, value_base, cosine, sine,
        )
    padding = -stretch_adapter.shape[0] % LANES
    stretch_row = jnp.pad(stretch_adapter, (0, padding))[None]
    moved, down_slice, rest = place_adapter(
        groups, cubes, cube, down_size, adapter_owner, stretch_row, normed_input, adapter_pool
    )
    rest = rest.reshape(-1, LANES)
    queries, gathered = keyval(
        cube,
        cycle_size,
        moved,
        down_slice.reshape(D // cube, 3 * ADAPTER_RANK),
        rest,
        query_base,
        key_base,
        value_base,
        cosine,
        sine,
    )
    gathered = gathered.reshape(cycle_size * tok_rows, -1)
    return attend(queries, gathered, rest)


def solution(mesh):
    placed = (
        P(("groups", "ctx"), None),
        P(("groups", "ctx"), None),
        P(("groups", "ctx"), None),
        P(("groups", "ctx"), None),
        P("ctx", None),
        P("groups"),
        P(),
    )
    return jax.shard_map(
        shards,
        mesh=mesh,
        in_specs=placed,
        out_specs=(P(("groups", "ctx"), None), P(("groups", "ctx"), None)),
        check_vma=False,
    )
```

```python
from functools import partial
import math

import jax
import jax.numpy as jnp
from jax import lax
from jax.experimental import pallas as pl
from jax.experimental.pallas import tpu as pltpu
from jax.sharding import PartitionSpec as P

D = 8192
QH = 32
KEYVALUE_HEADS = 4
HEAD_SIZE = 128
ADAPTER_RANK = 64
BLOCK_TOKENS = 512
QKV_POOL = 1900544


adapter_scale = 2.0
rope_base = 500000.0
mask_floor = -1e30


LANES = 128
MESH = pl.DeviceIdType.MESH
ON_CHIP = pl.BlockSpec(memory_space=pltpu.VMEM)
ANYWHERE = pl.BlockSpec(memory_space=pl.ANY)
SCALARS = pl.BlockSpec(memory_space=pltpu.SMEM)


def remote(src, dst, send_sem, recv_sem, group, ctx):
    return pltpu.make_async_remote_copy(
        src_ref=src,
        dst_ref=dst,
        send_sem=send_sem,
        recv_sem=recv_sem,
        device_id=(group, ctx),
        device_id_type=MESH,
    )


def place_adapter_kernel(
    groups, cubes, cube, down_size,
    owner_ref, stretch_ref, x_ref, pool_ref,
    x_out, down_out, rest_out,
    down_flat, rest_flat, down_source, rest_source,
    down_rows, rest_rows, down_send, rest_send, down_land, rest_land,
    stretch_land, table,
    s_flat, s_cube, r_cube, s_far, r_far, s_tree, r_tree, s_own, s_row, r_row, s_table,
):
    group = lax.axis_index("groups")
    ctx = lax.axis_index("ctx")
    inner = ctx % cube
    outer = ctx // cube
    home = group * cubes + outer
    kinds = groups * cubes
    width = x_out.shape[2] // groups
    down_piece = down_flat.shape[2]
    rest_piece = rest_flat.shape[2]

    def read_piece(row, k):
        piece = (rest_piece, down_piece)[row]
        start = (group * cube + (inner ^ k)) * piece + (down_size, 0)[row]
        return pltpu.make_async_copy(
            pool_ref.at[:, pl.ds(pl.multiple_of(start, LANES), piece)],
            (rest_flat, down_flat)[row].at[k],
            s_flat.at[row, k],
        )

    for row in range(2):
        for k in reversed(range(cube)):
            read_piece(row, k).start()

    barrier = pltpu.get_barrier_semaphore()
    for k in range(1, cube):
        pl.semaphore_signal(
            barrier, inc=1, device_id=(group, outer * cube + (inner ^ k)), device_id_type=MESH
        )
    for k in range(1, kinds):
        there = home ^ k
        pl.semaphore_signal(
            barrier,
            inc=1,
            device_id=(there // cubes, (there % cubes) * cube + inner),
            device_id_type=MESH,
        )
    pl.semaphore_wait(barrier, cube - 1 + kinds - 1)
    row_copies = []
    for step in range(1, groups):
        copy = remote(
            stretch_ref, stretch_land.at[step], s_row.at[step], r_row.at[step], group ^ step, ctx
        )
        copy.start()
        row_copies.append(copy)

    def columns(part, owner):
        return pl.ds(pl.multiple_of((part * cube + owner) * width, width), width)

    def cube_copy(row, k):
        peer = inner ^ k
        return remote(
            (rest_source, down_source)[row].at[k], (rest_rows, down_rows)[row].at[inner],
            s_cube.at[row, k], r_cube.at[row, k], group, outer * cube + peer,
        )

    def dense(row, k):
        flat = (rest_flat, down_flat)[row][k].astype(jnp.float32)
        return flat.reshape(-1, LANES).astype(jnp.bfloat16)

    def x_copy(part, k):
        peer = inner ^ k
        return remote(
            x_ref.at[:, columns(part, peer)],
            x_out.at[inner, :, pl.ds(part * width, width)],
            s_cube.at[2 + part, k], r_cube.at[2 + part, k],
            group, outer * cube + peer,
        )

    for row, (source, rows) in enumerate(((rest_source, rest_rows), (down_source, down_rows))):

        def spread(step, carry, row=row, source=source):
            k = cube - 1 - step
            read_piece(row, k).wait()
            source[k] = dense(row, k)
            cube_copy(row, k).start()
            return carry

        lax.fori_loop(0, cube - 1, spread, 0)
        read_piece(row, 0).wait()
        rows[inner] = dense(row, 0)

    to_table = [pltpu.make_async_copy(stretch_ref, table.at[0], s_table.at[0])]
    to_table[0].start()
    for step, copy in zip(range(1, groups), row_copies):
        copy.wait_recv()
        move = pltpu.make_async_copy(stretch_land.at[step], table.at[step], s_table.at[step])
        move.start()
        to_table.append(move)
    for move in to_table:
        move.wait()

    def slot_of(k):
        return owner_ref[table[k // cubes, 0, outer ^ (k % cubes)]]

    def chosen(part):
        return (part * cubes + lax.div(slot_of(0), cube)) ^ home

    owns = []
    for part in range(groups):
        own = pltpu.make_async_copy(
            x_ref.at[:, columns(part, inner)],
            x_out.at[inner, :, pl.ds(part * width, width)],
            s_own.at[part],
        )
        own.start()
        owns.append(own)

    far = []
    for row, (rows, outgoing, landing) in enumerate(
        ((rest_rows, rest_send, rest_land), (down_rows, down_send, down_land))
    ):
        for k in range(1, cube):
            cube_copy(row, k).wait_recv()
        coming = []
        for k in range(1, kinds):
            there = home ^ k
            outgoing[k] = rows[lax.rem(slot_of(k), cube)]
            copy = remote(
                outgoing.at[k], landing.at[k], s_far.at[row, k], r_far.at[row, k],
                there // cubes, (there % cubes) * cube + inner,
            )
            copy.start()
            coming.append(copy)
        landing[0] = rows[lax.rem(slot_of(0), cube)]
        far.append(coming)

    for copy in far[0]:
        copy.wait_recv()
    for part in range(groups):
        rest_out[part, inner] = rest_land[chosen(part)]
    tree = {}
    have = [[0] for _ in range(groups)]
    levels = cube.bit_length() - 1
    orders = []
    for part in range(groups):
        order = [1 << level for level in reversed(range(levels))]
        if part % 2:
            order[:2] = order[1::-1]
        orders.append(order)
    for stage in range(levels):
        for part in range(groups):
            bit = orders[part][stage]
            before = orders[part][stage - 1] if stage else 0
            for k in have[part]:
                if k & before:
                    tree[k, part].wait_recv()
            new = []
            for k in have[part]:
                slot = rest_out.at[part, inner ^ k]
                copy = remote(
                    slot, slot, s_tree.at[part, k ^ bit], r_tree.at[part, k ^ bit],
                    group, outer * cube + (inner ^ bit),
                )
                copy.start()
                tree[k ^ bit, part] = copy
                new.append(k ^ bit)
            have[part] = have[part] + new
        if stage == 0:
            for part in range(groups):
                for k in reversed(range(1, cube)):
                    x_copy(part, k).start()

    for copy in far[1]:
        copy.wait_recv()
    for part in range(groups):
        down_out[part] = down_land[chosen(part)]
    for (k, part), copy in tree.items():
        if k & orders[part][-1]:
            copy.wait_recv()
    for own in owns:
        own.wait()
    for part in range(groups):
        for k in range(1, cube):
            x_copy(part, k).wait_recv()
            x_copy(part, k).wait_send()
    for row in range(2):
        for k in range(1, cube):
            cube_copy(row, k).wait_send()
    for copy in row_copies + far[0] + far[1] + list(tree.values()):
        copy.wait_send()


def place_adapter(groups, cubes, cube, down_size, owner, stretch_row, x, pool):
    kinds = groups * cubes
    tokens, depth = x.shape
    down_piece = down_size // (groups * cube)
    rest_piece = (pool.shape[1] - down_size) // (groups * cube)
    down_shape = (down_piece // LANES, LANES)
    rest_shape = (rest_piece // LANES, LANES)
    bf16 = jnp.bfloat16
    dma = pltpu.SemaphoreType.DMA
    return pl.pallas_call(
        partial(place_adapter_kernel, groups, cubes, cube, down_size),
        out_shape=(
            jax.ShapeDtypeStruct((cube, tokens, depth // cube), bf16),
            jax.ShapeDtypeStruct((groups,) + down_shape, bf16),
            jax.ShapeDtypeStruct((groups, cube) + rest_shape, bf16),
        ),
        in_specs=[SCALARS, ON_CHIP, ON_CHIP, pl.BlockSpec(memory_space=pl.ANY)],
        out_specs=(ON_CHIP, ON_CHIP, ON_CHIP),
        scratch_shapes=[
            pltpu.VMEM((cube, 1, down_piece), bf16),
            pltpu.VMEM((cube, 1, rest_piece), bf16),
            pltpu.VMEM((cube,) + down_shape, bf16),
            pltpu.VMEM((cube,) + rest_shape, bf16),
            pltpu.VMEM((cube,) + down_shape, bf16),
            pltpu.VMEM((cube,) + rest_shape, bf16),
            pltpu.VMEM((kinds,) + down_shape, bf16),
            pltpu.VMEM((kinds,) + rest_shape, bf16),
            pltpu.VMEM((kinds,) + down_shape, bf16),
            pltpu.VMEM((kinds,) + rest_shape, bf16),
            pltpu.VMEM((groups,) + stretch_row.shape, jnp.int32),
            pltpu.SMEM((groups,) + stretch_row.shape, jnp.int32),
            dma((2, cube)),
            dma((2 + groups, cube)),
            dma((2 + groups, cube)),
            dma((2, kinds)),
            dma((2, kinds)),
            dma((groups, cube)),
            dma((groups, cube)),
            dma((groups,)),
            dma((groups,)),
            dma((groups,)),
            dma((groups,)),
        ],
        compiler_params=pltpu.CompilerParams(
            collective_id=0, has_side_effects=True, vmem_limit_bytes=60 * 1024 * 1024
        ),
    )(owner, stretch_row, x, pool)


def keyval_kernel(
    cube, count,
    x_any, w_ref, rest_any, query_ref, key_ref, value_ref, cos_ref, sin_ref,
    query_out, out_ref,
    x_ref, up_ref, s_in, wide, total, outgoing, landing, s_sem, r_sem, s_all, r_all,
):
    group = lax.axis_index("groups")
    ctx = lax.axis_index("ctx")
    inner = ctx % cube
    outer = ctx // cube
    levels = count.bit_length() - 1
    x_in = pltpu.make_async_copy(x_any, x_ref, s_in.at[0])
    x_in.start()
    up_in = pltpu.make_async_copy(
        rest_any.at[pl.ds(0, up_ref.shape[0])], up_ref, s_in.at[1]
    )
    up_in.start()
    barrier = pltpu.get_barrier_semaphore()
    apart = list(range(1, cube)) + [1 << n for n in range(levels) if 1 << n >= cube]
    for k in apart:
        pl.semaphore_signal(barrier, inc=1, device_id=(group, ctx ^ k), device_id_type=MESH)
    _, tokens, depth = x_ref.shape
    x_in.wait()
    product = jnp.dot(
        x_ref[...].reshape(cube * tokens, depth), w_ref[...], preferred_element_type=jnp.float32
    ).reshape(cube, tokens, w_ref.shape[1])
    total[...] = product
    outgoing[...] = product.astype(jnp.bfloat16)
    pl.semaphore_wait(barrier, len(apart))
    copies = []
    for k in range(1, cube):
        peer = inner ^ k
        copy = remote(
            outgoing.at[peer], landing.at[k], s_sem.at[k], r_sem.at[k], group, outer * cube + peer
        )
        copy.start()
        copies.append(copy)
    up_in.wait()
    wide[...] = up_ref[...].astype(jnp.float32)
    result = total[inner]
    for k, copy in zip(range(1, cube), copies):
        copy.wait_recv()
        result = result + landing[k].astype(jnp.float32)
    low = result.astype(jnp.bfloat16)
    half = HEAD_SIZE // 2
    query_rows = ADAPTER_RANK * QH
    kinds = 2 * KEYVALUE_HEADS
    for j in range(2 * KEYVALUE_HEADS):
        first = ADAPTER_RANK * (1 if j < KEYVALUE_HEADS else 2)
        delta = adapter_scale * jnp.dot(
            low[:, first : first + ADAPTER_RANK],
            wide[pl.ds(query_rows + j, ADAPTER_RANK, stride=kinds), :].astype(jnp.bfloat16),
            preferred_element_type=jnp.float32
        )
        base_ref = key_ref if j < KEYVALUE_HEADS else value_ref
        head = j % KEYVALUE_HEADS
        if j < KEYVALUE_HEADS:
            swapped = jnp.concatenate([delta[:, half:], delta[:, :half]], axis=1)
            delta = delta * cos_ref[...] + swapped * sin_ref[...]
        base = base_ref[:, head * HEAD_SIZE : (head + 1) * HEAD_SIZE].astype(jnp.float32)
        out_ref[ctx, :, j * HEAD_SIZE : (j + 1) * HEAD_SIZE] = (base + delta).astype(jnp.bfloat16)

    def query_head(head):
        up = wide[pl.ds(head, ADAPTER_RANK, stride=QH), :].astype(jnp.bfloat16)
        delta = adapter_scale * jnp.dot(
            low[:, :ADAPTER_RANK], up, preferred_element_type=jnp.float32
        )
        swapped = jnp.concatenate([delta[:, half:], delta[:, :half]], axis=1)
        delta = delta * cos_ref[...] + swapped * sin_ref[...]
        base = query_ref[:, head * HEAD_SIZE : (head + 1) * HEAD_SIZE].astype(jnp.float32)
        shared = QH // KEYVALUE_HEADS
        query_out[
            head // shared, (head % shared) * tokens : (head % shared + 1) * tokens, :
        ] = (base + delta).astype(jnp.bfloat16)

    kv_width = KEYVALUE_HEADS * HEAD_SIZE
    far_first = [1 << level for level in reversed(range(levels))]
    orders = (far_first, [2] + [bit for bit in far_first if bit != 2])
    have = [[0], [0]]
    moved = {}
    done = 0
    for stage in range(levels):
        for part in range(2):
            bit = orders[part][stage]
            before = orders[part][stage - 1] if stage else 0
            new = []
            for k in have[part]:
                if k & before:
                    moved[k, part].wait_recv()
                slot = out_ref.at[ctx ^ k, :, pl.ds(part * kv_width, kv_width)]
                copy = remote(
                    slot, slot, s_all.at[part, k ^ bit], r_all.at[part, k ^ bit], group, ctx ^ bit
                )
                copy.start()
                moved[k ^ bit, part] = copy
                new.append(k ^ bit)
            have[part] = have[part] + new
        until = QH * (stage + 1) // levels
        for head in range(done, until):
            query_head(head)
        done = until
    for (k, part), copy in moved.items():
        if k & orders[part][-1]:
            copy.wait_recv()
    for copy in copies + list(moved.values()):
        copy.wait_send()


def keyval(cube, count, x, w, rest, query_rows, key_rows, value_rows, cosine, sine):
    _, tokens, _ = x.shape
    shape = (cube, tokens, w.shape[1])
    up_rows = ADAPTER_RANK * (QH + 2 * KEYVALUE_HEADS)
    dma = pltpu.SemaphoreType.DMA
    return pl.pallas_call(
        partial(keyval_kernel, cube, count),
        out_shape=(
            jax.ShapeDtypeStruct(
                (KEYVALUE_HEADS, QH // KEYVALUE_HEADS * tokens, HEAD_SIZE), jnp.bfloat16
            ),
            jax.ShapeDtypeStruct(
                (count, tokens, 2 * KEYVALUE_HEADS * HEAD_SIZE), jnp.bfloat16
            ),
        ),
        in_specs=[ANYWHERE, ON_CHIP, ANYWHERE] + [ON_CHIP] * 5,
        out_specs=(ON_CHIP, ON_CHIP),
        scratch_shapes=[
            pltpu.VMEM(x.shape, jnp.bfloat16),
            pltpu.VMEM((up_rows, LANES), jnp.bfloat16),
            dma((2,)),
            pltpu.VMEM((up_rows, LANES), jnp.float32),
            pltpu.VMEM(shape, jnp.float32),
            pltpu.VMEM(shape, jnp.bfloat16),
            pltpu.VMEM(shape, jnp.bfloat16),
            dma((cube,)),
            dma((cube,)),
            dma((2, count)),
            dma((2, count)),
        ],
        compiler_params=pltpu.CompilerParams(
            collective_id=1, has_side_effects=True, vmem_limit_bytes=40 * 1024 * 1024
        ),
    )(x, w, rest, query_rows, key_rows, value_rows, cosine, sine)


def attend_kernel(
    step_keys, queries, kv_ref, rest_any,
    attended_ref, delta_ref,
    rest_ref, s_in, wide, permuted, run_max, run_sum, run_acc,
):
    tokens = attended_ref.shape[0]
    ctx = lax.axis_index("ctx")
    heads = QH // KEYVALUE_HEADS
    rows = heads * tokens
    half = HEAD_SIZE // 2
    query_rows = ADAPTER_RANK * QH
    raise_start = QH * half
    rest_in = pltpu.make_async_copy(
        rest_any.at[pl.ds(query_rows + 2 * ADAPTER_RANK * KEYVALUE_HEADS, rest_ref.shape[0])],
        rest_ref,
        s_in,
    )
    rest_in.start()
    first = ctx * tokens
    steps = (first + tokens + step_keys - 1) // step_keys
    row = lax.broadcasted_iota(jnp.int32, (rows, step_keys), 0)
    query_pos = first + lax.rem(row, tokens)
    key_off = lax.broadcasted_iota(jnp.int32, (rows, step_keys), 1)
    source = lax.broadcasted_iota(jnp.int32, (HEAD_SIZE, HEAD_SIZE), 0)
    target = lax.broadcasted_iota(jnp.int32, (HEAD_SIZE, HEAD_SIZE), 1)
    wanted = jnp.where(target < half, 2 * target, 2 * (target - half) + 1)
    shuffle = jnp.where(source == wanted, 1.0, 0.0).astype(jnp.bfloat16)
    for group in range(KEYVALUE_HEADS):
        run_max[...] = jnp.full_like(run_max, mask_floor)
        run_sum[...] = jnp.zeros_like(run_sum)
        run_acc[...] = jnp.zeros_like(run_acc)
        key_cols = slice(group * HEAD_SIZE, (group + 1) * HEAD_SIZE)
        value_first = (KEYVALUE_HEADS + group) * HEAD_SIZE

        def advance(step, carry):
            start = pl.multiple_of(step * step_keys, step_keys)
            keys = kv_ref[pl.ds(start, step_keys), key_cols]
            values = kv_ref[pl.ds(start, step_keys), value_first : value_first + HEAD_SIZE]
            scores = lax.dot_general(
                queries[group], keys, (((1,), (1,)), ((), ())),
                preferred_element_type=jnp.float32,
            ) * HEAD_SIZE ** (-0.5)
            scores = jnp.where(query_pos >= key_off + start, scores, mask_floor)
            new_max = jnp.maximum(run_max[...], jnp.max(scores, axis=1, keepdims=True))
            weights = jnp.exp(scores - new_max)
            rescale = jnp.exp(run_max[...] - new_max)
            run_sum[...] = run_sum[...] * rescale + jnp.sum(weights, axis=1, keepdims=True)
            run_acc[...] = run_acc[...] * rescale + jnp.dot(
                weights.astype(jnp.bfloat16), values, preferred_element_type=jnp.float32
            )
            run_max[...] = new_max
            return carry

        lax.fori_loop(0, steps, advance, 0)
        result = (run_acc[...] / run_sum[...]).astype(jnp.bfloat16)
        mixed = jnp.dot(result, shuffle, preferred_element_type=jnp.float32).astype(jnp.bfloat16)
        for j in range(heads):
            head = group * heads + j
            cols = slice(head * HEAD_SIZE, (head + 1) * HEAD_SIZE)
            attended_ref[:, cols] = result[j * tokens : (j + 1) * tokens]
            permuted[:, cols] = mixed[j * tokens : (j + 1) * tokens]
    rest_in.wait()
    wide[...] = rest_ref[raise_start:, :].astype(jnp.float32)
    narrow = jnp.zeros((tokens, ADAPTER_RANK), jnp.float32)
    for head in range(QH):
        block = rest_ref[head * half : (head + 1) * half, :]
        weight = jnp.concatenate([block[:, :half], block[:, half:]], axis=0)
        narrow = narrow + jnp.dot(
            permuted[:, head * HEAD_SIZE : (head + 1) * HEAD_SIZE],
            weight,
            preferred_element_type=jnp.float32,
        )
    narrow = narrow.astype(jnp.bfloat16)
    blocks = D // LANES
    for j in range(blocks):
        up = wide[pl.ds(j, ADAPTER_RANK, stride=blocks), :].astype(jnp.bfloat16)
        delta_ref[:, j * LANES : (j + 1) * LANES] = (
            adapter_scale * jnp.dot(narrow, up, preferred_element_type=jnp.float32)
        ).astype(jnp.bfloat16)


def attend(queries, kv, rest):
    rows = queries.shape[1]
    tokens = rows // (QH // KEYVALUE_HEADS)
    out_rows = ADAPTER_RANK * (QH * HEAD_SIZE + D) // LANES
    return pl.pallas_call(
        partial(attend_kernel, math.gcd(kv.shape[0], 1024)),
        out_shape=(
            jax.ShapeDtypeStruct((tokens, QH * HEAD_SIZE), jnp.bfloat16),
            jax.ShapeDtypeStruct((tokens, D), jnp.bfloat16),
        ),
        in_specs=[ON_CHIP, ON_CHIP, ANYWHERE],
        out_specs=(ON_CHIP, ON_CHIP),
        scratch_shapes=[
            pltpu.VMEM((out_rows, LANES), jnp.bfloat16),
            pltpu.SemaphoreType.DMA,
            pltpu.VMEM((ADAPTER_RANK * D // LANES, LANES), jnp.float32),
            pltpu.VMEM((tokens, QH * HEAD_SIZE), jnp.bfloat16),
            pltpu.VMEM((rows, 1), jnp.float32),
            pltpu.VMEM((rows, 1), jnp.float32),
            pltpu.VMEM((rows, HEAD_SIZE), jnp.float32),
        ],
        compiler_params=pltpu.CompilerParams(vmem_limit_bytes=56 * 1024 * 1024),
    )(queries, kv, rest)


PLANE = 4
DOWN_CHUNKS = 8
INNER_CHUNKS = 2
EARLY_CHUNKS = 4
OUT_CHUNKS = 2
FAR, NEAR, MID, BACK, CROSS, WIDE, PAIR, PAIR2 = range(8)


def section_rows():
    down = 3 * ADAPTER_RANK * D // LANES
    inner = ADAPTER_RANK * (QH + 2 * KEYVALUE_HEADS) * HEAD_SIZE // LANES
    outer = ADAPTER_RANK * (QH * HEAD_SIZE + D) // LANES
    return down, inner, outer


def item_table(slices):
    items = []
    first = 0
    for rows, chunks in zip(section_rows(), (DOWN_CHUNKS, 1, OUT_CHUNKS)):
        piece = rows // slices
        for chunk in range(chunks):
            items.append((first + chunk * (piece // chunks), piece, piece // chunks))
        first += rows
    return items


def fused_kernel(
    items,
    owner_ref, stretch_ref, x_any, pool_any, query_ref, key_ref, value_ref, cos_ref, sin_ref,
    attended_ref, delta_ref,
    flat, source, held, first_out, second_out, far_in, near_in, mid_in, cross_out, final,
    acts, spread_w, packed_a, packed_b, weights, total, low_out, low_in, wide_in, wide_out, queries, kv, permuted,
    run_max, run_sum, run_acc, row_out, row_in, table,
    s_flat, s_plane, r_plane, s_move, r_move, s_acts, r_acts, s_own, s_row, r_row, s_table,
    s_low, r_low, s_keys, r_keys,
):
    group = lax.axis_index("groups")
    ctx = lax.axis_index("ctx")
    lane = ctx % PLANE
    side = lane // 2
    core = lane % 2
    level = ctx // PLANE
    half_of = level // 2
    is_end = (level == 0) | (level == 3)
    is_inner = (level == 1) | (level == 2)
    tokens = x_any.shape[0]
    count = len(items)
    down_items = list(range(DOWN_CHUNKS))
    in_item = DOWN_CHUNKS
    end_items = down_items[:-INNER_CHUNKS]
    inner_items = down_items[-INNER_CHUNKS:]
    order = down_items[:EARLY_CHUNKS] + [in_item] + down_items[EARLY_CHUNKS:]
    out_items = list(range(DOWN_CHUNKS + 1, count))

    def read_piece(i, k):
        first, piece, rows = items[i]
        begin = (first + (group * PLANE + (lane ^ k)) * piece) * LANES
        return pltpu.make_async_copy(
            pool_any.at[:, pl.ds(pl.multiple_of(begin, LANES), rows * LANES)],
            flat[i].at[k],
            s_flat.at[i, k],
        )

    for i in range(count):
        for k in reversed(range(PLANE)):
            read_piece(i, k).start()

    def dense(i, k):
        return flat[i][k].astype(jnp.float32).reshape(-1, LANES).astype(jnp.bfloat16)

    def prepare(i):
        def step(n, carry):
            k = PLANE - 1 - n
            read_piece(i, k).wait()
            source[i][k] = dense(i, k)
            return carry

        lax.fori_loop(0, PLANE - 1, step, 0)
        read_piece(i, 0).wait()
        held[i][lane] = dense(i, 0)

    barrier = pltpu.get_barrier_semaphore()
    greeted = (1, 2, 3, 4, 5, 8, 12)
    for k in greeted:
        pl.semaphore_signal(barrier, inc=1, device_id=(group, ctx ^ k), device_id_type=MESH)
    pl.semaphore_signal(barrier, inc=1, device_id=(group ^ 1, ctx), device_id_type=MESH)
    mine_row = lax.broadcasted_iota(jnp.int32, row_out.shape, 1)
    row_out[...] = jnp.where(mine_row == 0, stretch_ref[0], stretch_ref[1])
    for i in order[:2]:
        prepare(i)
    pl.semaphore_wait(barrier, len(greeted) + 1)

    row_copy = remote(row_out, row_in, s_row, r_row, group ^ 1, ctx)
    row_copy.start()
    own_row = pltpu.make_async_copy(row_out, table.at[0], s_table.at[0])
    own_row.start()

    def plane_copy(i, k):
        return remote(
            source[i].at[k], held[i].at[lane], s_plane.at[i, k], r_plane.at[i, k], group, ctx ^ k
        )

    def scatter(i):
        for k in reversed(range(1, PLANE)):
            plane_copy(i, k).start()

    def slot(which, part):
        return owner_ref[table[which, 0, part]]

    def mine(which, part, where):
        return lax.div(slot(which, part), PLANE) == where

    def own_candidate(i, which, part):
        return held[i][lax.rem(slot(which, part), PLANE)]

    def move(i, kind):
        if kind == FAR:
            src, dst, there = first_out[i], far_in[i], (group, ctx ^ PLANE)
        elif kind == NEAR:
            src, dst, there = second_out[i], near_in[i], (group, ctx ^ PLANE)
        elif kind == MID:
            src, dst, there = first_out[i], mid_in[i], (group, ctx ^ (3 * PLANE))
        elif kind == BACK:
            src, dst, there = second_out[i], far_in[i], (group, ctx ^ PLANE)
        elif kind == CROSS:
            place = final[i].at[side, group] if i < in_item else final[i].at[lane, group]
            src, dst, there = cross_out[i], place, (group ^ 1, ctx)
        elif kind == WIDE:
            src = dst = final[i].at[side if i < in_item else lane]
            there = (group, ctx ^ 2)
        elif kind == PAIR:
            src = dst = final[i].at[lane]
            there = (group, ctx ^ 1)
        else:
            src = dst = final[i].at[lane ^ 2]
            there = (group, ctx ^ 1)
        return remote(src, dst, s_move.at[i, kind], r_move.at[i, kind], *there)

    def landed(i):
        for k in range(1, PLANE):
            plane_copy(i, k).wait_recv()

    def end_send(i):
        landed(i)
        for which in range(2):
            first_out[i][which] = own_candidate(i, which, 1 - half_of)
        move(i, FAR).start()
        if i not in end_items:
            for which in range(2):
                second_out[i][which] = own_candidate(i, which, half_of)
            move(i, NEAR).start()

    def settle(i, other_value, own_value):
        cross_out[i][...] = other_value
        move(i, CROSS).start()
        if i < in_item:
            final[i][side, group] = own_value
        else:
            final[i][lane, group] = own_value

    def end_settle(i):
        move(i, BACK).wait_recv()

        def value(which):
            return jnp.where(
                mine(which, half_of, level), own_candidate(i, which, half_of), far_in[i][which]
            )

        settle(i, value(1), value(0))

    def inner_across(i):
        landed(i)
        move(i, FAR).wait_recv()
        for which in range(2):
            first_out[i][which] = jnp.where(
                mine(which, 1 - half_of, level),
                own_candidate(i, which, 1 - half_of),
                far_in[i][which],
            )
        move(i, MID).start()

    def inner_back(i):
        move(i, MID).wait_recv()
        for which in range(2):
            second_out[i][which] = jnp.where(
                mine(which, half_of, level),
                own_candidate(i, which, half_of),
                mid_in[i][which],
            )
        if i not in inner_items:
            move(i, BACK).start()

    def inner_settle(i):
        move(i, NEAR).wait_recv()

        def value(which):
            return jnp.where(
                mine(which, half_of, level ^ 1), near_in[i][which], second_out[i][which]
            )

        settle(i, value(1), value(0))

    def gather_wide(i):
        move(i, CROSS).wait_recv()
        move(i, WIDE).start()
        move(i, PAIR).start()

    def gather_pair(i):
        move(i, WIDE).wait_recv()
        move(i, PAIR2).start()

    def gathered(i):
        move(i, PAIR).wait_recv()
        move(i, PAIR2).wait_recv()

    strip = D // (2 * PLANE)
    inner_width = strip * INNER_CHUNKS // DOWN_CHUNKS
    end_width = strip - inner_width

    near_by = (1, PLANE, PLANE + 1)

    def member(k):
        return k // PLANE * 2 + (core ^ (k % 2))

    def acts_copy(n, k, to_end):
        width = end_width if to_end else inner_width
        part, wing = n // 2, n % 2
        begin = (part * PLANE + wing * 2 + (core ^ (k % 2))) * strip + (0 if to_end else end_width)
        src = x_any.at[:, pl.ds(pl.multiple_of(begin, LANES), width)]
        dst = acts.at[n, k // PLANE * 2 + core, :, pl.ds(0, width)]
        if k == 0:
            return pltpu.make_async_copy(src, dst, s_own.at[n])
        return remote(src, dst, s_acts.at[n, k], r_acts.at[n, k], group, ctx ^ k)

    def acts_send():
        @pl.when(is_end)
        def _():
            for k in (PLANE, PLANE + 1, 1, 0):
                for n in range(4):
                    acts_copy(n, k, k < PLANE).start()

        @pl.when(is_inner)
        def _():
            for k in (PLANE, PLANE + 1, 1, 0):
                for n in range(4):
                    acts_copy(n, k, k >= PLANE).start()

    def acts_landed(to_end):
        for n in range(4):
            acts_copy(n, 0, to_end).wait()
            for k in near_by:
                acts_copy(n, k, to_end).wait_recv()

    def widen(i):
        move(i, CROSS).wait_recv()
        move(i, WIDE).start()

    def convert(i):
        move(i, WIDE).wait_recv()
        pairs = 2 * final[i].shape[2] // 3
        third = pairs // 2
        half = LANES // 2
        row = (i - (inner_items[0] if i in inner_items else 0)) * pairs
        for n in range(4):
            part, wing = n // 2, n % 2
            spread_w[...] = final[i][wing, part].astype(jnp.float32)
            first = spread_w[pl.ds(0, third, stride=3), :]
            second = spread_w[pl.ds(1, third, stride=3), :]
            last = spread_w[pl.ds(2, third, stride=3), :]
            packed_a[pl.ds(0, third, stride=2), :] = first
            packed_b[pl.ds(0, third, stride=2), :] = second
            packed_a[pl.ds(1, third, stride=2), :] = jnp.concatenate(
                [second[:, half:], last[:, :half]], axis=1
            )
            packed_b[pl.ds(1, third, stride=2), :] = jnp.concatenate(
                [last[:, half:], last[:, :half]], axis=1
            )
            weights[n, row : row + pairs, 0:LANES] = packed_a[...].astype(jnp.bfloat16)
            weights[n, row : row + pairs, LANES : 2 * LANES] = packed_b[...].astype(jnp.bfloat16)

    def product(width):
        sum_now = None
        for n in range(4):
            chunk = acts[n, :, :, 0:width].reshape(PLANE * tokens, width)
            term = jnp.dot(chunk, weights[n, 0:width, :], preferred_element_type=jnp.float32)
            sum_now = term if sum_now is None else sum_now + term
        total[...] = sum_now.reshape(PLANE, tokens, 2 * LANES)

    acts_send()
    scatter(order[0])
    scatter(order[1])
    for i in order[2:]:
        prepare(i)
        scatter(i)
    row_copy.wait_recv()
    own_row.wait()
    other_row = pltpu.make_async_copy(row_in, table.at[1], s_table.at[1])
    other_row.start()
    other_row.wait()
    for i in out_items:
        prepare(i)
    lag = 5
    steps = len(order)

    def at(n):
        return order[n] if 0 <= n < steps else None

    @pl.when(is_end)
    def _():
        for n in range(steps + lag + 2):
            if at(n) is not None:
                end_send(at(n))
            if at(n - lag) is not None and at(n - lag) not in inner_items:
                end_settle(at(n - lag))
            if at(n - lag - 1) in end_items:
                widen(at(n - lag - 1))
                if at(n - lag - 1) == end_items[-3]:
                    scatter(out_items[0])
            if at(n - lag - 2) in end_items:
                convert(at(n - lag - 2))
        scatter(out_items[1])
        end_send(out_items[0])
        acts_landed(True)
        product(end_width)

    @pl.when(is_inner)
    def _():
        for i in out_items:
            scatter(i)
        for n in range(steps + 4):
            if at(n) is not None:
                inner_across(at(n))
            if at(n - 1) is not None:
                inner_back(at(n - 1))
            if at(n - 2) is not None and at(n - 2) not in end_items:
                inner_settle(at(n - 2))
            if at(n - 3) in inner_items:
                widen(at(n - 3))
            if at(n - 4) in inner_items:
                convert(at(n - 4))
        acts_landed(False)
        product(inner_width)

    def at_inner(step, i):
        @pl.when(is_inner)
        def _():
            step(i)

    def at_end(step, i):
        @pl.when(is_end)
        def _():
            step(i)

    def low_copy(k):
        return remote(
            low_out.at[member(k)], low_in.at[near_by.index(k)],
            s_low.at[k], r_low.at[k], group, ctx ^ k,
        )

    low_out[...] = total[...].astype(jnp.bfloat16)
    for k in near_by[1:] + near_by[:1]:
        low_copy(k).start()

    gather_wide(in_item)
    at_end(end_send, out_items[1])
    at_inner(inner_across, out_items[0])
    result = total[core]
    gather_pair(in_item)
    for k in near_by:
        low_copy(k).wait_recv()
        result = result + low_in[near_by.index(k)].astype(jnp.float32)
    low = result.astype(jnp.bfloat16)
    gathered(in_item)
    at_inner(inner_back, out_items[0])
    in_rows = items[in_item][2]
    for part in range(2):
        for owner in range(PLANE):
            j = part * PLANE + owner
            wide_in[j * in_rows : (j + 1) * in_rows, :] = final[in_item][owner, part].astype(
                jnp.float32
            )

    half = HEAD_SIZE // 2
    query_rows = ADAPTER_RANK * QH
    kinds = 2 * KEYVALUE_HEADS
    for j in range(kinds):
        first = ADAPTER_RANK * (1 if j < KEYVALUE_HEADS else 2)
        delta = adapter_scale * jnp.dot(
            low[:, first : first + ADAPTER_RANK],
            wide_in[pl.ds(query_rows + j, ADAPTER_RANK, stride=kinds), :].astype(jnp.bfloat16),
            preferred_element_type=jnp.float32
        )
        base_ref = key_ref if j < KEYVALUE_HEADS else value_ref
        head = j % KEYVALUE_HEADS
        if j < KEYVALUE_HEADS:
            swapped = jnp.concatenate([delta[:, half:], delta[:, :half]], axis=1)
            delta = delta * cos_ref[...] + swapped * sin_ref[...]
        base = base_ref[:, head * HEAD_SIZE : (head + 1) * HEAD_SIZE].astype(jnp.float32)
        kv[ctx, :, j * HEAD_SIZE : (j + 1) * HEAD_SIZE] = (base + delta).astype(jnp.bfloat16)

    def query_head(head):
        up = wide_in[pl.ds(head, ADAPTER_RANK, stride=QH), :].astype(jnp.bfloat16)
        delta = adapter_scale * jnp.dot(
            low[:, :ADAPTER_RANK], up, preferred_element_type=jnp.float32
        )
        swapped = jnp.concatenate([delta[:, half:], delta[:, :half]], axis=1)
        delta = delta * cos_ref[...] + swapped * sin_ref[...]
        base = query_ref[:, head * HEAD_SIZE : (head + 1) * HEAD_SIZE].astype(jnp.float32)
        shared = QH // KEYVALUE_HEADS
        queries[
            head // shared, (head % shared) * tokens : (head % shared + 1) * tokens, :
        ] = (base + delta).astype(jnp.bfloat16)

    def keys_up(n):
        place = kv.at[ctx - PLANE * n]
        return remote(place, place, s_keys.at[n, 0], r_keys.at[n + 1, 0], group, ctx + PLANE)

    def keys_copy(n, kind):
        place = kv.at[(ctx ^ (2 if kind == 3 else 0)) - PLANE * n]
        return remote(
            place, place, s_keys.at[n, kind], r_keys.at[n, kind], group, ctx ^ (2 if kind == 1 else 1)
        )

    def keys_kick(n):
        @pl.when(level >= n)
        def _():
            if n > 0:
                place = kv.at[ctx - PLANE * n]
                remote(
                    place, place, s_keys.at[n - 1, 0], r_keys.at[n, 0], group, ctx - PLANE
                ).wait_recv()
            if n < 3:

                @pl.when(level < 3)
                def _():
                    keys_up(n).start()

            keys_copy(n, 1).start()
            keys_copy(n, 2).start()

    def keys_relay(n):
        @pl.when(level >= n)
        def _():
            keys_copy(n, 1).wait_recv()
            keys_copy(n, 3).start()

    def keys_drain(n):
        @pl.when(level >= n)
        def _():
            for kind in (1, 2, 3):
                keys_copy(n, kind).wait_send()
            if n < 3:

                @pl.when(level < 3)
                def _():
                    keys_up(n).wait_send()


    heads = QH // KEYVALUE_HEADS
    rows = heads * tokens
    keys_count = PLANE * tokens
    source_lane = lax.broadcasted_iota(jnp.int32, (HEAD_SIZE, HEAD_SIZE), 0)
    target_lane = lax.broadcasted_iota(jnp.int32, (HEAD_SIZE, HEAD_SIZE), 1)
    wanted = jnp.where(target_lane < half, 2 * target_lane, 2 * (target_lane - half) + 1)
    shuffle = jnp.where(source_lane == wanted, 1.0, 0.0).astype(jnp.bfloat16)
    factor = HEAD_SIZE ** (-0.5) * math.log2(math.e)

    def attend_block(n):
        @pl.when(level >= n)
        def _():
            keys_copy(n, 2).wait_recv()
            keys_copy(n, 3).wait_recv()
            first = PLANE * (level - n)
            for head in range(KEYVALUE_HEADS):
                keys = kv[pl.ds(first, PLANE), :, head * HEAD_SIZE : (head + 1) * HEAD_SIZE]
                value_first = (KEYVALUE_HEADS + head) * HEAD_SIZE
                values = kv[pl.ds(first, PLANE), :, value_first : value_first + HEAD_SIZE]
                keys = keys.reshape(keys_count, HEAD_SIZE)
                values = values.reshape(keys_count, HEAD_SIZE)
                scores = lax.dot_general(
                    queries[head], keys, (((1,), (1,)), ((), ())), preferred_element_type=jnp.float32
                )
                if n == 0:
                    query_pos = lane * tokens + lax.rem(
                        lax.broadcasted_iota(jnp.int32, (rows, keys_count), 0), tokens
                    )
                    key_pos = lax.broadcasted_iota(jnp.int32, (rows, keys_count), 1)
                    scores = jnp.where(query_pos >= key_pos, scores, mask_floor)
                top = jnp.max(scores, axis=1, keepdims=True)
                if n > 0:
                    top = jnp.maximum(top, run_max[head])
                weights = jnp.exp2((scores - top) * factor)
                norm = jnp.sum(weights, axis=1, keepdims=True)
                summed = jnp.dot(
                    weights.astype(jnp.bfloat16), values, preferred_element_type=jnp.float32
                )
                if n > 0:
                    rescale = jnp.exp2((run_max[head] - top) * factor)
                    norm = norm + run_sum[head] * rescale
                    summed = summed + run_acc[head] * rescale
                run_max[head] = top
                run_sum[head] = norm
                run_acc[head] = summed

    keys_kick(0)
    at_inner(inner_settle, out_items[0])
    at_inner(inner_across, out_items[1])
    for head in range(QH // 4):
        query_head(head)
    keys_relay(0)
    at_end(end_settle, out_items[0])
    keys_kick(1)
    for head in range(QH // 4, QH // 2):
        query_head(head)
    gather_wide(out_items[0])
    keys_relay(1)
    at_inner(inner_back, out_items[1])
    keys_kick(2)
    for head in range(QH // 2, QH):
        query_head(head)
    at_inner(inner_settle, out_items[1])
    at_end(end_settle, out_items[1])
    attend_block(0)
    keys_relay(2)
    keys_kick(3)
    gather_wide(out_items[1])
    gather_pair(out_items[0])
    attend_block(1)
    keys_relay(3)
    attend_block(2)
    gather_pair(out_items[1])
    attend_block(3)
    for head in range(KEYVALUE_HEADS):
        attended = (run_acc[head] / run_sum[head]).astype(jnp.bfloat16)
        mixed = jnp.dot(attended, shuffle, preferred_element_type=jnp.float32).astype(jnp.bfloat16)
        for j in range(heads):
            place = slice((head * heads + j) * HEAD_SIZE, (head * heads + j + 1) * HEAD_SIZE)
            attended_ref[:, place] = attended[j * tokens : (j + 1) * tokens]
            permuted[:, place] = mixed[j * tokens : (j + 1) * tokens]
    gathered(out_items[0])
    gathered(out_items[1])

    unit = items[out_items[0]][2]
    raise_start = QH * half

    def out_unit(n):
        j, chunk = n // OUT_CHUNKS, n % OUT_CHUNKS
        return final[out_items[chunk]].at[j % PLANE, j // PLANE]

    units = 2 * PLANE * OUT_CHUNKS
    for n in range(units):
        low_row = max(n * unit, raise_start)
        high_row = (n + 1) * unit
        if high_row > low_row:
            wide_out[low_row - raise_start : high_row - raise_start, :] = out_unit(n)[
                low_row - n * unit : unit, :
            ].astype(jnp.float32)
    narrow = jnp.zeros((tokens, ADAPTER_RANK), jnp.float32)
    for head in range(QH):
        begin = head * half
        block = out_unit(begin // unit)[begin % unit : begin % unit + half, :]
        weight = jnp.concatenate([block[:, :half], block[:, half:]], axis=0)
        narrow = narrow + jnp.dot(
            permuted[:, head * HEAD_SIZE : (head + 1) * HEAD_SIZE],
            weight,
            preferred_element_type=jnp.float32,
        )
    narrow = narrow.astype(jnp.bfloat16)
    blocks = D // LANES
    for j in range(blocks):
        up = wide_out[pl.ds(j, ADAPTER_RANK, stride=blocks), :].astype(jnp.bfloat16)
        delta_ref[:, j * LANES : (j + 1) * LANES] = (
            adapter_scale * jnp.dot(narrow, up, preferred_element_type=jnp.float32)
        ).astype(jnp.bfloat16)

    row_copy.wait_send()
    for i in range(count):
        for k in range(1, PLANE):
            plane_copy(i, k).wait_send()
        if i >= in_item:
            for kind in (CROSS, WIDE, PAIR, PAIR2):
                move(i, kind).wait_send()
    for k in near_by:
        low_copy(k).wait_send()
    for n in range(4):
        keys_drain(n)

    @pl.when(is_end)
    def _():
        for i in range(count):
            move(i, FAR).wait_send()
            if i not in end_items:
                move(i, NEAR).wait_send()
            if i in end_items:
                move(i, CROSS).wait_send()
                move(i, WIDE).wait_send()
        for k in near_by:
            for n in range(4):
                acts_copy(n, k, k < PLANE).wait_send()

    @pl.when(is_inner)
    def _():
        for i in range(count):
            move(i, MID).wait_send()
            if i not in inner_items:
                move(i, BACK).wait_send()
            if i in inner_items:
                move(i, CROSS).wait_send()
                move(i, WIDE).wait_send()
        for k in near_by:
            for n in range(4):
                acts_copy(n, k, k >= PLANE).wait_send()


def fused(owner, stretch, x, pool, query_rows, key_rows, value_rows, cosine, sine):
    items = item_table(2 * PLANE)
    tokens = x.shape[0]
    bf16 = jnp.bfloat16
    f32 = jnp.float32
    dma = pltpu.SemaphoreType.DMA
    vmem = pltpu.VMEM
    count = len(items)
    sizes = [rows for _, _, rows in items]

    def each(*lead):
        return [vmem(lead + (rows, LANES), bf16) for rows in sizes]

    down_rows, in_rows, out_rows = section_rows()
    final = [
        vmem(((2, 2) if i < DOWN_CHUNKS else (PLANE, 2)) + (rows, LANES), bf16)
        for i, rows in enumerate(sizes)
    ]
    end_width = D // (2 * PLANE) * (DOWN_CHUNKS - INNER_CHUNKS) // DOWN_CHUNKS
    heads = QH // KEYVALUE_HEADS
    kv_columns = 2 * KEYVALUE_HEADS * HEAD_SIZE
    devices = 4 * PLANE
    scratch = [
        [vmem((PLANE, 1, rows * LANES), bf16) for rows in sizes],
        each(PLANE),
        each(PLANE),
        each(2),
        each(2),
        each(2),
        each(2),
        each(2),
        each(),
        final,
        vmem((4, PLANE, tokens, end_width), bf16),
        vmem((sizes[0], LANES), f32),
        vmem((2 * sizes[0] // 3, LANES), f32),
        vmem((2 * sizes[0] // 3, LANES), f32),
        vmem((4, end_width, 2 * LANES), bf16),
        vmem((PLANE, tokens, 2 * LANES), f32),
        vmem((PLANE, tokens, 2 * LANES), bf16),
        vmem((3, tokens, 2 * LANES), bf16),
        vmem((in_rows, LANES), f32),
        vmem((ADAPTER_RANK * D // LANES, LANES), f32),
        vmem((KEYVALUE_HEADS, heads * tokens, HEAD_SIZE), bf16),
        vmem((devices, tokens, kv_columns), bf16),
        vmem((tokens, QH * HEAD_SIZE), bf16),
        vmem((KEYVALUE_HEADS, heads * tokens, 1), f32),
        vmem((KEYVALUE_HEADS, heads * tokens, 1), f32),
        vmem((KEYVALUE_HEADS, heads * tokens, HEAD_SIZE), f32),
        vmem((1, LANES), jnp.int32),
        vmem((1, LANES), jnp.int32),
        pltpu.SMEM((2, 1, LANES), jnp.int32),
        dma((count, PLANE)),
        dma((count, PLANE)),
        dma((count, PLANE)),
        dma((count, 8)),
        dma((count, 8)),
        dma((4, 2 * PLANE)),
        dma((4, 2 * PLANE)),
        dma((4,)),
        dma,
        dma,
        dma((2,)),
        dma((2 * PLANE,)),
        dma((2 * PLANE,)),
        dma((4, 4)),
        dma((4, 4)),
    ]
    return pl.pallas_call(
        partial(fused_kernel, items),
        out_shape=(
            jax.ShapeDtypeStruct((tokens, QH * HEAD_SIZE), bf16),
            jax.ShapeDtypeStruct((tokens, D), bf16),
        ),
        in_specs=[SCALARS, SCALARS, ANYWHERE, ANYWHERE] + [ON_CHIP] * 5,
        out_specs=(ON_CHIP, ON_CHIP),
        scratch_shapes=scratch,
        compiler_params=pltpu.CompilerParams(
            collective_id=2, has_side_effects=True, vmem_limit_bytes=60 * 1024 * 1024
        ),
    )(owner, stretch, x, pool, query_rows, key_rows, value_rows, cosine, sine)


def shards(
    normed_input, query_base, key_base, value_base, adapter_pool, stretch_adapter, adapter_owner
):
    cycle_size = lax.axis_size("ctx")
    my_index = lax.axis_index("ctx")
    tok_rows = normed_input.shape[0]
    token_positions = my_index * tok_rows + jnp.arange(tok_rows, dtype=jnp.int32)
    groups = lax.axis_size("groups")
    cube = BLOCK_TOKENS // tok_rows
    cubes = cycle_size // cube
    down_size = 3 * ADAPTER_RANK * D
    half_dim = HEAD_SIZE // 2
    frequency = rope_base ** (-(jnp.arange(half_dim, dtype=jnp.float32) * 2.0) / HEAD_SIZE)
    angle = token_positions.astype(jnp.float32)[:, None] * frequency[None, :]
    cosine = jnp.cos(angle)
    sine = jnp.sin(angle)
    cosine = jnp.concatenate([cosine, cosine], axis=1)
    sine = jnp.concatenate([-sine, sine], axis=1)
    if groups == 2 and cube == 2 * PLANE and cubes == 2:
        return fused(
            adapter_owner, stretch_adapter, normed_input, adapter_pool,
            query_base, key_base, value_base, cosine, sine,
        )
    padding = -stretch_adapter.shape[0] % LANES
    stretch_row = jnp.pad(stretch_adapter, (0, padding))[None]
    moved, down_slice, rest = place_adapter(
        groups, cubes, cube, down_size, adapter_owner, stretch_row, normed_input, adapter_pool
    )
    rest = rest.reshape(-1, LANES)
    queries, gathered = keyval(
        cube,
        cycle_size,
        moved,
        down_slice.reshape(D // cube, 3 * ADAPTER_RANK),
        rest,
        query_base,
        key_base,
        value_base,
        cosine,
        sine,
    )
    gathered = gathered.reshape(cycle_size * tok_rows, -1)
    return attend(queries, gathered, rest)


def solution(mesh):
    placed = (
        P(("groups", "ctx"), None),
        P(("groups", "ctx"), None),
        P(("groups", "ctx"), None),
        P(("groups", "ctx"), None),
        P("ctx", None),
        P("groups"),
        P(),
    )
    return jax.shard_map(
        shards,
        mesh=mesh,
        in_specs=placed,
        out_specs=(P(("groups", "ctx"), None), P(("groups", "ctx"), None)),
        check_vma=False,
    )
```

```python
from functools import partial
import math

import jax
import jax.numpy as jnp
from jax import lax
from jax.experimental import pallas as pl
from jax.experimental.pallas import tpu as pltpu
from jax.sharding import PartitionSpec as P

D = 8192
QH = 32
KEYVALUE_HEADS = 4
HEAD_SIZE = 128
ADAPTER_RANK = 64
BLOCK_TOKENS = 512
QKV_POOL = 1900544


adapter_scale = 2.0
rope_base = 500000.0
mask_floor = -1e30


LANES = 128
MESH = pl.DeviceIdType.MESH
ON_CHIP = pl.BlockSpec(memory_space=pltpu.VMEM)
ANYWHERE = pl.BlockSpec(memory_space=pl.ANY)
SCALARS = pl.BlockSpec(memory_space=pltpu.SMEM)


def remote(src, dst, send_sem, recv_sem, group, ctx):
    return pltpu.make_async_remote_copy(
        src_ref=src,
        dst_ref=dst,
        send_sem=send_sem,
        recv_sem=recv_sem,
        device_id=(group, ctx),
        device_id_type=MESH,
    )


def place_adapter_kernel(
    groups, cubes, cube, down_size,
    owner_ref, stretch_ref, x_ref, pool_ref,
    x_out, down_out, rest_out,
    down_flat, rest_flat, down_source, rest_source,
    down_rows, rest_rows, down_send, rest_send, down_land, rest_land,
    stretch_land, table,
    s_flat, s_cube, r_cube, s_far, r_far, s_tree, r_tree, s_own, s_row, r_row, s_table,
):
    group = lax.axis_index("groups")
    ctx = lax.axis_index("ctx")
    inner = ctx % cube
    outer = ctx // cube
    home = group * cubes + outer
    kinds = groups * cubes
    width = x_out.shape[2] // groups
    down_piece = down_flat.shape[2]
    rest_piece = rest_flat.shape[2]

    def read_piece(row, k):
        piece = (rest_piece, down_piece)[row]
        start = (group * cube + (inner ^ k)) * piece + (down_size, 0)[row]
        return pltpu.make_async_copy(
            pool_ref.at[:, pl.ds(pl.multiple_of(start, LANES), piece)],
            (rest_flat, down_flat)[row].at[k],
            s_flat.at[row, k],
        )

    for row in range(2):
        for k in reversed(range(cube)):
            read_piece(row, k).start()

    barrier = pltpu.get_barrier_semaphore()
    for k in range(1, cube):
        pl.semaphore_signal(
            barrier, inc=1, device_id=(group, outer * cube + (inner ^ k)), device_id_type=MESH
        )
    for k in range(1, kinds):
        there = home ^ k
        pl.semaphore_signal(
            barrier,
            inc=1,
            device_id=(there // cubes, (there % cubes) * cube + inner),
            device_id_type=MESH,
        )
    pl.semaphore_wait(barrier, cube - 1 + kinds - 1)
    row_copies = []
    for step in range(1, groups):
        copy = remote(
            stretch_ref, stretch_land.at[step], s_row.at[step], r_row.at[step], group ^ step, ctx
        )
        copy.start()
        row_copies.append(copy)

    def columns(part, owner):
        return pl.ds(pl.multiple_of((part * cube + owner) * width, width), width)

    def cube_copy(row, k):
        peer = inner ^ k
        return remote(
            (rest_source, down_source)[row].at[k], (rest_rows, down_rows)[row].at[inner],
            s_cube.at[row, k], r_cube.at[row, k], group, outer * cube + peer,
        )

    def dense(row, k):
        flat = (rest_flat, down_flat)[row][k].astype(jnp.float32)
        return flat.reshape(-1, LANES).astype(jnp.bfloat16)

    def x_copy(part, k):
        peer = inner ^ k
        return remote(
            x_ref.at[:, columns(part, peer)],
            x_out.at[inner, :, pl.ds(part * width, width)],
            s_cube.at[2 + part, k], r_cube.at[2 + part, k],
            group, outer * cube + peer,
        )

    for row, (source, rows) in enumerate(((rest_source, rest_rows), (down_source, down_rows))):

        def spread(step, carry, row=row, source=source):
            k = cube - 1 - step
            read_piece(row, k).wait()
            source[k] = dense(row, k)
            cube_copy(row, k).start()
            return carry

        lax.fori_loop(0, cube - 1, spread, 0)
        read_piece(row, 0).wait()
        rows[inner] = dense(row, 0)

    to_table = [pltpu.make_async_copy(stretch_ref, table.at[0], s_table.at[0])]
    to_table[0].start()
    for step, copy in zip(range(1, groups), row_copies):
        copy.wait_recv()
        move = pltpu.make_async_copy(stretch_land.at[step], table.at[step], s_table.at[step])
        move.start()
        to_table.append(move)
    for move in to_table:
        move.wait()

    def slot_of(k):
        return owner_ref[table[k // cubes, 0, outer ^ (k % cubes)]]

    def chosen(part):
        return (part * cubes + lax.div(slot_of(0), cube)) ^ home

    owns = []
    for part in range(groups):
        own = pltpu.make_async_copy(
            x_ref.at[:, columns(part, inner)],
            x_out.at[inner, :, pl.ds(part * width, width)],
            s_own.at[part],
        )
        own.start()
        owns.append(own)

    far = []
    for row, (rows, outgoing, landing) in enumerate(
        ((rest_rows, rest_send, rest_land), (down_rows, down_send, down_land))
    ):
        for k in range(1, cube):
            cube_copy(row, k).wait_recv()
        coming = []
        for k in range(1, kinds):
            there = home ^ k
            outgoing[k] = rows[lax.rem(slot_of(k), cube)]
            copy = remote(
                outgoing.at[k], landing.at[k], s_far.at[row, k], r_far.at[row, k],
                there // cubes, (there % cubes) * cube + inner,
            )
            copy.start()
            coming.append(copy)
        landing[0] = rows[lax.rem(slot_of(0), cube)]
        far.append(coming)

    for copy in far[0]:
        copy.wait_recv()
    for part in range(groups):
        rest_out[part, inner] = rest_land[chosen(part)]
    tree = {}
    have = [[0] for _ in range(groups)]
    levels = cube.bit_length() - 1
    orders = []
    for part in range(groups):
        order = [1 << level for level in reversed(range(levels))]
        if part % 2:
            order[:2] = order[1::-1]
        orders.append(order)
    for stage in range(levels):
        for part in range(groups):
            bit = orders[part][stage]
            before = orders[part][stage - 1] if stage else 0
            for k in have[part]:
                if k & before:
                    tree[k, part].wait_recv()
            new = []
            for k in have[part]:
                slot = rest_out.at[part, inner ^ k]
                copy = remote(
                    slot, slot, s_tree.at[part, k ^ bit], r_tree.at[part, k ^ bit],
                    group, outer * cube + (inner ^ bit),
                )
                copy.start()
                tree[k ^ bit, part] = copy
                new.append(k ^ bit)
            have[part] = have[part] + new
        if stage == 0:
            for part in range(groups):
                for k in reversed(range(1, cube)):
                    x_copy(part, k).start()

    for copy in far[1]:
        copy.wait_recv()
    for part in range(groups):
        down_out[part] = down_land[chosen(part)]
    for (k, part), copy in tree.items():
        if k & orders[part][-1]:
            copy.wait_recv()
    for own in owns:
        own.wait()
    for part in range(groups):
        for k in range(1, cube):
            x_copy(part, k).wait_recv()
            x_copy(part, k).wait_send()
    for row in range(2):
        for k in range(1, cube):
            cube_copy(row, k).wait_send()
    for copy in row_copies + far[0] + far[1] + list(tree.values()):
        copy.wait_send()


def place_adapter(groups, cubes, cube, down_size, owner, stretch_row, x, pool):
    kinds = groups * cubes
    tokens, depth = x.shape
    down_piece = down_size // (groups * cube)
    rest_piece = (pool.shape[1] - down_size) // (groups * cube)
    down_shape = (down_piece // LANES, LANES)
    rest_shape = (rest_piece // LANES, LANES)
    bf16 = jnp.bfloat16
    dma = pltpu.SemaphoreType.DMA
    return pl.pallas_call(
        partial(place_adapter_kernel, groups, cubes, cube, down_size),
        out_shape=(
            jax.ShapeDtypeStruct((cube, tokens, depth // cube), bf16),
            jax.ShapeDtypeStruct((groups,) + down_shape, bf16),
            jax.ShapeDtypeStruct((groups, cube) + rest_shape, bf16),
        ),
        in_specs=[SCALARS, ON_CHIP, ON_CHIP, pl.BlockSpec(memory_space=pl.ANY)],
        out_specs=(ON_CHIP, ON_CHIP, ON_CHIP),
        scratch_shapes=[
            pltpu.VMEM((cube, 1, down_piece), bf16),
            pltpu.VMEM((cube, 1, rest_piece), bf16),
            pltpu.VMEM((cube,) + down_shape, bf16),
            pltpu.VMEM((cube,) + rest_shape, bf16),
            pltpu.VMEM((cube,) + down_shape, bf16),
            pltpu.VMEM((cube,) + rest_shape, bf16),
            pltpu.VMEM((kinds,) + down_shape, bf16),
            pltpu.VMEM((kinds,) + rest_shape, bf16),
            pltpu.VMEM((kinds,) + down_shape, bf16),
            pltpu.VMEM((kinds,) + rest_shape, bf16),
            pltpu.VMEM((groups,) + stretch_row.shape, jnp.int32),
            pltpu.SMEM((groups,) + stretch_row.shape, jnp.int32),
            dma((2, cube)),
            dma((2 + groups, cube)),
            dma((2 + groups, cube)),
            dma((2, kinds)),
            dma((2, kinds)),
            dma((groups, cube)),
            dma((groups, cube)),
            dma((groups,)),
            dma((groups,)),
            dma((groups,)),
            dma((groups,)),
        ],
        compiler_params=pltpu.CompilerParams(
            collective_id=0, has_side_effects=True, vmem_limit_bytes=60 * 1024 * 1024
        ),
    )(owner, stretch_row, x, pool)


def keyval_kernel(
    cube, count,
    x_any, w_ref, rest_any, query_ref, key_ref, value_ref, cos_ref, sin_ref,
    query_out, out_ref,
    x_ref, up_ref, s_in, wide, total, outgoing, landing, s_sem, r_sem, s_all, r_all,
):
    group = lax.axis_index("groups")
    ctx = lax.axis_index("ctx")
    inner = ctx % cube
    outer = ctx // cube
    levels = count.bit_length() - 1
    x_in = pltpu.make_async_copy(x_any, x_ref, s_in.at[0])
    x_in.start()
    up_in = pltpu.make_async_copy(
        rest_any.at[pl.ds(0, up_ref.shape[0])], up_ref, s_in.at[1]
    )
    up_in.start()
    barrier = pltpu.get_barrier_semaphore()
    apart = list(range(1, cube)) + [1 << n for n in range(levels) if 1 << n >= cube]
    for k in apart:
        pl.semaphore_signal(barrier, inc=1, device_id=(group, ctx ^ k), device_id_type=MESH)
    _, tokens, depth = x_ref.shape
    x_in.wait()
    product = jnp.dot(
        x_ref[...].reshape(cube * tokens, depth), w_ref[...], preferred_element_type=jnp.float32
    ).reshape(cube, tokens, w_ref.shape[1])
    total[...] = product
    outgoing[...] = product.astype(jnp.bfloat16)
    pl.semaphore_wait(barrier, len(apart))
    copies = []
    for k in range(1, cube):
        peer = inner ^ k
        copy = remote(
            outgoing.at[peer], landing.at[k], s_sem.at[k], r_sem.at[k], group, outer * cube + peer
        )
        copy.start()
        copies.append(copy)
    up_in.wait()
    wide[...] = up_ref[...].astype(jnp.float32)
    result = total[inner]
    for k, copy in zip(range(1, cube), copies):
        copy.wait_recv()
        result = result + landing[k].astype(jnp.float32)
    low = result.astype(jnp.bfloat16)
    half = HEAD_SIZE // 2
    query_rows = ADAPTER_RANK * QH
    kinds = 2 * KEYVALUE_HEADS
    for j in range(2 * KEYVALUE_HEADS):
        first = ADAPTER_RANK * (1 if j < KEYVALUE_HEADS else 2)
        delta = adapter_scale * jnp.dot(
            low[:, first : first + ADAPTER_RANK],
            wide[pl.ds(query_rows + j, ADAPTER_RANK, stride=kinds), :].astype(jnp.bfloat16),
            preferred_element_type=jnp.float32
        )
        base_ref = key_ref if j < KEYVALUE_HEADS else value_ref
        head = j % KEYVALUE_HEADS
        if j < KEYVALUE_HEADS:
            swapped = jnp.concatenate([delta[:, half:], delta[:, :half]], axis=1)
            delta = delta * cos_ref[...] + swapped * sin_ref[...]
        base = base_ref[:, head * HEAD_SIZE : (head + 1) * HEAD_SIZE].astype(jnp.float32)
        out_ref[ctx, :, j * HEAD_SIZE : (j + 1) * HEAD_SIZE] = (base + delta).astype(jnp.bfloat16)

    def query_head(head):
        up = wide[pl.ds(head, ADAPTER_RANK, stride=QH), :].astype(jnp.bfloat16)
        delta = adapter_scale * jnp.dot(
            low[:, :ADAPTER_RANK], up, preferred_element_type=jnp.float32
        )
        swapped = jnp.concatenate([delta[:, half:], delta[:, :half]], axis=1)
        delta = delta * cos_ref[...] + swapped * sin_ref[...]
        base = query_ref[:, head * HEAD_SIZE : (head + 1) * HEAD_SIZE].astype(jnp.float32)
        shared = QH // KEYVALUE_HEADS
        query_out[
            head // shared, (head % shared) * tokens : (head % shared + 1) * tokens, :
        ] = (base + delta).astype(jnp.bfloat16)

    kv_width = KEYVALUE_HEADS * HEAD_SIZE
    far_first = [1 << level for level in reversed(range(levels))]
    orders = (far_first, [2] + [bit for bit in far_first if bit != 2])
    have = [[0], [0]]
    moved = {}
    done = 0
    for stage in range(levels):
        for part in range(2):
            bit = orders[part][stage]
            before = orders[part][stage - 1] if stage else 0
            new = []
            for k in have[part]:
                if k & before:
                    moved[k, part].wait_recv()
                slot = out_ref.at[ctx ^ k, :, pl.ds(part * kv_width, kv_width)]
                copy = remote(
                    slot, slot, s_all.at[part, k ^ bit], r_all.at[part, k ^ bit], group, ctx ^ bit
                )
                copy.start()
                moved[k ^ bit, part] = copy
                new.append(k ^ bit)
            have[part] = have[part] + new
        until = QH * (stage + 1) // levels
        for head in range(done, until):
            query_head(head)
        done = until
    for (k, part), copy in moved.items():
        if k & orders[part][-1]:
            copy.wait_recv()
    for copy in copies + list(moved.values()):
        copy.wait_send()


def keyval(cube, count, x, w, rest, query_rows, key_rows, value_rows, cosine, sine):
    _, tokens, _ = x.shape
    shape = (cube, tokens, w.shape[1])
    up_rows = ADAPTER_RANK * (QH + 2 * KEYVALUE_HEADS)
    dma = pltpu.SemaphoreType.DMA
    return pl.pallas_call(
        partial(keyval_kernel, cube, count),
        out_shape=(
            jax.ShapeDtypeStruct(
                (KEYVALUE_HEADS, QH // KEYVALUE_HEADS * tokens, HEAD_SIZE), jnp.bfloat16
            ),
            jax.ShapeDtypeStruct(
                (count, tokens, 2 * KEYVALUE_HEADS * HEAD_SIZE), jnp.bfloat16
            ),
        ),
        in_specs=[ANYWHERE, ON_CHIP, ANYWHERE] + [ON_CHIP] * 5,
        out_specs=(ON_CHIP, ON_CHIP),
        scratch_shapes=[
            pltpu.VMEM(x.shape, jnp.bfloat16),
            pltpu.VMEM((up_rows, LANES), jnp.bfloat16),
            dma((2,)),
            pltpu.VMEM((up_rows, LANES), jnp.float32),
            pltpu.VMEM(shape, jnp.float32),
            pltpu.VMEM(shape, jnp.bfloat16),
            pltpu.VMEM(shape, jnp.bfloat16),
            dma((cube,)),
            dma((cube,)),
            dma((2, count)),
            dma((2, count)),
        ],
        compiler_params=pltpu.CompilerParams(
            collective_id=1, has_side_effects=True, vmem_limit_bytes=40 * 1024 * 1024
        ),
    )(x, w, rest, query_rows, key_rows, value_rows, cosine, sine)


def attend_kernel(
    step_keys, queries, kv_ref, rest_any,
    attended_ref, delta_ref,
    rest_ref, s_in, wide, permuted, run_max, run_sum, run_acc,
):
    tokens = attended_ref.shape[0]
    ctx = lax.axis_index("ctx")
    heads = QH // KEYVALUE_HEADS
    rows = heads * tokens
    half = HEAD_SIZE // 2
    query_rows = ADAPTER_RANK * QH
    raise_start = QH * half
    rest_in = pltpu.make_async_copy(
        rest_any.at[pl.ds(query_rows + 2 * ADAPTER_RANK * KEYVALUE_HEADS, rest_ref.shape[0])],
        rest_ref,
        s_in,
    )
    rest_in.start()
    first = ctx * tokens
    steps = (first + tokens + step_keys - 1) // step_keys
    row = lax.broadcasted_iota(jnp.int32, (rows, step_keys), 0)
    query_pos = first + lax.rem(row, tokens)
    key_off = lax.broadcasted_iota(jnp.int32, (rows, step_keys), 1)
    source = lax.broadcasted_iota(jnp.int32, (HEAD_SIZE, HEAD_SIZE), 0)
    target = lax.broadcasted_iota(jnp.int32, (HEAD_SIZE, HEAD_SIZE), 1)
    wanted = jnp.where(target < half, 2 * target, 2 * (target - half) + 1)
    shuffle = jnp.where(source == wanted, 1.0, 0.0).astype(jnp.bfloat16)
    for group in range(KEYVALUE_HEADS):
        run_max[...] = jnp.full_like(run_max, mask_floor)
        run_sum[...] = jnp.zeros_like(run_sum)
        run_acc[...] = jnp.zeros_like(run_acc)
        key_cols = slice(group * HEAD_SIZE, (group + 1) * HEAD_SIZE)
        value_first = (KEYVALUE_HEADS + group) * HEAD_SIZE

        def advance(step, carry):
            start = pl.multiple_of(step * step_keys, step_keys)
            keys = kv_ref[pl.ds(start, step_keys), key_cols]
            values = kv_ref[pl.ds(start, step_keys), value_first : value_first + HEAD_SIZE]
            scores = lax.dot_general(
                queries[group], keys, (((1,), (1,)), ((), ())),
                preferred_element_type=jnp.float32,
            ) * HEAD_SIZE ** (-0.5)
            scores = jnp.where(query_pos >= key_off + start, scores, mask_floor)
            new_max = jnp.maximum(run_max[...], jnp.max(scores, axis=1, keepdims=True))
            weights = jnp.exp(scores - new_max)
            rescale = jnp.exp(run_max[...] - new_max)
            run_sum[...] = run_sum[...] * rescale + jnp.sum(weights, axis=1, keepdims=True)
            run_acc[...] = run_acc[...] * rescale + jnp.dot(
                weights.astype(jnp.bfloat16), values, preferred_element_type=jnp.float32
            )
            run_max[...] = new_max
            return carry

        lax.fori_loop(0, steps, advance, 0)
        result = (run_acc[...] / run_sum[...]).astype(jnp.bfloat16)
        mixed = jnp.dot(result, shuffle, preferred_element_type=jnp.float32).astype(jnp.bfloat16)
        for j in range(heads):
            head = group * heads + j
            cols = slice(head * HEAD_SIZE, (head + 1) * HEAD_SIZE)
            attended_ref[:, cols] = result[j * tokens : (j + 1) * tokens]
            permuted[:, cols] = mixed[j * tokens : (j + 1) * tokens]
    rest_in.wait()
    wide[...] = rest_ref[raise_start:, :].astype(jnp.float32)
    narrow = jnp.zeros((tokens, ADAPTER_RANK), jnp.float32)
    for head in range(QH):
        block = rest_ref[head * half : (head + 1) * half, :]
        weight = jnp.concatenate([block[:, :half], block[:, half:]], axis=0)
        narrow = narrow + jnp.dot(
            permuted[:, head * HEAD_SIZE : (head + 1) * HEAD_SIZE],
            weight,
            preferred_element_type=jnp.float32,
        )
    narrow = narrow.astype(jnp.bfloat16)
    blocks = D // LANES
    for j in range(blocks):
        up = wide[pl.ds(j, ADAPTER_RANK, stride=blocks), :].astype(jnp.bfloat16)
        delta_ref[:, j * LANES : (j + 1) * LANES] = (
            adapter_scale * jnp.dot(narrow, up, preferred_element_type=jnp.float32)
        ).astype(jnp.bfloat16)


def attend(queries, kv, rest):
    rows = queries.shape[1]
    tokens = rows // (QH // KEYVALUE_HEADS)
    out_rows = ADAPTER_RANK * (QH * HEAD_SIZE + D) // LANES
    return pl.pallas_call(
        partial(attend_kernel, math.gcd(kv.shape[0], 1024)),
        out_shape=(
            jax.ShapeDtypeStruct((tokens, QH * HEAD_SIZE), jnp.bfloat16),
            jax.ShapeDtypeStruct((tokens, D), jnp.bfloat16),
        ),
        in_specs=[ON_CHIP, ON_CHIP, ANYWHERE],
        out_specs=(ON_CHIP, ON_CHIP),
        scratch_shapes=[
            pltpu.VMEM((out_rows, LANES), jnp.bfloat16),
            pltpu.SemaphoreType.DMA,
            pltpu.VMEM((ADAPTER_RANK * D // LANES, LANES), jnp.float32),
            pltpu.VMEM((tokens, QH * HEAD_SIZE), jnp.bfloat16),
            pltpu.VMEM((rows, 1), jnp.float32),
            pltpu.VMEM((rows, 1), jnp.float32),
            pltpu.VMEM((rows, HEAD_SIZE), jnp.float32),
        ],
        compiler_params=pltpu.CompilerParams(vmem_limit_bytes=56 * 1024 * 1024),
    )(queries, kv, rest)


PLANE = 4
DOWN_CHUNKS = 8
INNER_CHUNKS = 2
EARLY_CHUNKS = 4
OUT_CHUNKS = 2
FAR, NEAR, MID, BACK, CROSS, WIDE, PAIR, PAIR2 = range(8)


def section_rows():
    down = 3 * ADAPTER_RANK * D // LANES
    inner = ADAPTER_RANK * (QH + 2 * KEYVALUE_HEADS) * HEAD_SIZE // LANES
    outer = ADAPTER_RANK * (QH * HEAD_SIZE + D) // LANES
    return down, inner, outer


def item_table(slices):
    items = []
    first = 0
    for rows, chunks in zip(section_rows(), (DOWN_CHUNKS, 1, OUT_CHUNKS)):
        piece = rows // slices
        for chunk in range(chunks):
            items.append((first + chunk * (piece // chunks), piece, piece // chunks))
        first += rows
    return items


def fused_kernel(
    items,
    owner_ref, stretch_ref, x_any, pool_any, query_ref, key_ref, value_ref, cos_ref, sin_ref,
    attended_ref, delta_ref,
    flat, source, held, first_out, second_out, far_in, near_in, mid_in, cross_out, final,
    acts, spread_w, packed_a, packed_b, weights, total, low_out, low_in, wide_in, wide_out, queries, kv, permuted,
    run_max, run_sum, run_acc, row_out, row_in, table,
    s_flat, s_plane, r_plane, s_move, r_move, s_acts, r_acts, s_own, s_row, r_row, s_table,
    s_low, r_low, s_keys, r_keys,
):
    group = lax.axis_index("groups")
    ctx = lax.axis_index("ctx")
    lane = ctx % PLANE
    side = lane // 2
    core = lane % 2
    level = ctx // PLANE
    half_of = level // 2
    is_end = (level == 0) | (level == 3)
    is_inner = (level == 1) | (level == 2)
    tokens = x_any.shape[0]
    count = len(items)
    down_items = list(range(DOWN_CHUNKS))
    in_item = DOWN_CHUNKS
    end_items = down_items[:-INNER_CHUNKS]
    inner_items = down_items[-INNER_CHUNKS:]
    order = down_items[:EARLY_CHUNKS] + [in_item] + down_items[EARLY_CHUNKS:]
    out_items = list(range(DOWN_CHUNKS + 1, count))

    def read_piece(i, k):
        first, piece, rows = items[i]
        begin = (first + (group * PLANE + (lane ^ k)) * piece) * LANES
        return pltpu.make_async_copy(
            pool_any.at[:, pl.ds(pl.multiple_of(begin, LANES), rows * LANES)],
            flat[i].at[k],
            s_flat.at[i, k],
        )

    for i in range(count):
        for k in reversed(range(PLANE)):
            read_piece(i, k).start()

    def dense(i, k):
        return flat[i][k].astype(jnp.float32).reshape(-1, LANES).astype(jnp.bfloat16)

    def prepare(i):
        def step(n, carry):
            k = PLANE - 1 - n
            read_piece(i, k).wait()
            source[i][k] = dense(i, k)
            return carry

        lax.fori_loop(0, PLANE - 1, step, 0)
        read_piece(i, 0).wait()
        held[i][lane] = dense(i, 0)

    barrier = pltpu.get_barrier_semaphore()
    greeted = (1, 2, 3, 4, 5, 8, 12)
    for k in greeted:
        pl.semaphore_signal(barrier, inc=1, device_id=(group, ctx ^ k), device_id_type=MESH)
    pl.semaphore_signal(barrier, inc=1, device_id=(group ^ 1, ctx), device_id_type=MESH)
    mine_row = lax.broadcasted_iota(jnp.int32, row_out.shape, 1)
    row_out[...] = jnp.where(mine_row == 0, stretch_ref[0], stretch_ref[1])
    for i in order[:2]:
        prepare(i)
    pl.semaphore_wait(barrier, len(greeted) + 1)

    row_copy = remote(row_out, row_in, s_row, r_row, group ^ 1, ctx)
    row_copy.start()
    own_row = pltpu.make_async_copy(row_out, table.at[0], s_table.at[0])
    own_row.start()

    def plane_copy(i, k):
        return remote(
            source[i].at[k], held[i].at[lane], s_plane.at[i, k], r_plane.at[i, k], group, ctx ^ k
        )

    def scatter(i):
        for k in reversed(range(1, PLANE)):
            plane_copy(i, k).start()

    def slot(which, part):
        return owner_ref[table[which, 0, part]]

    def mine(which, part, where):
        return lax.div(slot(which, part), PLANE) == where

    def own_candidate(i, which, part):
        return held[i][lax.rem(slot(which, part), PLANE)]

    def move(i, kind):
        if kind == FAR:
            src, dst, there = first_out[i], far_in[i], (group, ctx ^ PLANE)
        elif kind == NEAR:
            src, dst, there = second_out[i], near_in[i], (group, ctx ^ PLANE)
        elif kind == MID:
            src, dst, there = first_out[i], mid_in[i], (group, ctx ^ (3 * PLANE))
        elif kind == BACK:
            src, dst, there = second_out[i], far_in[i], (group, ctx ^ PLANE)
        elif kind == CROSS:
            place = final[i].at[side, group] if i < in_item else final[i].at[lane, group]
            src, dst, there = cross_out[i], place, (group ^ 1, ctx)
        elif kind == WIDE:
            src = dst = final[i].at[side if i < in_item else lane]
            there = (group, ctx ^ 2)
        elif kind == PAIR:
            src = dst = final[i].at[lane]
            there = (group, ctx ^ 1)
        else:
            src = dst = final[i].at[lane ^ 2]
            there = (group, ctx ^ 1)
        return remote(src, dst, s_move.at[i, kind], r_move.at[i, kind], *there)

    def landed(i):
        for k in range(1, PLANE):
            plane_copy(i, k).wait_recv()

    def end_far(i):
        landed(i)
        for which in range(2):
            first_out[i][which] = own_candidate(i, which, 1 - half_of)
        move(i, FAR).start()

    def end_near(i):
        for which in range(2):
            second_out[i][which] = own_candidate(i, which, half_of)
        move(i, NEAR).start()

    def end_send(i):
        end_far(i)
        if i not in end_items:
            end_near(i)

    def settle(i, other_value, own_value):
        cross_out[i][...] = other_value
        move(i, CROSS).start()
        if i < in_item:
            final[i][side, group] = own_value
        else:
            final[i][lane, group] = own_value

    def end_settle(i):
        move(i, BACK).wait_recv()

        def value(which):
            return jnp.where(
                mine(which, half_of, level), own_candidate(i, which, half_of), far_in[i][which]
            )

        settle(i, value(1), value(0))

    def inner_across(i):
        landed(i)
        move(i, FAR).wait_recv()
        for which in range(2):
            first_out[i][which] = jnp.where(
                mine(which, 1 - half_of, level),
                own_candidate(i, which, 1 - half_of),
                far_in[i][which],
            )
        move(i, MID).start()

    def inner_back(i):
        move(i, MID).wait_recv()
        for which in range(2):
            second_out[i][which] = jnp.where(
                mine(which, half_of, level),
                own_candidate(i, which, half_of),
                mid_in[i][which],
            )
        if i not in inner_items:
            move(i, BACK).start()

    def inner_settle(i):
        move(i, NEAR).wait_recv()

        def value(which):
            return jnp.where(
                mine(which, half_of, level ^ 1), near_in[i][which], second_out[i][which]
            )

        settle(i, value(1), value(0))

    def gather_wide(i):
        move(i, CROSS).wait_recv()
        move(i, WIDE).start()
        move(i, PAIR).start()

    def gather_pair(i):
        move(i, WIDE).wait_recv()
        move(i, PAIR2).start()

    def gathered(i):
        move(i, PAIR).wait_recv()
        move(i, PAIR2).wait_recv()

    strip = D // (2 * PLANE)
    inner_width = strip * INNER_CHUNKS // DOWN_CHUNKS
    end_width = strip - inner_width

    near_by = (1, PLANE, PLANE + 1)

    def member(k):
        return k // PLANE * 2 + (core ^ (k % 2))

    def acts_copy(n, k, to_end):
        width = end_width if to_end else inner_width
        part, wing = n // 2, n % 2
        begin = (part * PLANE + wing * 2 + (core ^ (k % 2))) * strip + (0 if to_end else end_width)
        src = x_any.at[:, pl.ds(pl.multiple_of(begin, LANES), width)]
        dst = acts.at[n, k // PLANE * 2 + core, :, pl.ds(0, width)]
        if k == 0:
            return pltpu.make_async_copy(src, dst, s_own.at[n])
        return remote(src, dst, s_acts.at[n, k], r_acts.at[n, k], group, ctx ^ k)

    def acts_send():
        @pl.when(is_end)
        def _():
            for k in (PLANE, PLANE + 1, 1, 0):
                for n in range(4):
                    acts_copy(n, k, k < PLANE).start()

        @pl.when(is_inner)
        def _():
            for k in (PLANE, PLANE + 1, 1, 0):
                for n in range(4):
                    acts_copy(n, k, k >= PLANE).start()

    def acts_landed(to_end):
        for n in range(4):
            acts_copy(n, 0, to_end).wait()
            for k in near_by:
                acts_copy(n, k, to_end).wait_recv()

    def widen(i):
        move(i, CROSS).wait_recv()
        move(i, WIDE).start()

    def convert(i):
        move(i, WIDE).wait_recv()
        pairs = 2 * final[i].shape[2] // 3
        third = pairs // 2
        half = LANES // 2
        row = (i - (inner_items[0] if i in inner_items else 0)) * pairs
        for n in range(4):
            part, wing = n // 2, n % 2
            spread_w[...] = final[i][wing, part].astype(jnp.float32)
            first = spread_w[pl.ds(0, third, stride=3), :]
            second = spread_w[pl.ds(1, third, stride=3), :]
            last = spread_w[pl.ds(2, third, stride=3), :]
            packed_a[pl.ds(0, third, stride=2), :] = first
            packed_b[pl.ds(0, third, stride=2), :] = second
            packed_a[pl.ds(1, third, stride=2), :] = jnp.concatenate(
                [second[:, half:], last[:, :half]], axis=1
            )
            packed_b[pl.ds(1, third, stride=2), :] = jnp.concatenate(
                [last[:, half:], last[:, :half]], axis=1
            )
            weights[n, row : row + pairs, 0:LANES] = packed_a[...].astype(jnp.bfloat16)
            weights[n, row : row + pairs, LANES : 2 * LANES] = packed_b[...].astype(jnp.bfloat16)

    def product(width):
        sum_now = None
        for n in range(4):
            chunk = acts[n, :, :, 0:width].reshape(PLANE * tokens, width)
            term = jnp.dot(chunk, weights[n, 0:width, :], preferred_element_type=jnp.float32)
            sum_now = term if sum_now is None else sum_now + term
        total[...] = sum_now.reshape(PLANE, tokens, 2 * LANES)

    acts_send()
    scatter(order[0])
    scatter(order[1])
    for i in order[2:]:
        prepare(i)
        scatter(i)
    row_copy.wait_recv()
    own_row.wait()
    other_row = pltpu.make_async_copy(row_in, table.at[1], s_table.at[1])
    other_row.start()
    other_row.wait()
    for i in out_items:
        prepare(i)
    lag = 4
    steps = len(order)

    def at(n):
        return order[n] if 0 <= n < steps else None

    @pl.when(is_end)
    def _():
        for n in range(steps + lag + 2):
            if at(n) is not None:
                end_send(at(n))
            if at(n - lag) is not None and at(n - lag) not in inner_items:
                end_settle(at(n - lag))
            if at(n - lag - 1) in end_items:
                widen(at(n - lag - 1))
                if at(n - lag - 1) == end_items[-5]:
                    scatter(out_items[0])
            if at(n - lag - 2) in end_items:
                convert(at(n - lag - 2))
        scatter(out_items[1])
        acts_landed(True)
        product(end_width)
        end_far(out_items[0])

    @pl.when(is_inner)
    def _():
        for i in out_items:
            scatter(i)
        for n in range(steps + 4):
            if at(n) is not None:
                inner_across(at(n))
            if at(n - 1) is not None:
                inner_back(at(n - 1))
            if at(n - 2) is not None and at(n - 2) not in end_items:
                inner_settle(at(n - 2))
            if at(n - 3) in inner_items:
                widen(at(n - 3))
            if at(n - 4) in inner_items:
                convert(at(n - 4))
        acts_landed(False)
        product(inner_width)

    def at_inner(step, i):
        @pl.when(is_inner)
        def _():
            step(i)

    def at_end(step, i):
        @pl.when(is_end)
        def _():
            step(i)

    def low_copy(k):
        return remote(
            low_out.at[member(k)], low_in.at[near_by.index(k)],
            s_low.at[k], r_low.at[k], group, ctx ^ k,
        )

    low_out[...] = total[...].astype(jnp.bfloat16)
    for k in near_by[1:] + near_by[:1]:
        low_copy(k).start()

    gather_wide(in_item)
    at_end(end_far, out_items[1])
    at_end(end_near, out_items[0])
    at_inner(inner_across, out_items[0])
    result = total[core]
    gather_pair(in_item)
    for k in near_by:
        low_copy(k).wait_recv()
        result = result + low_in[near_by.index(k)].astype(jnp.float32)
    low = result.astype(jnp.bfloat16)
    gathered(in_item)
    at_inner(inner_back, out_items[0])
    in_rows = items[in_item][2]
    for part in range(2):
        for owner in range(PLANE):
            j = part * PLANE + owner
            wide_in[j * in_rows : (j + 1) * in_rows, :] = final[in_item][owner, part].astype(
                jnp.float32
            )

    half = HEAD_SIZE // 2
    query_rows = ADAPTER_RANK * QH
    kinds = 2 * KEYVALUE_HEADS
    for j in range(kinds):
        first = ADAPTER_RANK * (1 if j < KEYVALUE_HEADS else 2)
        delta = adapter_scale * jnp.dot(
            low[:, first : first + ADAPTER_RANK],
            wide_in[pl.ds(query_rows + j, ADAPTER_RANK, stride=kinds), :].astype(jnp.bfloat16),
            preferred_element_type=jnp.float32
        )
        base_ref = key_ref if j < KEYVALUE_HEADS else value_ref
        head = j % KEYVALUE_HEADS
        if j < KEYVALUE_HEADS:
            swapped = jnp.concatenate([delta[:, half:], delta[:, :half]], axis=1)
            delta = delta * cos_ref[...] + swapped * sin_ref[...]
        base = base_ref[:, head * HEAD_SIZE : (head + 1) * HEAD_SIZE].astype(jnp.float32)
        kv[ctx, :, j * HEAD_SIZE : (j + 1) * HEAD_SIZE] = (base + delta).astype(jnp.bfloat16)

    def query_head(head):
        up = wide_in[pl.ds(head, ADAPTER_RANK, stride=QH), :].astype(jnp.bfloat16)
        delta = adapter_scale * jnp.dot(
            low[:, :ADAPTER_RANK], up, preferred_element_type=jnp.float32
        )
        swapped = jnp.concatenate([delta[:, half:], delta[:, :half]], axis=1)
        delta = delta * cos_ref[...] + swapped * sin_ref[...]
        base = query_ref[:, head * HEAD_SIZE : (head + 1) * HEAD_SIZE].astype(jnp.float32)
        shared = QH // KEYVALUE_HEADS
        queries[
            head // shared, (head % shared) * tokens : (head % shared + 1) * tokens, :
        ] = (base + delta).astype(jnp.bfloat16)

    def keys_up(n):
        place = kv.at[ctx - PLANE * n]
        return remote(place, place, s_keys.at[n, 0], r_keys.at[n + 1, 0], group, ctx + PLANE)

    def keys_copy(n, kind):
        place = kv.at[(ctx ^ (2 if kind == 3 else 0)) - PLANE * n]
        return remote(
            place, place, s_keys.at[n, kind], r_keys.at[n, kind], group, ctx ^ (2 if kind == 1 else 1)
        )

    def keys_kick(n):
        @pl.when(level >= n)
        def _():
            if n > 0:
                place = kv.at[ctx - PLANE * n]
                remote(
                    place, place, s_keys.at[n - 1, 0], r_keys.at[n, 0], group, ctx - PLANE
                ).wait_recv()
            if n < 3:

                @pl.when(level < 3)
                def _():
                    keys_up(n).start()

            keys_copy(n, 1).start()
            keys_copy(n, 2).start()

    def keys_relay(n):
        @pl.when(level >= n)
        def _():
            keys_copy(n, 1).wait_recv()
            keys_copy(n, 3).start()

    def keys_drain(n):
        @pl.when(level >= n)
        def _():
            for kind in (1, 2, 3):
                keys_copy(n, kind).wait_send()
            if n < 3:

                @pl.when(level < 3)
                def _():
                    keys_up(n).wait_send()


    heads = QH // KEYVALUE_HEADS
    rows = heads * tokens
    keys_count = PLANE * tokens
    source_lane = lax.broadcasted_iota(jnp.int32, (HEAD_SIZE, HEAD_SIZE), 0)
    target_lane = lax.broadcasted_iota(jnp.int32, (HEAD_SIZE, HEAD_SIZE), 1)
    wanted = jnp.where(target_lane < half, 2 * target_lane, 2 * (target_lane - half) + 1)
    shuffle = jnp.where(source_lane == wanted, 1.0, 0.0).astype(jnp.bfloat16)
    factor = HEAD_SIZE ** (-0.5) * math.log2(math.e)

    def attend_block(n):
        @pl.when(level >= n)
        def _():
            keys_copy(n, 2).wait_recv()
            keys_copy(n, 3).wait_recv()
            first = PLANE * (level - n)
            for head in range(KEYVALUE_HEADS):
                keys = kv[pl.ds(first, PLANE), :, head * HEAD_SIZE : (head + 1) * HEAD_SIZE]
                value_first = (KEYVALUE_HEADS + head) * HEAD_SIZE
                values = kv[pl.ds(first, PLANE), :, value_first : value_first + HEAD_SIZE]
                keys = keys.reshape(keys_count, HEAD_SIZE)
                values = values.reshape(keys_count, HEAD_SIZE)
                scores = lax.dot_general(
                    queries[head], keys, (((1,), (1,)), ((), ())), preferred_element_type=jnp.float32
                )
                if n == 0:
                    query_pos = lane * tokens + lax.rem(
                        lax.broadcasted_iota(jnp.int32, (rows, keys_count), 0), tokens
                    )
                    key_pos = lax.broadcasted_iota(jnp.int32, (rows, keys_count), 1)
                    scores = jnp.where(query_pos >= key_pos, scores, mask_floor)
                top = jnp.max(scores, axis=1, keepdims=True)
                if n > 0:
                    top = jnp.maximum(top, run_max[head])
                weights = jnp.exp2((scores - top) * factor)
                norm = jnp.sum(weights, axis=1, keepdims=True)
                summed = jnp.dot(
                    weights.astype(jnp.bfloat16), values, preferred_element_type=jnp.float32
                )
                if n > 0:
                    rescale = jnp.exp2((run_max[head] - top) * factor)
                    norm = norm + run_sum[head] * rescale
                    summed = summed + run_acc[head] * rescale
                run_max[head] = top
                run_sum[head] = norm
                run_acc[head] = summed

    keys_kick(0)
    at_end(end_near, out_items[1])
    at_inner(inner_across, out_items[1])
    at_inner(inner_settle, out_items[0])
    for head in range(QH // 4):
        query_head(head)
    keys_relay(0)
    at_end(end_settle, out_items[0])
    keys_kick(1)
    at_inner(inner_back, out_items[1])
    for head in range(QH // 4, QH // 2):
        query_head(head)
    gather_wide(out_items[0])
    keys_relay(1)
    keys_kick(2)
    for head in range(QH // 2, QH):
        query_head(head)
    at_inner(inner_settle, out_items[1])
    at_end(end_settle, out_items[1])
    attend_block(0)
    keys_relay(2)
    keys_kick(3)
    gather_wide(out_items[1])
    gather_pair(out_items[0])
    attend_block(1)
    keys_relay(3)
    attend_block(2)
    gather_pair(out_items[1])
    attend_block(3)
    for head in range(KEYVALUE_HEADS):
        attended = (run_acc[head] / run_sum[head]).astype(jnp.bfloat16)
        mixed = jnp.dot(attended, shuffle, preferred_element_type=jnp.float32).astype(jnp.bfloat16)
        for j in range(heads):
            place = slice((head * heads + j) * HEAD_SIZE, (head * heads + j + 1) * HEAD_SIZE)
            attended_ref[:, place] = attended[j * tokens : (j + 1) * tokens]
            permuted[:, place] = mixed[j * tokens : (j + 1) * tokens]
    gathered(out_items[0])
    gathered(out_items[1])

    unit = items[out_items[0]][2]
    raise_start = QH * half

    def out_unit(n):
        j, chunk = n // OUT_CHUNKS, n % OUT_CHUNKS
        return final[out_items[chunk]].at[j % PLANE, j // PLANE]

    units = 2 * PLANE * OUT_CHUNKS
    for n in range(units):
        low_row = max(n * unit, raise_start)
        high_row = (n + 1) * unit
        if high_row > low_row:
            wide_out[low_row - raise_start : high_row - raise_start, :] = out_unit(n)[
                low_row - n * unit : unit, :
            ].astype(jnp.float32)
    narrow = jnp.zeros((tokens, ADAPTER_RANK), jnp.float32)
    for head in range(QH):
        begin = head * half
        block = out_unit(begin // unit)[begin % unit : begin % unit + half, :]
        weight = jnp.concatenate([block[:, :half], block[:, half:]], axis=0)
        narrow = narrow + jnp.dot(
            permuted[:, head * HEAD_SIZE : (head + 1) * HEAD_SIZE],
            weight,
            preferred_element_type=jnp.float32,
        )
    narrow = narrow.astype(jnp.bfloat16)
    blocks = D // LANES
    for j in range(blocks):
        up = wide_out[pl.ds(j, ADAPTER_RANK, stride=blocks), :].astype(jnp.bfloat16)
        delta_ref[:, j * LANES : (j + 1) * LANES] = (
            adapter_scale * jnp.dot(narrow, up, preferred_element_type=jnp.float32)
        ).astype(jnp.bfloat16)

    row_copy.wait_send()
    for i in range(count):
        for k in range(1, PLANE):
            plane_copy(i, k).wait_send()
        if i >= in_item:
            for kind in (CROSS, WIDE, PAIR, PAIR2):
                move(i, kind).wait_send()
    for k in near_by:
        low_copy(k).wait_send()
    for n in range(4):
        keys_drain(n)

    @pl.when(is_end)
    def _():
        for i in range(count):
            move(i, FAR).wait_send()
            if i not in end_items:
                move(i, NEAR).wait_send()
            if i in end_items:
                move(i, CROSS).wait_send()
                move(i, WIDE).wait_send()
        for k in near_by:
            for n in range(4):
                acts_copy(n, k, k < PLANE).wait_send()

    @pl.when(is_inner)
    def _():
        for i in range(count):
            move(i, MID).wait_send()
            if i not in inner_items:
                move(i, BACK).wait_send()
            if i in inner_items:
                move(i, CROSS).wait_send()
                move(i, WIDE).wait_send()
        for k in near_by:
            for n in range(4):
                acts_copy(n, k, k >= PLANE).wait_send()


def deliver_kernel(attended_ref, delta_ref, attended_out, delta_out, sems):
    copies = [
        pltpu.make_async_copy(attended_ref, attended_out, sems.at[0]),
        pltpu.make_async_copy(delta_ref, delta_out, sems.at[1]),
    ]
    for copy in copies:
        copy.start()
    for copy in copies:
        copy.wait()


def deliver(attended, delta):
    return pl.pallas_call(
        deliver_kernel,
        out_shape=tuple(jax.ShapeDtypeStruct(a.shape, a.dtype) for a in (attended, delta)),
        in_specs=[ON_CHIP, ON_CHIP],
        out_specs=(ANYWHERE, ANYWHERE),
        scratch_shapes=[pltpu.SemaphoreType.DMA((2,))],
        compiler_params=pltpu.CompilerParams(vmem_limit_bytes=56 * 1024 * 1024),
    )(attended, delta)


def fused(owner, stretch, x, pool, query_rows, key_rows, value_rows, cosine, sine):
    items = item_table(2 * PLANE)
    tokens = x.shape[0]
    bf16 = jnp.bfloat16
    f32 = jnp.float32
    dma = pltpu.SemaphoreType.DMA
    vmem = pltpu.VMEM
    count = len(items)
    sizes = [rows for _, _, rows in items]

    def each(*lead):
        return [vmem(lead + (rows, LANES), bf16) for rows in sizes]

    down_rows, in_rows, out_rows = section_rows()
    final = [
        vmem(((2, 2) if i < DOWN_CHUNKS else (PLANE, 2)) + (rows, LANES), bf16)
        for i, rows in enumerate(sizes)
    ]
    end_width = D // (2 * PLANE) * (DOWN_CHUNKS - INNER_CHUNKS) // DOWN_CHUNKS
    heads = QH // KEYVALUE_HEADS
    kv_columns = 2 * KEYVALUE_HEADS * HEAD_SIZE
    devices = 4 * PLANE
    scratch = [
        [vmem((PLANE, 1, rows * LANES), bf16) for rows in sizes],
        each(PLANE),
        each(PLANE),
        each(2),
        each(2),
        each(2),
        each(2),
        each(2),
        each(),
        final,
        vmem((4, PLANE, tokens, end_width), bf16),
        vmem((sizes[0], LANES), f32),
        vmem((2 * sizes[0] // 3, LANES), f32),
        vmem((2 * sizes[0] // 3, LANES), f32),
        vmem((4, end_width, 2 * LANES), bf16),
        vmem((PLANE, tokens, 2 * LANES), f32),
        vmem((PLANE, tokens, 2 * LANES), bf16),
        vmem((3, tokens, 2 * LANES), bf16),
        vmem((in_rows, LANES), f32),
        vmem((ADAPTER_RANK * D // LANES, LANES), f32),
        vmem((KEYVALUE_HEADS, heads * tokens, HEAD_SIZE), bf16),
        vmem((devices, tokens, kv_columns), bf16),
        vmem((tokens, QH * HEAD_SIZE), bf16),
        vmem((KEYVALUE_HEADS, heads * tokens, 1), f32),
        vmem((KEYVALUE_HEADS, heads * tokens, 1), f32),
        vmem((KEYVALUE_HEADS, heads * tokens, HEAD_SIZE), f32),
        vmem((1, LANES), jnp.int32),
        vmem((1, LANES), jnp.int32),
        pltpu.SMEM((2, 1, LANES), jnp.int32),
        dma((count, PLANE)),
        dma((count, PLANE)),
        dma((count, PLANE)),
        dma((count, 8)),
        dma((count, 8)),
        dma((4, 2 * PLANE)),
        dma((4, 2 * PLANE)),
        dma((4,)),
        dma,
        dma,
        dma((2,)),
        dma((2 * PLANE,)),
        dma((2 * PLANE,)),
        dma((4, 4)),
        dma((4, 4)),
    ]
    return pl.pallas_call(
        partial(fused_kernel, items),
        out_shape=(
            jax.ShapeDtypeStruct((tokens, QH * HEAD_SIZE), bf16),
            jax.ShapeDtypeStruct((tokens, D), bf16),
        ),
        in_specs=[SCALARS, SCALARS, ANYWHERE, ANYWHERE] + [ON_CHIP] * 5,
        out_specs=(ON_CHIP, ON_CHIP),
        scratch_shapes=scratch,
        compiler_params=pltpu.CompilerParams(
            collective_id=2, has_side_effects=True, vmem_limit_bytes=60 * 1024 * 1024
        ),
    )(owner, stretch, x, pool, query_rows, key_rows, value_rows, cosine, sine)


def shards(
    normed_input, query_base, key_base, value_base, adapter_pool, stretch_adapter, adapter_owner
):
    cycle_size = lax.axis_size("ctx")
    my_index = lax.axis_index("ctx")
    tok_rows = normed_input.shape[0]
    token_positions = my_index * tok_rows + jnp.arange(tok_rows, dtype=jnp.int32)
    groups = lax.axis_size("groups")
    cube = BLOCK_TOKENS // tok_rows
    cubes = cycle_size // cube
    down_size = 3 * ADAPTER_RANK * D
    half_dim = HEAD_SIZE // 2
    frequency = rope_base ** (-(jnp.arange(half_dim, dtype=jnp.float32) * 2.0) / HEAD_SIZE)
    angle = token_positions.astype(jnp.float32)[:, None] * frequency[None, :]
    cosine = jnp.cos(angle)
    sine = jnp.sin(angle)
    cosine = jnp.concatenate([cosine, cosine], axis=1)
    sine = jnp.concatenate([-sine, sine], axis=1)
    if groups == 2 and cube == 2 * PLANE and cubes == 2:
        return deliver(*fused(
            adapter_owner, stretch_adapter, normed_input, adapter_pool,
            query_base, key_base, value_base, cosine, sine,
        ))
    padding = -stretch_adapter.shape[0] % LANES
    stretch_row = jnp.pad(stretch_adapter, (0, padding))[None]
    moved, down_slice, rest = place_adapter(
        groups, cubes, cube, down_size, adapter_owner, stretch_row, normed_input, adapter_pool
    )
    rest = rest.reshape(-1, LANES)
    queries, gathered = keyval(
        cube,
        cycle_size,
        moved,
        down_slice.reshape(D // cube, 3 * ADAPTER_RANK),
        rest,
        query_base,
        key_base,
        value_base,
        cosine,
        sine,
    )
    gathered = gathered.reshape(cycle_size * tok_rows, -1)
    return attend(queries, gathered, rest)


def solution(mesh):
    placed = (
        P(("groups", "ctx"), None),
        P(("groups", "ctx"), None),
        P(("groups", "ctx"), None),
        P(("groups", "ctx"), None),
        P("ctx", None),
        P("groups"),
        P(),
    )
    return jax.shard_map(
        shards,
        mesh=mesh,
        in_specs=placed,
        out_specs=(P(("groups", "ctx"), None), P(("groups", "ctx"), None)),
        check_vma=False,
    )
```

```python
from functools import partial
import math

import jax
import jax.numpy as jnp
from jax import lax
from jax.experimental import pallas as pl
from jax.experimental.pallas import tpu as pltpu
from jax.sharding import PartitionSpec as P

D = 8192
QH = 32
KEYVALUE_HEADS = 4
HEAD_SIZE = 128
ADAPTER_RANK = 64
BLOCK_TOKENS = 512
QKV_POOL = 1900544


adapter_scale = 2.0
rope_base = 500000.0
mask_floor = -1e30


LANES = 128
MESH = pl.DeviceIdType.MESH
ON_CHIP = pl.BlockSpec(memory_space=pltpu.VMEM)
ANYWHERE = pl.BlockSpec(memory_space=pl.ANY)
SCALARS = pl.BlockSpec(memory_space=pltpu.SMEM)


def remote(src, dst, send_sem, recv_sem, group, ctx):
    return pltpu.make_async_remote_copy(
        src_ref=src,
        dst_ref=dst,
        send_sem=send_sem,
        recv_sem=recv_sem,
        device_id=(group, ctx),
        device_id_type=MESH,
    )


def place_adapter_kernel(
    groups, cubes, cube, down_size,
    owner_ref, stretch_ref, x_ref, pool_ref,
    x_out, down_out, rest_out,
    down_flat, rest_flat, down_source, rest_source,
    down_rows, rest_rows, down_send, rest_send, down_land, rest_land,
    stretch_land, table,
    s_flat, s_cube, r_cube, s_far, r_far, s_tree, r_tree, s_own, s_row, r_row, s_table,
):
    group = lax.axis_index("groups")
    ctx = lax.axis_index("ctx")
    inner = ctx % cube
    outer = ctx // cube
    home = group * cubes + outer
    kinds = groups * cubes
    width = x_out.shape[2] // groups
    down_piece = down_flat.shape[2]
    rest_piece = rest_flat.shape[2]

    def read_piece(row, k):
        piece = (rest_piece, down_piece)[row]
        start = (group * cube + (inner ^ k)) * piece + (down_size, 0)[row]
        return pltpu.make_async_copy(
            pool_ref.at[:, pl.ds(pl.multiple_of(start, LANES), piece)],
            (rest_flat, down_flat)[row].at[k],
            s_flat.at[row, k],
        )

    for row in range(2):
        for k in reversed(range(cube)):
            read_piece(row, k).start()

    barrier = pltpu.get_barrier_semaphore()
    for k in range(1, cube):
        pl.semaphore_signal(
            barrier, inc=1, device_id=(group, outer * cube + (inner ^ k)), device_id_type=MESH
        )
    for k in range(1, kinds):
        there = home ^ k
        pl.semaphore_signal(
            barrier,
            inc=1,
            device_id=(there // cubes, (there % cubes) * cube + inner),
            device_id_type=MESH,
        )
    pl.semaphore_wait(barrier, cube - 1 + kinds - 1)
    row_copies = []
    for step in range(1, groups):
        copy = remote(
            stretch_ref, stretch_land.at[step], s_row.at[step], r_row.at[step], group ^ step, ctx
        )
        copy.start()
        row_copies.append(copy)

    def columns(part, owner):
        return pl.ds(pl.multiple_of((part * cube + owner) * width, width), width)

    def cube_copy(row, k):
        peer = inner ^ k
        return remote(
            (rest_source, down_source)[row].at[k], (rest_rows, down_rows)[row].at[inner],
            s_cube.at[row, k], r_cube.at[row, k], group, outer * cube + peer,
        )

    def dense(row, k):
        flat = (rest_flat, down_flat)[row][k].astype(jnp.float32)
        return flat.reshape(-1, LANES).astype(jnp.bfloat16)

    def x_copy(part, k):
        peer = inner ^ k
        return remote(
            x_ref.at[:, columns(part, peer)],
            x_out.at[inner, :, pl.ds(part * width, width)],
            s_cube.at[2 + part, k], r_cube.at[2 + part, k],
            group, outer * cube + peer,
        )

    for row, (source, rows) in enumerate(((rest_source, rest_rows), (down_source, down_rows))):

        def spread(step, carry, row=row, source=source):
            k = cube - 1 - step
            read_piece(row, k).wait()
            source[k] = dense(row, k)
            cube_copy(row, k).start()
            return carry

        lax.fori_loop(0, cube - 1, spread, 0)
        read_piece(row, 0).wait()
        rows[inner] = dense(row, 0)

    to_table = [pltpu.make_async_copy(stretch_ref, table.at[0], s_table.at[0])]
    to_table[0].start()
    for step, copy in zip(range(1, groups), row_copies):
        copy.wait_recv()
        move = pltpu.make_async_copy(stretch_land.at[step], table.at[step], s_table.at[step])
        move.start()
        to_table.append(move)
    for move in to_table:
        move.wait()

    def slot_of(k):
        return owner_ref[table[k // cubes, 0, outer ^ (k % cubes)]]

    def chosen(part):
        return (part * cubes + lax.div(slot_of(0), cube)) ^ home

    owns = []
    for part in range(groups):
        own = pltpu.make_async_copy(
            x_ref.at[:, columns(part, inner)],
            x_out.at[inner, :, pl.ds(part * width, width)],
            s_own.at[part],
        )
        own.start()
        owns.append(own)

    far = []
    for row, (rows, outgoing, landing) in enumerate(
        ((rest_rows, rest_send, rest_land), (down_rows, down_send, down_land))
    ):
        for k in range(1, cube):
            cube_copy(row, k).wait_recv()
        coming = []
        for k in range(1, kinds):
            there = home ^ k
            outgoing[k] = rows[lax.rem(slot_of(k), cube)]
            copy = remote(
                outgoing.at[k], landing.at[k], s_far.at[row, k], r_far.at[row, k],
                there // cubes, (there % cubes) * cube + inner,
            )
            copy.start()
            coming.append(copy)
        landing[0] = rows[lax.rem(slot_of(0), cube)]
        far.append(coming)

    for copy in far[0]:
        copy.wait_recv()
    for part in range(groups):
        rest_out[part, inner] = rest_land[chosen(part)]
    tree = {}
    have = [[0] for _ in range(groups)]
    levels = cube.bit_length() - 1
    orders = []
    for part in range(groups):
        order = [1 << level for level in reversed(range(levels))]
        if part % 2:
            order[:2] = order[1::-1]
        orders.append(order)
    for stage in range(levels):
        for part in range(groups):
            bit = orders[part][stage]
            before = orders[part][stage - 1] if stage else 0
            for k in have[part]:
                if k & before:
                    tree[k, part].wait_recv()
            new = []
            for k in have[part]:
                slot = rest_out.at[part, inner ^ k]
                copy = remote(
                    slot, slot, s_tree.at[part, k ^ bit], r_tree.at[part, k ^ bit],
                    group, outer * cube + (inner ^ bit),
                )
                copy.start()
                tree[k ^ bit, part] = copy
                new.append(k ^ bit)
            have[part] = have[part] + new
        if stage == 0:
            for part in range(groups):
                for k in reversed(range(1, cube)):
                    x_copy(part, k).start()

    for copy in far[1]:
        copy.wait_recv()
    for part in range(groups):
        down_out[part] = down_land[chosen(part)]
    for (k, part), copy in tree.items():
        if k & orders[part][-1]:
            copy.wait_recv()
    for own in owns:
        own.wait()
    for part in range(groups):
        for k in range(1, cube):
            x_copy(part, k).wait_recv()
            x_copy(part, k).wait_send()
    for row in range(2):
        for k in range(1, cube):
            cube_copy(row, k).wait_send()
    for copy in row_copies + far[0] + far[1] + list(tree.values()):
        copy.wait_send()


def place_adapter(groups, cubes, cube, down_size, owner, stretch_row, x, pool):
    kinds = groups * cubes
    tokens, depth = x.shape
    down_piece = down_size // (groups * cube)
    rest_piece = (pool.shape[1] - down_size) // (groups * cube)
    down_shape = (down_piece // LANES, LANES)
    rest_shape = (rest_piece // LANES, LANES)
    bf16 = jnp.bfloat16
    dma = pltpu.SemaphoreType.DMA
    return pl.pallas_call(
        partial(place_adapter_kernel, groups, cubes, cube, down_size),
        out_shape=(
            jax.ShapeDtypeStruct((cube, tokens, depth // cube), bf16),
            jax.ShapeDtypeStruct((groups,) + down_shape, bf16),
            jax.ShapeDtypeStruct((groups, cube) + rest_shape, bf16),
        ),
        in_specs=[SCALARS, ON_CHIP, ON_CHIP, pl.BlockSpec(memory_space=pl.ANY)],
        out_specs=(ON_CHIP, ON_CHIP, ON_CHIP),
        scratch_shapes=[
            pltpu.VMEM((cube, 1, down_piece), bf16),
            pltpu.VMEM((cube, 1, rest_piece), bf16),
            pltpu.VMEM((cube,) + down_shape, bf16),
            pltpu.VMEM((cube,) + rest_shape, bf16),
            pltpu.VMEM((cube,) + down_shape, bf16),
            pltpu.VMEM((cube,) + rest_shape, bf16),
            pltpu.VMEM((kinds,) + down_shape, bf16),
            pltpu.VMEM((kinds,) + rest_shape, bf16),
            pltpu.VMEM((kinds,) + down_shape, bf16),
            pltpu.VMEM((kinds,) + rest_shape, bf16),
            pltpu.VMEM((groups,) + stretch_row.shape, jnp.int32),
            pltpu.SMEM((groups,) + stretch_row.shape, jnp.int32),
            dma((2, cube)),
            dma((2 + groups, cube)),
            dma((2 + groups, cube)),
            dma((2, kinds)),
            dma((2, kinds)),
            dma((groups, cube)),
            dma((groups, cube)),
            dma((groups,)),
            dma((groups,)),
            dma((groups,)),
            dma((groups,)),
        ],
        compiler_params=pltpu.CompilerParams(
            collective_id=0, has_side_effects=True, vmem_limit_bytes=60 * 1024 * 1024
        ),
    )(owner, stretch_row, x, pool)


def keyval_kernel(
    cube, count,
    x_any, w_ref, rest_any, query_ref, key_ref, value_ref, cos_ref, sin_ref,
    query_out, out_ref,
    x_ref, up_ref, s_in, wide, total, outgoing, landing, s_sem, r_sem, s_all, r_all,
):
    group = lax.axis_index("groups")
    ctx = lax.axis_index("ctx")
    inner = ctx % cube
    outer = ctx // cube
    levels = count.bit_length() - 1
    x_in = pltpu.make_async_copy(x_any, x_ref, s_in.at[0])
    x_in.start()
    up_in = pltpu.make_async_copy(
        rest_any.at[pl.ds(0, up_ref.shape[0])], up_ref, s_in.at[1]
    )
    up_in.start()
    barrier = pltpu.get_barrier_semaphore()
    apart = list(range(1, cube)) + [1 << n for n in range(levels) if 1 << n >= cube]
    for k in apart:
        pl.semaphore_signal(barrier, inc=1, device_id=(group, ctx ^ k), device_id_type=MESH)
    _, tokens, depth = x_ref.shape
    x_in.wait()
    product = jnp.dot(
        x_ref[...].reshape(cube * tokens, depth), w_ref[...], preferred_element_type=jnp.float32
    ).reshape(cube, tokens, w_ref.shape[1])
    total[...] = product
    outgoing[...] = product.astype(jnp.bfloat16)
    pl.semaphore_wait(barrier, len(apart))
    copies = []
    for k in range(1, cube):
        peer = inner ^ k
        copy = remote(
            outgoing.at[peer], landing.at[k], s_sem.at[k], r_sem.at[k], group, outer * cube + peer
        )
        copy.start()
        copies.append(copy)
    up_in.wait()
    wide[...] = up_ref[...].astype(jnp.float32)
    result = total[inner]
    for k, copy in zip(range(1, cube), copies):
        copy.wait_recv()
        result = result + landing[k].astype(jnp.float32)
    low = result.astype(jnp.bfloat16)
    half = HEAD_SIZE // 2
    query_rows = ADAPTER_RANK * QH
    kinds = 2 * KEYVALUE_HEADS
    for j in range(2 * KEYVALUE_HEADS):
        first = ADAPTER_RANK * (1 if j < KEYVALUE_HEADS else 2)
        delta = adapter_scale * jnp.dot(
            low[:, first : first + ADAPTER_RANK],
            wide[pl.ds(query_rows + j, ADAPTER_RANK, stride=kinds), :].astype(jnp.bfloat16),
            preferred_element_type=jnp.float32
        )
        base_ref = key_ref if j < KEYVALUE_HEADS else value_ref
        head = j % KEYVALUE_HEADS
        if j < KEYVALUE_HEADS:
            swapped = jnp.concatenate([delta[:, half:], delta[:, :half]], axis=1)
            delta = delta * cos_ref[...] + swapped * sin_ref[...]
        base = base_ref[:, head * HEAD_SIZE : (head + 1) * HEAD_SIZE].astype(jnp.float32)
        out_ref[ctx, :, j * HEAD_SIZE : (j + 1) * HEAD_SIZE] = (base + delta).astype(jnp.bfloat16)

    def query_head(head):
        up = wide[pl.ds(head, ADAPTER_RANK, stride=QH), :].astype(jnp.bfloat16)
        delta = adapter_scale * jnp.dot(
            low[:, :ADAPTER_RANK], up, preferred_element_type=jnp.float32
        )
        swapped = jnp.concatenate([delta[:, half:], delta[:, :half]], axis=1)
        delta = delta * cos_ref[...] + swapped * sin_ref[...]
        base = query_ref[:, head * HEAD_SIZE : (head + 1) * HEAD_SIZE].astype(jnp.float32)
        shared = QH // KEYVALUE_HEADS
        query_out[
            head // shared, (head % shared) * tokens : (head % shared + 1) * tokens, :
        ] = (base + delta).astype(jnp.bfloat16)

    kv_width = KEYVALUE_HEADS * HEAD_SIZE
    far_first = [1 << level for level in reversed(range(levels))]
    orders = (far_first, [2] + [bit for bit in far_first if bit != 2])
    have = [[0], [0]]
    moved = {}
    done = 0
    for stage in range(levels):
        for part in range(2):
            bit = orders[part][stage]
            before = orders[part][stage - 1] if stage else 0
            new = []
            for k in have[part]:
                if k & before:
                    moved[k, part].wait_recv()
                slot = out_ref.at[ctx ^ k, :, pl.ds(part * kv_width, kv_width)]
                copy = remote(
                    slot, slot, s_all.at[part, k ^ bit], r_all.at[part, k ^ bit], group, ctx ^ bit
                )
                copy.start()
                moved[k ^ bit, part] = copy
                new.append(k ^ bit)
            have[part] = have[part] + new
        until = QH * (stage + 1) // levels
        for head in range(done, until):
            query_head(head)
        done = until
    for (k, part), copy in moved.items():
        if k & orders[part][-1]:
            copy.wait_recv()
    for copy in copies + list(moved.values()):
        copy.wait_send()


def keyval(cube, count, x, w, rest, query_rows, key_rows, value_rows, cosine, sine):
    _, tokens, _ = x.shape
    shape = (cube, tokens, w.shape[1])
    up_rows = ADAPTER_RANK * (QH + 2 * KEYVALUE_HEADS)
    dma = pltpu.SemaphoreType.DMA
    return pl.pallas_call(
        partial(keyval_kernel, cube, count),
        out_shape=(
            jax.ShapeDtypeStruct(
                (KEYVALUE_HEADS, QH // KEYVALUE_HEADS * tokens, HEAD_SIZE), jnp.bfloat16
            ),
            jax.ShapeDtypeStruct(
                (count, tokens, 2 * KEYVALUE_HEADS * HEAD_SIZE), jnp.bfloat16
            ),
        ),
        in_specs=[ANYWHERE, ON_CHIP, ANYWHERE] + [ON_CHIP] * 5,
        out_specs=(ON_CHIP, ON_CHIP),
        scratch_shapes=[
            pltpu.VMEM(x.shape, jnp.bfloat16),
            pltpu.VMEM((up_rows, LANES), jnp.bfloat16),
            dma((2,)),
            pltpu.VMEM((up_rows, LANES), jnp.float32),
            pltpu.VMEM(shape, jnp.float32),
            pltpu.VMEM(shape, jnp.bfloat16),
            pltpu.VMEM(shape, jnp.bfloat16),
            dma((cube,)),
            dma((cube,)),
            dma((2, count)),
            dma((2, count)),
        ],
        compiler_params=pltpu.CompilerParams(
            collective_id=1, has_side_effects=True, vmem_limit_bytes=40 * 1024 * 1024
        ),
    )(x, w, rest, query_rows, key_rows, value_rows, cosine, sine)


def attend_kernel(
    step_keys, queries, kv_ref, rest_any,
    attended_ref, delta_ref,
    rest_ref, s_in, wide, permuted, run_max, run_sum, run_acc,
):
    tokens = attended_ref.shape[0]
    ctx = lax.axis_index("ctx")
    heads = QH // KEYVALUE_HEADS
    rows = heads * tokens
    half = HEAD_SIZE // 2
    query_rows = ADAPTER_RANK * QH
    raise_start = QH * half
    rest_in = pltpu.make_async_copy(
        rest_any.at[pl.ds(query_rows + 2 * ADAPTER_RANK * KEYVALUE_HEADS, rest_ref.shape[0])],
        rest_ref,
        s_in,
    )
    rest_in.start()
    first = ctx * tokens
    steps = (first + tokens + step_keys - 1) // step_keys
    row = lax.broadcasted_iota(jnp.int32, (rows, step_keys), 0)
    query_pos = first + lax.rem(row, tokens)
    key_off = lax.broadcasted_iota(jnp.int32, (rows, step_keys), 1)
    source = lax.broadcasted_iota(jnp.int32, (HEAD_SIZE, HEAD_SIZE), 0)
    target = lax.broadcasted_iota(jnp.int32, (HEAD_SIZE, HEAD_SIZE), 1)
    wanted = jnp.where(target < half, 2 * target, 2 * (target - half) + 1)
    shuffle = jnp.where(source == wanted, 1.0, 0.0).astype(jnp.bfloat16)
    for group in range(KEYVALUE_HEADS):
        run_max[...] = jnp.full_like(run_max, mask_floor)
        run_sum[...] = jnp.zeros_like(run_sum)
        run_acc[...] = jnp.zeros_like(run_acc)
        key_cols = slice(group * HEAD_SIZE, (group + 1) * HEAD_SIZE)
        value_first = (KEYVALUE_HEADS + group) * HEAD_SIZE

        def advance(step, carry):
            start = pl.multiple_of(step * step_keys, step_keys)
            keys = kv_ref[pl.ds(start, step_keys), key_cols]
            values = kv_ref[pl.ds(start, step_keys), value_first : value_first + HEAD_SIZE]
            scores = lax.dot_general(
                queries[group], keys, (((1,), (1,)), ((), ())),
                preferred_element_type=jnp.float32,
            ) * HEAD_SIZE ** (-0.5)
            scores = jnp.where(query_pos >= key_off + start, scores, mask_floor)
            new_max = jnp.maximum(run_max[...], jnp.max(scores, axis=1, keepdims=True))
            weights = jnp.exp(scores - new_max)
            rescale = jnp.exp(run_max[...] - new_max)
            run_sum[...] = run_sum[...] * rescale + jnp.sum(weights, axis=1, keepdims=True)
            run_acc[...] = run_acc[...] * rescale + jnp.dot(
                weights.astype(jnp.bfloat16), values, preferred_element_type=jnp.float32
            )
            run_max[...] = new_max
            return carry

        lax.fori_loop(0, steps, advance, 0)
        result = (run_acc[...] / run_sum[...]).astype(jnp.bfloat16)
        mixed = jnp.dot(result, shuffle, preferred_element_type=jnp.float32).astype(jnp.bfloat16)
        for j in range(heads):
            head = group * heads + j
            cols = slice(head * HEAD_SIZE, (head + 1) * HEAD_SIZE)
            attended_ref[:, cols] = result[j * tokens : (j + 1) * tokens]
            permuted[:, cols] = mixed[j * tokens : (j + 1) * tokens]
    rest_in.wait()
    wide[...] = rest_ref[raise_start:, :].astype(jnp.float32)
    narrow = jnp.zeros((tokens, ADAPTER_RANK), jnp.float32)
    for head in range(QH):
        block = rest_ref[head * half : (head + 1) * half, :]
        weight = jnp.concatenate([block[:, :half], block[:, half:]], axis=0)
        narrow = narrow + jnp.dot(
            permuted[:, head * HEAD_SIZE : (head + 1) * HEAD_SIZE],
            weight,
            preferred_element_type=jnp.float32,
        )
    narrow = narrow.astype(jnp.bfloat16)
    blocks = D // LANES
    for j in range(blocks):
        up = wide[pl.ds(j, ADAPTER_RANK, stride=blocks), :].astype(jnp.bfloat16)
        delta_ref[:, j * LANES : (j + 1) * LANES] = (
            adapter_scale * jnp.dot(narrow, up, preferred_element_type=jnp.float32)
        ).astype(jnp.bfloat16)


def attend(queries, kv, rest):
    rows = queries.shape[1]
    tokens = rows // (QH // KEYVALUE_HEADS)
    out_rows = ADAPTER_RANK * (QH * HEAD_SIZE + D) // LANES
    return pl.pallas_call(
        partial(attend_kernel, math.gcd(kv.shape[0], 1024)),
        out_shape=(
            jax.ShapeDtypeStruct((tokens, QH * HEAD_SIZE), jnp.bfloat16),
            jax.ShapeDtypeStruct((tokens, D), jnp.bfloat16),
        ),
        in_specs=[ON_CHIP, ON_CHIP, ANYWHERE],
        out_specs=(ON_CHIP, ON_CHIP),
        scratch_shapes=[
            pltpu.VMEM((out_rows, LANES), jnp.bfloat16),
            pltpu.SemaphoreType.DMA,
            pltpu.VMEM((ADAPTER_RANK * D // LANES, LANES), jnp.float32),
            pltpu.VMEM((tokens, QH * HEAD_SIZE), jnp.bfloat16),
            pltpu.VMEM((rows, 1), jnp.float32),
            pltpu.VMEM((rows, 1), jnp.float32),
            pltpu.VMEM((rows, HEAD_SIZE), jnp.float32),
        ],
        compiler_params=pltpu.CompilerParams(vmem_limit_bytes=56 * 1024 * 1024),
    )(queries, kv, rest)


PLANE = 4
DOWN_CHUNKS = 8
INNER_CHUNKS = 2
EARLY_CHUNKS = 3
OUT_CHUNKS = 2
FAR, NEAR, MID, BACK, CROSS, WIDE, PAIR, PAIR2 = range(8)


def section_rows():
    down = 3 * ADAPTER_RANK * D // LANES
    inner = ADAPTER_RANK * (QH + 2 * KEYVALUE_HEADS) * HEAD_SIZE // LANES
    outer = ADAPTER_RANK * (QH * HEAD_SIZE + D) // LANES
    return down, inner, outer


def item_table(slices):
    items = []
    first = 0
    for rows, chunks in zip(section_rows(), (DOWN_CHUNKS, 1, OUT_CHUNKS)):
        piece = rows // slices
        for chunk in range(chunks):
            items.append((first + chunk * (piece // chunks), piece, piece // chunks))
        first += rows
    return items


def fused_kernel(
    items,
    owner_ref, stretch_ref, x_any, pool_any, query_ref, key_ref, value_ref, cos_ref, sin_ref,
    attended_ref, delta_ref,
    flat, source, held, first_out, second_out, far_in, near_in, mid_in, cross_out, final,
    acts, spread_w, packed_a, packed_b, weights, total, low_out, low_in, wide_in, wide_out, queries, kv, permuted,
    run_max, run_sum, run_acc, row_out, row_in, table,
    s_flat, s_plane, r_plane, s_move, r_move, s_acts, r_acts, s_own, s_row, r_row, s_table,
    s_low, r_low, s_keys, r_keys,
):
    group = lax.axis_index("groups")
    ctx = lax.axis_index("ctx")
    lane = ctx % PLANE
    side = lane // 2
    core = lane % 2
    level = ctx // PLANE
    half_of = level // 2
    is_end = (level == 0) | (level == 3)
    is_inner = (level == 1) | (level == 2)
    tokens = x_any.shape[0]
    count = len(items)
    down_items = list(range(DOWN_CHUNKS))
    in_item = DOWN_CHUNKS
    end_items = down_items[:-INNER_CHUNKS]
    inner_items = down_items[-INNER_CHUNKS:]
    order = down_items[:EARLY_CHUNKS] + [in_item] + down_items[EARLY_CHUNKS:]
    out_items = list(range(DOWN_CHUNKS + 1, count))

    def read_piece(i, k):
        first, piece, rows = items[i]
        begin = (first + (group * PLANE + (lane ^ k)) * piece) * LANES
        return pltpu.make_async_copy(
            pool_any.at[:, pl.ds(pl.multiple_of(begin, LANES), rows * LANES)],
            flat[i].at[k],
            s_flat.at[i, k],
        )

    for i in range(count):
        for k in reversed(range(PLANE)):
            read_piece(i, k).start()

    def dense(i, k):
        return flat[i][k].astype(jnp.float32).reshape(-1, LANES).astype(jnp.bfloat16)

    def prepare(i):
        def step(n, carry):
            k = PLANE - 1 - n
            read_piece(i, k).wait()
            source[i][k] = dense(i, k)
            return carry

        lax.fori_loop(0, PLANE - 1, step, 0)
        read_piece(i, 0).wait()
        held[i][lane] = dense(i, 0)

    barrier = pltpu.get_barrier_semaphore()
    greeted = (1, 2, 3, 4, 5, 8, 12)
    for k in greeted:
        pl.semaphore_signal(barrier, inc=1, device_id=(group, ctx ^ k), device_id_type=MESH)
    pl.semaphore_signal(barrier, inc=1, device_id=(group ^ 1, ctx), device_id_type=MESH)
    mine_row = lax.broadcasted_iota(jnp.int32, row_out.shape, 1)
    row_out[...] = jnp.where(mine_row == 0, stretch_ref[0], stretch_ref[1])
    for i in order[:2]:
        prepare(i)
    pl.semaphore_wait(barrier, len(greeted) + 1)

    row_copy = remote(row_out, row_in, s_row, r_row, group ^ 1, ctx)
    row_copy.start()
    own_row = pltpu.make_async_copy(row_out, table.at[0], s_table.at[0])
    own_row.start()

    def plane_copy(i, k):
        return remote(
            source[i].at[k], held[i].at[lane], s_plane.at[i, k], r_plane.at[i, k], group, ctx ^ k
        )

    def scatter(i):
        for k in reversed(range(1, PLANE)):
            plane_copy(i, k).start()

    def slot(which, part):
        return owner_ref[table[which, 0, part]]

    def mine(which, part, where):
        return lax.div(slot(which, part), PLANE) == where

    def own_candidate(i, which, part):
        return held[i][lax.rem(slot(which, part), PLANE)]

    def move(i, kind):
        if kind == FAR:
            src, dst, there = first_out[i], far_in[i], (group, ctx ^ PLANE)
        elif kind == NEAR:
            src, dst, there = second_out[i], near_in[i], (group, ctx ^ PLANE)
        elif kind == MID:
            src, dst, there = first_out[i], mid_in[i], (group, ctx ^ (3 * PLANE))
        elif kind == BACK:
            src, dst, there = second_out[i], far_in[i], (group, ctx ^ PLANE)
        elif kind == CROSS:
            place = final[i].at[side, group] if i < in_item else final[i].at[lane, group]
            src, dst, there = cross_out[i], place, (group ^ 1, ctx)
        elif kind == WIDE:
            src = dst = final[i].at[side if i < in_item else lane]
            there = (group, ctx ^ 2)
        elif kind == PAIR:
            src = dst = final[i].at[lane]
            there = (group, ctx ^ 1)
        else:
            src = dst = final[i].at[lane ^ 2]
            there = (group, ctx ^ 1)
        return remote(src, dst, s_move.at[i, kind], r_move.at[i, kind], *there)

    def landed(i):
        for k in range(1, PLANE):
            plane_copy(i, k).wait_recv()

    def end_far(i):
        landed(i)
        for which in range(2):
            first_out[i][which] = own_candidate(i, which, 1 - half_of)
        move(i, FAR).start()

    def end_near(i):
        for which in range(2):
            second_out[i][which] = own_candidate(i, which, half_of)
        move(i, NEAR).start()

    def end_send(i):
        end_far(i)
        if i not in end_items:
            end_near(i)

    def settle(i, other_value, own_value):
        cross_out[i][...] = other_value
        move(i, CROSS).start()
        if i < in_item:
            final[i][side, group] = own_value
        else:
            final[i][lane, group] = own_value

    def end_settle(i):
        move(i, BACK).wait_recv()

        def value(which):
            return jnp.where(
                mine(which, half_of, level), own_candidate(i, which, half_of), far_in[i][which]
            )

        settle(i, value(1), value(0))

    def inner_across(i):
        landed(i)
        move(i, FAR).wait_recv()
        for which in range(2):
            first_out[i][which] = jnp.where(
                mine(which, 1 - half_of, level),
                own_candidate(i, which, 1 - half_of),
                far_in[i][which],
            )
        move(i, MID).start()

    def inner_back(i):
        move(i, MID).wait_recv()
        for which in range(2):
            second_out[i][which] = jnp.where(
                mine(which, half_of, level),
                own_candidate(i, which, half_of),
                mid_in[i][which],
            )
        if i not in inner_items:
            move(i, BACK).start()

    def inner_settle(i):
        move(i, NEAR).wait_recv()

        def value(which):
            return jnp.where(
                mine(which, half_of, level ^ 1), near_in[i][which], second_out[i][which]
            )

        settle(i, value(1), value(0))

    def gather_wide(i):
        move(i, CROSS).wait_recv()
        move(i, WIDE).start()
        move(i, PAIR).start()

    def gather_pair(i):
        move(i, WIDE).wait_recv()
        move(i, PAIR2).start()

    def gathered(i):
        move(i, PAIR).wait_recv()
        move(i, PAIR2).wait_recv()

    strip = D // (2 * PLANE)
    inner_width = strip * INNER_CHUNKS // DOWN_CHUNKS
    end_width = strip - inner_width

    near_by = (1, PLANE, PLANE + 1)

    def member(k):
        return k // PLANE * 2 + (core ^ (k % 2))

    def acts_copy(n, k, to_end):
        width = end_width if to_end else inner_width
        part, wing = n // 2, n % 2
        begin = (part * PLANE + wing * 2 + (core ^ (k % 2))) * strip + (0 if to_end else end_width)
        src = x_any.at[:, pl.ds(pl.multiple_of(begin, LANES), width)]
        dst = acts.at[n, k // PLANE * 2 + core, :, pl.ds(0, width)]
        if k == 0:
            return pltpu.make_async_copy(src, dst, s_own.at[n])
        return remote(src, dst, s_acts.at[n, k], r_acts.at[n, k], group, ctx ^ k)

    def acts_send():
        @pl.when(is_end)
        def _():
            for k in (PLANE, PLANE + 1, 1, 0):
                for n in range(4):
                    acts_copy(n, k, k < PLANE).start()

        @pl.when(is_inner)
        def _():
            for k in (PLANE, PLANE + 1, 1, 0):
                for n in range(4):
                    acts_copy(n, k, k >= PLANE).start()

    def acts_landed(to_end):
        for n in range(4):
            acts_copy(n, 0, to_end).wait()
            for k in near_by:
                acts_copy(n, k, to_end).wait_recv()

    def widen(i):
        move(i, CROSS).wait_recv()
        move(i, WIDE).start()

    def convert(i):
        move(i, WIDE).wait_recv()
        pairs = 2 * final[i].shape[2] // 3
        third = pairs // 2
        half = LANES // 2
        row = (i - (inner_items[0] if i in inner_items else 0)) * pairs
        for n in range(4):
            part, wing = n // 2, n % 2
            spread_w[...] = final[i][wing, part].astype(jnp.float32)
            first = spread_w[pl.ds(0, third, stride=3), :]
            second = spread_w[pl.ds(1, third, stride=3), :]
            last = spread_w[pl.ds(2, third, stride=3), :]
            packed_a[pl.ds(0, third, stride=2), :] = first
            packed_b[pl.ds(0, third, stride=2), :] = second
            packed_a[pl.ds(1, third, stride=2), :] = jnp.concatenate(
                [second[:, half:], last[:, :half]], axis=1
            )
            packed_b[pl.ds(1, third, stride=2), :] = jnp.concatenate(
                [last[:, half:], last[:, :half]], axis=1
            )
            weights[n, row : row + pairs, 0:LANES] = packed_a[...].astype(jnp.bfloat16)
            weights[n, row : row + pairs, LANES : 2 * LANES] = packed_b[...].astype(jnp.bfloat16)

    def product(width):
        sum_now = None
        for n in range(4):
            chunk = acts[n, :, :, 0:width].reshape(PLANE * tokens, width)
            term = jnp.dot(chunk, weights[n, 0:width, :], preferred_element_type=jnp.float32)
            sum_now = term if sum_now is None else sum_now + term
        total[...] = sum_now.reshape(PLANE, tokens, 2 * LANES)

    acts_send()
    scatter(order[0])
    scatter(order[1])
    for i in order[2:]:
        prepare(i)
        scatter(i)
    row_copy.wait_recv()
    own_row.wait()
    other_row = pltpu.make_async_copy(row_in, table.at[1], s_table.at[1])
    other_row.start()
    other_row.wait()
    for i in out_items:
        prepare(i)
    lag = 4
    steps = len(order)

    def at(n):
        return order[n] if 0 <= n < steps else None

    @pl.when(is_end)
    def _():
        for n in range(steps + lag + 2):
            if at(n) is not None:
                end_send(at(n))
            if at(n - lag) is not None and at(n - lag) not in inner_items:
                end_settle(at(n - lag))
            if at(n - lag - 1) in end_items:
                widen(at(n - lag - 1))
                if at(n - lag - 1) == end_items[-5]:
                    scatter(out_items[0])
            if at(n - lag - 2) in end_items:
                convert(at(n - lag - 2))
        scatter(out_items[1])
        acts_landed(True)
        product(end_width)
        end_far(out_items[0])

    @pl.when(is_inner)
    def _():
        for i in out_items:
            scatter(i)
        for n in range(steps + 4):
            if at(n) is not None:
                inner_across(at(n))
            if at(n - 1) is not None:
                inner_back(at(n - 1))
            if at(n - 2) is not None and at(n - 2) not in end_items:
                inner_settle(at(n - 2))
            if at(n - 3) in inner_items:
                widen(at(n - 3))
            if at(n - 4) in inner_items:
                convert(at(n - 4))
        acts_landed(False)
        product(inner_width)

    def at_inner(step, i):
        @pl.when(is_inner)
        def _():
            step(i)

    def at_end(step, i):
        @pl.when(is_end)
        def _():
            step(i)

    def low_copy(k):
        return remote(
            low_out.at[member(k)], low_in.at[near_by.index(k)],
            s_low.at[k], r_low.at[k], group, ctx ^ k,
        )

    low_out[...] = total[...].astype(jnp.bfloat16)
    for k in near_by[1:] + near_by[:1]:
        low_copy(k).start()

    gather_wide(in_item)
    at_end(end_far, out_items[1])
    at_end(end_near, out_items[0])
    at_inner(inner_across, out_items[0])
    result = total[core]
    gather_pair(in_item)
    for k in near_by:
        low_copy(k).wait_recv()
        result = result + low_in[near_by.index(k)].astype(jnp.float32)
    low = result.astype(jnp.bfloat16)
    gathered(in_item)
    at_inner(inner_back, out_items[0])
    in_rows = items[in_item][2]
    for part in range(2):
        for owner in range(PLANE):
            j = part * PLANE + owner
            wide_in[j * in_rows : (j + 1) * in_rows, :] = final[in_item][owner, part].astype(
                jnp.float32
            )

    half = HEAD_SIZE // 2
    query_rows = ADAPTER_RANK * QH
    kinds = 2 * KEYVALUE_HEADS
    for j in range(kinds):
        first = ADAPTER_RANK * (1 if j < KEYVALUE_HEADS else 2)
        delta = adapter_scale * jnp.dot(
            low[:, first : first + ADAPTER_RANK],
            wide_in[pl.ds(query_rows + j, ADAPTER_RANK, stride=kinds), :].astype(jnp.bfloat16),
            preferred_element_type=jnp.float32
        )
        base_ref = key_ref if j < KEYVALUE_HEADS else value_ref
        head = j % KEYVALUE_HEADS
        if j < KEYVALUE_HEADS:
            swapped = jnp.concatenate([delta[:, half:], delta[:, :half]], axis=1)
            delta = delta * cos_ref[...] + swapped * sin_ref[...]
        base = base_ref[:, head * HEAD_SIZE : (head + 1) * HEAD_SIZE].astype(jnp.float32)
        kv[ctx, :, j * HEAD_SIZE : (j + 1) * HEAD_SIZE] = (base + delta).astype(jnp.bfloat16)

    def query_head(head):
        up = wide_in[pl.ds(head, ADAPTER_RANK, stride=QH), :].astype(jnp.bfloat16)
        delta = adapter_scale * jnp.dot(
            low[:, :ADAPTER_RANK], up, preferred_element_type=jnp.float32
        )
        swapped = jnp.concatenate([delta[:, half:], delta[:, :half]], axis=1)
        delta = delta * cos_ref[...] + swapped * sin_ref[...]
        base = query_ref[:, head * HEAD_SIZE : (head + 1) * HEAD_SIZE].astype(jnp.float32)
        shared = QH // KEYVALUE_HEADS
        queries[
            head // shared, (head % shared) * tokens : (head % shared + 1) * tokens, :
        ] = (base + delta).astype(jnp.bfloat16)

    def keys_up(n):
        place = kv.at[ctx - PLANE * n]
        return remote(place, place, s_keys.at[n, 0], r_keys.at[n + 1, 0], group, ctx + PLANE)

    def keys_copy(n, kind):
        place = kv.at[(ctx ^ (2 if kind == 3 else 0)) - PLANE * n]
        return remote(
            place, place, s_keys.at[n, kind], r_keys.at[n, kind], group, ctx ^ (2 if kind == 1 else 1)
        )

    def keys_kick(n):
        @pl.when(level >= n)
        def _():
            if n > 0:
                place = kv.at[ctx - PLANE * n]
                remote(
                    place, place, s_keys.at[n - 1, 0], r_keys.at[n, 0], group, ctx - PLANE
                ).wait_recv()
            if n < 3:

                @pl.when(level < 3)
                def _():
                    keys_up(n).start()

            keys_copy(n, 1).start()
            keys_copy(n, 2).start()

    def keys_relay(n):
        @pl.when(level >= n)
        def _():
            keys_copy(n, 1).wait_recv()
            keys_copy(n, 3).start()

    def keys_drain(n):
        @pl.when(level >= n)
        def _():
            for kind in (1, 2, 3):
                keys_copy(n, kind).wait_send()
            if n < 3:

                @pl.when(level < 3)
                def _():
                    keys_up(n).wait_send()


    heads = QH // KEYVALUE_HEADS
    rows = heads * tokens
    keys_count = PLANE * tokens
    source_lane = lax.broadcasted_iota(jnp.int32, (HEAD_SIZE, HEAD_SIZE), 0)
    target_lane = lax.broadcasted_iota(jnp.int32, (HEAD_SIZE, HEAD_SIZE), 1)
    wanted = jnp.where(target_lane < half, 2 * target_lane, 2 * (target_lane - half) + 1)
    shuffle = jnp.where(source_lane == wanted, 1.0, 0.0).astype(jnp.bfloat16)
    factor = HEAD_SIZE ** (-0.5) * math.log2(math.e)

    def attend_block(n):
        @pl.when(level >= n)
        def _():
            keys_copy(n, 2).wait_recv()
            keys_copy(n, 3).wait_recv()
            first = PLANE * (level - n)
            for head in range(KEYVALUE_HEADS):
                keys = kv[pl.ds(first, PLANE), :, head * HEAD_SIZE : (head + 1) * HEAD_SIZE]
                value_first = (KEYVALUE_HEADS + head) * HEAD_SIZE
                values = kv[pl.ds(first, PLANE), :, value_first : value_first + HEAD_SIZE]
                keys = keys.reshape(keys_count, HEAD_SIZE)
                values = values.reshape(keys_count, HEAD_SIZE)
                scores = lax.dot_general(
                    queries[head], keys, (((1,), (1,)), ((), ())), preferred_element_type=jnp.float32
                )
                if n == 0:
                    query_pos = lane * tokens + lax.rem(
                        lax.broadcasted_iota(jnp.int32, (rows, keys_count), 0), tokens
                    )
                    key_pos = lax.broadcasted_iota(jnp.int32, (rows, keys_count), 1)
                    scores = jnp.where(query_pos >= key_pos, scores, mask_floor)
                top = jnp.max(scores, axis=1, keepdims=True)
                if n > 0:
                    top = jnp.maximum(top, run_max[head])
                weights = jnp.exp2((scores - top) * factor)
                norm = jnp.sum(weights, axis=1, keepdims=True)
                summed = jnp.dot(
                    weights.astype(jnp.bfloat16), values, preferred_element_type=jnp.float32
                )
                if n > 0:
                    rescale = jnp.exp2((run_max[head] - top) * factor)
                    norm = norm + run_sum[head] * rescale
                    summed = summed + run_acc[head] * rescale
                run_max[head] = top
                run_sum[head] = norm
                run_acc[head] = summed

    keys_kick(0)
    at_end(end_near, out_items[1])
    at_inner(inner_across, out_items[1])
    at_inner(inner_settle, out_items[0])
    for head in range(QH // 4):
        query_head(head)
    keys_relay(0)
    at_end(end_settle, out_items[0])
    keys_kick(1)
    at_inner(inner_back, out_items[1])
    for head in range(QH // 4, QH // 2):
        query_head(head)
    gather_wide(out_items[0])
    keys_relay(1)
    keys_kick(2)
    for head in range(QH // 2, QH):
        query_head(head)
    at_inner(inner_settle, out_items[1])
    at_end(end_settle, out_items[1])
    attend_block(0)
    keys_relay(2)
    keys_kick(3)
    gather_wide(out_items[1])
    gather_pair(out_items[0])
    attend_block(1)
    keys_relay(3)
    attend_block(2)
    gather_pair(out_items[1])
    attend_block(3)
    for head in range(KEYVALUE_HEADS):
        attended = (run_acc[head] / run_sum[head]).astype(jnp.bfloat16)
        mixed = jnp.dot(attended, shuffle, preferred_element_type=jnp.float32).astype(jnp.bfloat16)
        for j in range(heads):
            place = slice((head * heads + j) * HEAD_SIZE, (head * heads + j + 1) * HEAD_SIZE)
            attended_ref[:, place] = attended[j * tokens : (j + 1) * tokens]
            permuted[:, place] = mixed[j * tokens : (j + 1) * tokens]
    gathered(out_items[0])
    gathered(out_items[1])

    unit = items[out_items[0]][2]
    raise_start = QH * half

    def out_unit(n):
        j, chunk = n // OUT_CHUNKS, n % OUT_CHUNKS
        return final[out_items[chunk]].at[j % PLANE, j // PLANE]

    units = 2 * PLANE * OUT_CHUNKS
    for n in range(units):
        low_row = max(n * unit, raise_start)
        high_row = (n + 1) * unit
        if high_row > low_row:
            wide_out[low_row - raise_start : high_row - raise_start, :] = out_unit(n)[
                low_row - n * unit : unit, :
            ].astype(jnp.float32)
    narrow = jnp.zeros((tokens, ADAPTER_RANK), jnp.float32)
    for head in range(QH):
        begin = head * half
        block = out_unit(begin // unit)[begin % unit : begin % unit + half, :]
        weight = jnp.concatenate([block[:, :half], block[:, half:]], axis=0)
        narrow = narrow + jnp.dot(
            permuted[:, head * HEAD_SIZE : (head + 1) * HEAD_SIZE],
            weight,
            preferred_element_type=jnp.float32,
        )
    narrow = narrow.astype(jnp.bfloat16)
    blocks = D // LANES
    for j in range(blocks):
        up = wide_out[pl.ds(j, ADAPTER_RANK, stride=blocks), :].astype(jnp.bfloat16)
        delta_ref[:, j * LANES : (j + 1) * LANES] = (
            adapter_scale * jnp.dot(narrow, up, preferred_element_type=jnp.float32)
        ).astype(jnp.bfloat16)

    row_copy.wait_send()
    for i in range(count):
        for k in range(1, PLANE):
            plane_copy(i, k).wait_send()
        if i >= in_item:
            for kind in (CROSS, WIDE, PAIR, PAIR2):
                move(i, kind).wait_send()
    for k in near_by:
        low_copy(k).wait_send()
    for n in range(4):
        keys_drain(n)

    @pl.when(is_end)
    def _():
        for i in range(count):
            move(i, FAR).wait_send()
            if i not in end_items:
                move(i, NEAR).wait_send()
            if i in end_items:
                move(i, CROSS).wait_send()
                move(i, WIDE).wait_send()
        for k in near_by:
            for n in range(4):
                acts_copy(n, k, k < PLANE).wait_send()

    @pl.when(is_inner)
    def _():
        for i in range(count):
            move(i, MID).wait_send()
            if i not in inner_items:
                move(i, BACK).wait_send()
            if i in inner_items:
                move(i, CROSS).wait_send()
                move(i, WIDE).wait_send()
        for k in near_by:
            for n in range(4):
                acts_copy(n, k, k >= PLANE).wait_send()


def deliver_kernel(attended_ref, delta_ref, attended_out, delta_out, sems):
    copies = [
        pltpu.make_async_copy(attended_ref, attended_out, sems.at[0]),
        pltpu.make_async_copy(delta_ref, delta_out, sems.at[1]),
    ]
    for copy in copies:
        copy.start()
    for copy in copies:
        copy.wait()


def deliver(attended, delta):
    return pl.pallas_call(
        deliver_kernel,
        out_shape=tuple(jax.ShapeDtypeStruct(a.shape, a.dtype) for a in (attended, delta)),
        in_specs=[ON_CHIP, ON_CHIP],
        out_specs=(ANYWHERE, ANYWHERE),
        scratch_shapes=[pltpu.SemaphoreType.DMA((2,))],
        compiler_params=pltpu.CompilerParams(vmem_limit_bytes=56 * 1024 * 1024),
    )(attended, delta)


def fused(owner, stretch, x, pool, query_rows, key_rows, value_rows, cosine, sine):
    items = item_table(2 * PLANE)
    tokens = x.shape[0]
    bf16 = jnp.bfloat16
    f32 = jnp.float32
    dma = pltpu.SemaphoreType.DMA
    vmem = pltpu.VMEM
    count = len(items)
    sizes = [rows for _, _, rows in items]

    def each(*lead):
        return [vmem(lead + (rows, LANES), bf16) for rows in sizes]

    down_rows, in_rows, out_rows = section_rows()
    final = [
        vmem(((2, 2) if i < DOWN_CHUNKS else (PLANE, 2)) + (rows, LANES), bf16)
        for i, rows in enumerate(sizes)
    ]
    end_width = D // (2 * PLANE) * (DOWN_CHUNKS - INNER_CHUNKS) // DOWN_CHUNKS
    heads = QH // KEYVALUE_HEADS
    kv_columns = 2 * KEYVALUE_HEADS * HEAD_SIZE
    devices = 4 * PLANE
    scratch = [
        [vmem((PLANE, 1, rows * LANES), bf16) for rows in sizes],
        each(PLANE),
        each(PLANE),
        each(2),
        each(2),
        each(2),
        each(2),
        each(2),
        each(),
        final,
        vmem((4, PLANE, tokens, end_width), bf16),
        vmem((sizes[0], LANES), f32),
        vmem((2 * sizes[0] // 3, LANES), f32),
        vmem((2 * sizes[0] // 3, LANES), f32),
        vmem((4, end_width, 2 * LANES), bf16),
        vmem((PLANE, tokens, 2 * LANES), f32),
        vmem((PLANE, tokens, 2 * LANES), bf16),
        vmem((3, tokens, 2 * LANES), bf16),
        vmem((in_rows, LANES), f32),
        vmem((ADAPTER_RANK * D // LANES, LANES), f32),
        vmem((KEYVALUE_HEADS, heads * tokens, HEAD_SIZE), bf16),
        vmem((devices, tokens, kv_columns), bf16),
        vmem((tokens, QH * HEAD_SIZE), bf16),
        vmem((KEYVALUE_HEADS, heads * tokens, 1), f32),
        vmem((KEYVALUE_HEADS, heads * tokens, 1), f32),
        vmem((KEYVALUE_HEADS, heads * tokens, HEAD_SIZE), f32),
        vmem((1, LANES), jnp.int32),
        vmem((1, LANES), jnp.int32),
        pltpu.SMEM((2, 1, LANES), jnp.int32),
        dma((count, PLANE)),
        dma((count, PLANE)),
        dma((count, PLANE)),
        dma((count, 8)),
        dma((count, 8)),
        dma((4, 2 * PLANE)),
        dma((4, 2 * PLANE)),
        dma((4,)),
        dma,
        dma,
        dma((2,)),
        dma((2 * PLANE,)),
        dma((2 * PLANE,)),
        dma((4, 4)),
        dma((4, 4)),
    ]
    return pl.pallas_call(
        partial(fused_kernel, items),
        out_shape=(
            jax.ShapeDtypeStruct((tokens, QH * HEAD_SIZE), bf16),
            jax.ShapeDtypeStruct((tokens, D), bf16),
        ),
        in_specs=[SCALARS, SCALARS, ANYWHERE, ANYWHERE] + [ON_CHIP] * 5,
        out_specs=(ON_CHIP, ON_CHIP),
        scratch_shapes=scratch,
        compiler_params=pltpu.CompilerParams(
            collective_id=2, has_side_effects=True, vmem_limit_bytes=60 * 1024 * 1024
        ),
    )(owner, stretch, x, pool, query_rows, key_rows, value_rows, cosine, sine)


def shards(
    normed_input, query_base, key_base, value_base, adapter_pool, stretch_adapter, adapter_owner
):
    cycle_size = lax.axis_size("ctx")
    my_index = lax.axis_index("ctx")
    tok_rows = normed_input.shape[0]
    token_positions = my_index * tok_rows + jnp.arange(tok_rows, dtype=jnp.int32)
    groups = lax.axis_size("groups")
    cube = BLOCK_TOKENS // tok_rows
    cubes = cycle_size // cube
    down_size = 3 * ADAPTER_RANK * D
    half_dim = HEAD_SIZE // 2
    frequency = rope_base ** (-(jnp.arange(half_dim, dtype=jnp.float32) * 2.0) / HEAD_SIZE)
    angle = token_positions.astype(jnp.float32)[:, None] * frequency[None, :]
    cosine = jnp.cos(angle)
    sine = jnp.sin(angle)
    cosine = jnp.concatenate([cosine, cosine], axis=1)
    sine = jnp.concatenate([-sine, sine], axis=1)
    if groups == 2 and cube == 2 * PLANE and cubes == 2:
        return deliver(*fused(
            adapter_owner, stretch_adapter, normed_input, adapter_pool,
            query_base, key_base, value_base, cosine, sine,
        ))
    padding = -stretch_adapter.shape[0] % LANES
    stretch_row = jnp.pad(stretch_adapter, (0, padding))[None]
    moved, down_slice, rest = place_adapter(
        groups, cubes, cube, down_size, adapter_owner, stretch_row, normed_input, adapter_pool
    )
    rest = rest.reshape(-1, LANES)
    queries, gathered = keyval(
        cube,
        cycle_size,
        moved,
        down_slice.reshape(D // cube, 3 * ADAPTER_RANK),
        rest,
        query_base,
        key_base,
        value_base,
        cosine,
        sine,
    )
    gathered = gathered.reshape(cycle_size * tok_rows, -1)
    return attend(queries, gathered, rest)


def solution(mesh):
    placed = (
        P(("groups", "ctx"), None),
        P(("groups", "ctx"), None),
        P(("groups", "ctx"), None),
        P(("groups", "ctx"), None),
        P("ctx", None),
        P("groups"),
        P(),
    )
    return jax.shard_map(
        shards,
        mesh=mesh,
        in_specs=placed,
        out_specs=(P(("groups", "ctx"), None), P(("groups", "ctx"), None)),
        check_vma=False,
    )
```

```python
from functools import partial
import math

import jax
import jax.numpy as jnp
from jax import lax
from jax.experimental import pallas as pl
from jax.experimental.pallas import tpu as pltpu
from jax.sharding import PartitionSpec as P

D = 8192
QH = 32
KEYVALUE_HEADS = 4
HEAD_SIZE = 128
ADAPTER_RANK = 64
BLOCK_TOKENS = 512
QKV_POOL = 1900544


adapter_scale = 2.0
rope_base = 500000.0
mask_floor = -1e30


LANES = 128
MESH = pl.DeviceIdType.MESH
ON_CHIP = pl.BlockSpec(memory_space=pltpu.VMEM)
ANYWHERE = pl.BlockSpec(memory_space=pl.ANY)
SCALARS = pl.BlockSpec(memory_space=pltpu.SMEM)


def remote(src, dst, send_sem, recv_sem, group, ctx):
    return pltpu.make_async_remote_copy(
        src_ref=src,
        dst_ref=dst,
        send_sem=send_sem,
        recv_sem=recv_sem,
        device_id=(group, ctx),
        device_id_type=MESH,
    )


def place_adapter_kernel(
    groups, cubes, cube, down_size,
    owner_ref, stretch_ref, x_ref, pool_ref,
    x_out, down_out, rest_out,
    down_flat, rest_flat, down_source, rest_source,
    down_rows, rest_rows, down_send, rest_send, down_land, rest_land,
    stretch_land, table,
    s_flat, s_cube, r_cube, s_far, r_far, s_tree, r_tree, s_own, s_row, r_row, s_table,
):
    group = lax.axis_index("groups")
    ctx = lax.axis_index("ctx")
    inner = ctx % cube
    outer = ctx // cube
    home = group * cubes + outer
    kinds = groups * cubes
    width = x_out.shape[2] // groups
    down_piece = down_flat.shape[2]
    rest_piece = rest_flat.shape[2]

    def read_piece(row, k):
        piece = (rest_piece, down_piece)[row]
        start = (group * cube + (inner ^ k)) * piece + (down_size, 0)[row]
        return pltpu.make_async_copy(
            pool_ref.at[:, pl.ds(pl.multiple_of(start, LANES), piece)],
            (rest_flat, down_flat)[row].at[k],
            s_flat.at[row, k],
        )

    for row in range(2):
        for k in reversed(range(cube)):
            read_piece(row, k).start()

    barrier = pltpu.get_barrier_semaphore()
    for k in range(1, cube):
        pl.semaphore_signal(
            barrier, inc=1, device_id=(group, outer * cube + (inner ^ k)), device_id_type=MESH
        )
    for k in range(1, kinds):
        there = home ^ k
        pl.semaphore_signal(
            barrier,
            inc=1,
            device_id=(there // cubes, (there % cubes) * cube + inner),
            device_id_type=MESH,
        )
    pl.semaphore_wait(barrier, cube - 1 + kinds - 1)
    row_copies = []
    for step in range(1, groups):
        copy = remote(
            stretch_ref, stretch_land.at[step], s_row.at[step], r_row.at[step], group ^ step, ctx
        )
        copy.start()
        row_copies.append(copy)

    def columns(part, owner):
        return pl.ds(pl.multiple_of((part * cube + owner) * width, width), width)

    def cube_copy(row, k):
        peer = inner ^ k
        return remote(
            (rest_source, down_source)[row].at[k], (rest_rows, down_rows)[row].at[inner],
            s_cube.at[row, k], r_cube.at[row, k], group, outer * cube + peer,
        )

    def dense(row, k):
        flat = (rest_flat, down_flat)[row][k].astype(jnp.float32)
        return flat.reshape(-1, LANES).astype(jnp.bfloat16)

    def x_copy(part, k):
        peer = inner ^ k
        return remote(
            x_ref.at[:, columns(part, peer)],
            x_out.at[inner, :, pl.ds(part * width, width)],
            s_cube.at[2 + part, k], r_cube.at[2 + part, k],
            group, outer * cube + peer,
        )

    for row, (source, rows) in enumerate(((rest_source, rest_rows), (down_source, down_rows))):

        def spread(step, carry, row=row, source=source):
            k = cube - 1 - step
            read_piece(row, k).wait()
            source[k] = dense(row, k)
            cube_copy(row, k).start()
            return carry

        lax.fori_loop(0, cube - 1, spread, 0)
        read_piece(row, 0).wait()
        rows[inner] = dense(row, 0)

    to_table = [pltpu.make_async_copy(stretch_ref, table.at[0], s_table.at[0])]
    to_table[0].start()
    for step, copy in zip(range(1, groups), row_copies):
        copy.wait_recv()
        move = pltpu.make_async_copy(stretch_land.at[step], table.at[step], s_table.at[step])
        move.start()
        to_table.append(move)
    for move in to_table:
        move.wait()

    def slot_of(k):
        return owner_ref[table[k // cubes, 0, outer ^ (k % cubes)]]

    def chosen(part):
        return (part * cubes + lax.div(slot_of(0), cube)) ^ home

    owns = []
    for part in range(groups):
        own = pltpu.make_async_copy(
            x_ref.at[:, columns(part, inner)],
            x_out.at[inner, :, pl.ds(part * width, width)],
            s_own.at[part],
        )
        own.start()
        owns.append(own)

    far = []
    for row, (rows, outgoing, landing) in enumerate(
        ((rest_rows, rest_send, rest_land), (down_rows, down_send, down_land))
    ):
        for k in range(1, cube):
            cube_copy(row, k).wait_recv()
        coming = []
        for k in range(1, kinds):
            there = home ^ k
            outgoing[k] = rows[lax.rem(slot_of(k), cube)]
            copy = remote(
                outgoing.at[k], landing.at[k], s_far.at[row, k], r_far.at[row, k],
                there // cubes, (there % cubes) * cube + inner,
            )
            copy.start()
            coming.append(copy)
        landing[0] = rows[lax.rem(slot_of(0), cube)]
        far.append(coming)

    for copy in far[0]:
        copy.wait_recv()
    for part in range(groups):
        rest_out[part, inner] = rest_land[chosen(part)]
    tree = {}
    have = [[0] for _ in range(groups)]
    levels = cube.bit_length() - 1
    orders = []
    for part in range(groups):
        order = [1 << level for level in reversed(range(levels))]
        if part % 2:
            order[:2] = order[1::-1]
        orders.append(order)
    for stage in range(levels):
        for part in range(groups):
            bit = orders[part][stage]
            before = orders[part][stage - 1] if stage else 0
            for k in have[part]:
                if k & before:
                    tree[k, part].wait_recv()
            new = []
            for k in have[part]:
                slot = rest_out.at[part, inner ^ k]
                copy = remote(
                    slot, slot, s_tree.at[part, k ^ bit], r_tree.at[part, k ^ bit],
                    group, outer * cube + (inner ^ bit),
                )
                copy.start()
                tree[k ^ bit, part] = copy
                new.append(k ^ bit)
            have[part] = have[part] + new
        if stage == 0:
            for part in range(groups):
                for k in reversed(range(1, cube)):
                    x_copy(part, k).start()

    for copy in far[1]:
        copy.wait_recv()
    for part in range(groups):
        down_out[part] = down_land[chosen(part)]
    for (k, part), copy in tree.items():
        if k & orders[part][-1]:
            copy.wait_recv()
    for own in owns:
        own.wait()
    for part in range(groups):
        for k in range(1, cube):
            x_copy(part, k).wait_recv()
            x_copy(part, k).wait_send()
    for row in range(2):
        for k in range(1, cube):
            cube_copy(row, k).wait_send()
    for copy in row_copies + far[0] + far[1] + list(tree.values()):
        copy.wait_send()


def place_adapter(groups, cubes, cube, down_size, owner, stretch_row, x, pool):
    kinds = groups * cubes
    tokens, depth = x.shape
    down_piece = down_size // (groups * cube)
    rest_piece = (pool.shape[1] - down_size) // (groups * cube)
    down_shape = (down_piece // LANES, LANES)
    rest_shape = (rest_piece // LANES, LANES)
    bf16 = jnp.bfloat16
    dma = pltpu.SemaphoreType.DMA
    return pl.pallas_call(
        partial(place_adapter_kernel, groups, cubes, cube, down_size),
        out_shape=(
            jax.ShapeDtypeStruct((cube, tokens, depth // cube), bf16),
            jax.ShapeDtypeStruct((groups,) + down_shape, bf16),
            jax.ShapeDtypeStruct((groups, cube) + rest_shape, bf16),
        ),
        in_specs=[SCALARS, ON_CHIP, ON_CHIP, pl.BlockSpec(memory_space=pl.ANY)],
        out_specs=(ON_CHIP, ON_CHIP, ON_CHIP),
        scratch_shapes=[
            pltpu.VMEM((cube, 1, down_piece), bf16),
            pltpu.VMEM((cube, 1, rest_piece), bf16),
            pltpu.VMEM((cube,) + down_shape, bf16),
            pltpu.VMEM((cube,) + rest_shape, bf16),
            pltpu.VMEM((cube,) + down_shape, bf16),
            pltpu.VMEM((cube,) + rest_shape, bf16),
            pltpu.VMEM((kinds,) + down_shape, bf16),
            pltpu.VMEM((kinds,) + rest_shape, bf16),
            pltpu.VMEM((kinds,) + down_shape, bf16),
            pltpu.VMEM((kinds,) + rest_shape, bf16),
            pltpu.VMEM((groups,) + stretch_row.shape, jnp.int32),
            pltpu.SMEM((groups,) + stretch_row.shape, jnp.int32),
            dma((2, cube)),
            dma((2 + groups, cube)),
            dma((2 + groups, cube)),
            dma((2, kinds)),
            dma((2, kinds)),
            dma((groups, cube)),
            dma((groups, cube)),
            dma((groups,)),
            dma((groups,)),
            dma((groups,)),
            dma((groups,)),
        ],
        compiler_params=pltpu.CompilerParams(
            collective_id=0, has_side_effects=True, vmem_limit_bytes=60 * 1024 * 1024
        ),
    )(owner, stretch_row, x, pool)


def keyval_kernel(
    cube, count,
    x_any, w_ref, rest_any, query_ref, key_ref, value_ref, cos_ref, sin_ref,
    query_out, out_ref,
    x_ref, up_ref, s_in, wide, total, outgoing, landing, s_sem, r_sem, s_all, r_all,
):
    group = lax.axis_index("groups")
    ctx = lax.axis_index("ctx")
    inner = ctx % cube
    outer = ctx // cube
    levels = count.bit_length() - 1
    x_in = pltpu.make_async_copy(x_any, x_ref, s_in.at[0])
    x_in.start()
    up_in = pltpu.make_async_copy(
        rest_any.at[pl.ds(0, up_ref.shape[0])], up_ref, s_in.at[1]
    )
    up_in.start()
    barrier = pltpu.get_barrier_semaphore()
    apart = list(range(1, cube)) + [1 << n for n in range(levels) if 1 << n >= cube]
    for k in apart:
        pl.semaphore_signal(barrier, inc=1, device_id=(group, ctx ^ k), device_id_type=MESH)
    _, tokens, depth = x_ref.shape
    x_in.wait()
    product = jnp.dot(
        x_ref[...].reshape(cube * tokens, depth), w_ref[...], preferred_element_type=jnp.float32
    ).reshape(cube, tokens, w_ref.shape[1])
    total[...] = product
    outgoing[...] = product.astype(jnp.bfloat16)
    pl.semaphore_wait(barrier, len(apart))
    copies = []
    for k in range(1, cube):
        peer = inner ^ k
        copy = remote(
            outgoing.at[peer], landing.at[k], s_sem.at[k], r_sem.at[k], group, outer * cube + peer
        )
        copy.start()
        copies.append(copy)
    up_in.wait()
    wide[...] = up_ref[...].astype(jnp.float32)
    result = total[inner]
    for k, copy in zip(range(1, cube), copies):
        copy.wait_recv()
        result = result + landing[k].astype(jnp.float32)
    low = result.astype(jnp.bfloat16)
    half = HEAD_SIZE // 2
    query_rows = ADAPTER_RANK * QH
    kinds = 2 * KEYVALUE_HEADS
    for j in range(2 * KEYVALUE_HEADS):
        first = ADAPTER_RANK * (1 if j < KEYVALUE_HEADS else 2)
        delta = adapter_scale * jnp.dot(
            low[:, first : first + ADAPTER_RANK],
            wide[pl.ds(query_rows + j, ADAPTER_RANK, stride=kinds), :].astype(jnp.bfloat16),
            preferred_element_type=jnp.float32
        )
        base_ref = key_ref if j < KEYVALUE_HEADS else value_ref
        head = j % KEYVALUE_HEADS
        if j < KEYVALUE_HEADS:
            swapped = jnp.concatenate([delta[:, half:], delta[:, :half]], axis=1)
            delta = delta * cos_ref[...] + swapped * sin_ref[...]
        base = base_ref[:, head * HEAD_SIZE : (head + 1) * HEAD_SIZE].astype(jnp.float32)
        out_ref[ctx, :, j * HEAD_SIZE : (j + 1) * HEAD_SIZE] = (base + delta).astype(jnp.bfloat16)

    def query_head(head):
        up = wide[pl.ds(head, ADAPTER_RANK, stride=QH), :].astype(jnp.bfloat16)
        delta = adapter_scale * jnp.dot(
            low[:, :ADAPTER_RANK], up, preferred_element_type=jnp.float32
        )
        swapped = jnp.concatenate([delta[:, half:], delta[:, :half]], axis=1)
        delta = delta * cos_ref[...] + swapped * sin_ref[...]
        base = query_ref[:, head * HEAD_SIZE : (head + 1) * HEAD_SIZE].astype(jnp.float32)
        shared = QH // KEYVALUE_HEADS
        query_out[
            head // shared, (head % shared) * tokens : (head % shared + 1) * tokens, :
        ] = (base + delta).astype(jnp.bfloat16)

    kv_width = KEYVALUE_HEADS * HEAD_SIZE
    far_first = [1 << level for level in reversed(range(levels))]
    orders = (far_first, [2] + [bit for bit in far_first if bit != 2])
    have = [[0], [0]]
    moved = {}
    done = 0
    for stage in range(levels):
        for part in range(2):
            bit = orders[part][stage]
            before = orders[part][stage - 1] if stage else 0
            new = []
            for k in have[part]:
                if k & before:
                    moved[k, part].wait_recv()
                slot = out_ref.at[ctx ^ k, :, pl.ds(part * kv_width, kv_width)]
                copy = remote(
                    slot, slot, s_all.at[part, k ^ bit], r_all.at[part, k ^ bit], group, ctx ^ bit
                )
                copy.start()
                moved[k ^ bit, part] = copy
                new.append(k ^ bit)
            have[part] = have[part] + new
        until = QH * (stage + 1) // levels
        for head in range(done, until):
            query_head(head)
        done = until
    for (k, part), copy in moved.items():
        if k & orders[part][-1]:
            copy.wait_recv()
    for copy in copies + list(moved.values()):
        copy.wait_send()


def keyval(cube, count, x, w, rest, query_rows, key_rows, value_rows, cosine, sine):
    _, tokens, _ = x.shape
    shape = (cube, tokens, w.shape[1])
    up_rows = ADAPTER_RANK * (QH + 2 * KEYVALUE_HEADS)
    dma = pltpu.SemaphoreType.DMA
    return pl.pallas_call(
        partial(keyval_kernel, cube, count),
        out_shape=(
            jax.ShapeDtypeStruct(
                (KEYVALUE_HEADS, QH // KEYVALUE_HEADS * tokens, HEAD_SIZE), jnp.bfloat16
            ),
            jax.ShapeDtypeStruct(
                (count, tokens, 2 * KEYVALUE_HEADS * HEAD_SIZE), jnp.bfloat16
            ),
        ),
        in_specs=[ANYWHERE, ON_CHIP, ANYWHERE] + [ON_CHIP] * 5,
        out_specs=(ON_CHIP, ON_CHIP),
        scratch_shapes=[
            pltpu.VMEM(x.shape, jnp.bfloat16),
            pltpu.VMEM((up_rows, LANES), jnp.bfloat16),
            dma((2,)),
            pltpu.VMEM((up_rows, LANES), jnp.float32),
            pltpu.VMEM(shape, jnp.float32),
            pltpu.VMEM(shape, jnp.bfloat16),
            pltpu.VMEM(shape, jnp.bfloat16),
            dma((cube,)),
            dma((cube,)),
            dma((2, count)),
            dma((2, count)),
        ],
        compiler_params=pltpu.CompilerParams(
            collective_id=1, has_side_effects=True, vmem_limit_bytes=40 * 1024 * 1024
        ),
    )(x, w, rest, query_rows, key_rows, value_rows, cosine, sine)


def attend_kernel(
    step_keys, queries, kv_ref, rest_any,
    attended_ref, delta_ref,
    rest_ref, s_in, wide, permuted, run_max, run_sum, run_acc,
):
    tokens = attended_ref.shape[0]
    ctx = lax.axis_index("ctx")
    heads = QH // KEYVALUE_HEADS
    rows = heads * tokens
    half = HEAD_SIZE // 2
    query_rows = ADAPTER_RANK * QH
    raise_start = QH * half
    rest_in = pltpu.make_async_copy(
        rest_any.at[pl.ds(query_rows + 2 * ADAPTER_RANK * KEYVALUE_HEADS, rest_ref.shape[0])],
        rest_ref,
        s_in,
    )
    rest_in.start()
    first = ctx * tokens
    steps = (first + tokens + step_keys - 1) // step_keys
    row = lax.broadcasted_iota(jnp.int32, (rows, step_keys), 0)
    query_pos = first + lax.rem(row, tokens)
    key_off = lax.broadcasted_iota(jnp.int32, (rows, step_keys), 1)
    source = lax.broadcasted_iota(jnp.int32, (HEAD_SIZE, HEAD_SIZE), 0)
    target = lax.broadcasted_iota(jnp.int32, (HEAD_SIZE, HEAD_SIZE), 1)
    wanted = jnp.where(target < half, 2 * target, 2 * (target - half) + 1)
    shuffle = jnp.where(source == wanted, 1.0, 0.0).astype(jnp.bfloat16)
    for group in range(KEYVALUE_HEADS):
        run_max[...] = jnp.full_like(run_max, mask_floor)
        run_sum[...] = jnp.zeros_like(run_sum)
        run_acc[...] = jnp.zeros_like(run_acc)
        key_cols = slice(group * HEAD_SIZE, (group + 1) * HEAD_SIZE)
        value_first = (KEYVALUE_HEADS + group) * HEAD_SIZE

        def advance(step, carry):
            start = pl.multiple_of(step * step_keys, step_keys)
            keys = kv_ref[pl.ds(start, step_keys), key_cols]
            values = kv_ref[pl.ds(start, step_keys), value_first : value_first + HEAD_SIZE]
            scores = lax.dot_general(
                queries[group], keys, (((1,), (1,)), ((), ())),
                preferred_element_type=jnp.float32,
            ) * HEAD_SIZE ** (-0.5)
            scores = jnp.where(query_pos >= key_off + start, scores, mask_floor)
            new_max = jnp.maximum(run_max[...], jnp.max(scores, axis=1, keepdims=True))
            weights = jnp.exp(scores - new_max)
            rescale = jnp.exp(run_max[...] - new_max)
            run_sum[...] = run_sum[...] * rescale + jnp.sum(weights, axis=1, keepdims=True)
            run_acc[...] = run_acc[...] * rescale + jnp.dot(
                weights.astype(jnp.bfloat16), values, preferred_element_type=jnp.float32
            )
            run_max[...] = new_max
            return carry

        lax.fori_loop(0, steps, advance, 0)
        result = (run_acc[...] / run_sum[...]).astype(jnp.bfloat16)
        mixed = jnp.dot(result, shuffle, preferred_element_type=jnp.float32).astype(jnp.bfloat16)
        for j in range(heads):
            head = group * heads + j
            cols = slice(head * HEAD_SIZE, (head + 1) * HEAD_SIZE)
            attended_ref[:, cols] = result[j * tokens : (j + 1) * tokens]
            permuted[:, cols] = mixed[j * tokens : (j + 1) * tokens]
    rest_in.wait()
    wide[...] = rest_ref[raise_start:, :].astype(jnp.float32)
    narrow = jnp.zeros((tokens, ADAPTER_RANK), jnp.float32)
    for head in range(QH):
        block = rest_ref[head * half : (head + 1) * half, :]
        weight = jnp.concatenate([block[:, :half], block[:, half:]], axis=0)
        narrow = narrow + jnp.dot(
            permuted[:, head * HEAD_SIZE : (head + 1) * HEAD_SIZE],
            weight,
            preferred_element_type=jnp.float32,
        )
    narrow = narrow.astype(jnp.bfloat16)
    blocks = D // LANES
    for j in range(blocks):
        up = wide[pl.ds(j, ADAPTER_RANK, stride=blocks), :].astype(jnp.bfloat16)
        delta_ref[:, j * LANES : (j + 1) * LANES] = (
            adapter_scale * jnp.dot(narrow, up, preferred_element_type=jnp.float32)
        ).astype(jnp.bfloat16)


def attend(queries, kv, rest):
    rows = queries.shape[1]
    tokens = rows // (QH // KEYVALUE_HEADS)
    out_rows = ADAPTER_RANK * (QH * HEAD_SIZE + D) // LANES
    return pl.pallas_call(
        partial(attend_kernel, math.gcd(kv.shape[0], 1024)),
        out_shape=(
            jax.ShapeDtypeStruct((tokens, QH * HEAD_SIZE), jnp.bfloat16),
            jax.ShapeDtypeStruct((tokens, D), jnp.bfloat16),
        ),
        in_specs=[ON_CHIP, ON_CHIP, ANYWHERE],
        out_specs=(ON_CHIP, ON_CHIP),
        scratch_shapes=[
            pltpu.VMEM((out_rows, LANES), jnp.bfloat16),
            pltpu.SemaphoreType.DMA,
            pltpu.VMEM((ADAPTER_RANK * D // LANES, LANES), jnp.float32),
            pltpu.VMEM((tokens, QH * HEAD_SIZE), jnp.bfloat16),
            pltpu.VMEM((rows, 1), jnp.float32),
            pltpu.VMEM((rows, 1), jnp.float32),
            pltpu.VMEM((rows, HEAD_SIZE), jnp.float32),
        ],
        compiler_params=pltpu.CompilerParams(vmem_limit_bytes=56 * 1024 * 1024),
    )(queries, kv, rest)


PLANE = 4
DOWN_CHUNKS = 8
INNER_CHUNKS = 2
EARLY_CHUNKS = 3
OUT_CHUNKS = 2
FAR, NEAR, MID, BACK, CROSS, WIDE, PAIR, PAIR2 = range(8)


def section_rows():
    down = 3 * ADAPTER_RANK * D // LANES
    inner = ADAPTER_RANK * (QH + 2 * KEYVALUE_HEADS) * HEAD_SIZE // LANES
    outer = ADAPTER_RANK * (QH * HEAD_SIZE + D) // LANES
    return down, inner, outer


def item_table(slices):
    items = []
    first = 0
    for rows, chunks in zip(section_rows(), (DOWN_CHUNKS, 1, OUT_CHUNKS)):
        piece = rows // slices
        for chunk in range(chunks):
            items.append((first + chunk * (piece // chunks), piece, piece // chunks))
        first += rows
    return items


def fused_kernel(
    items,
    owner_ref, stretch_ref, x_any, pool_any, query_ref, key_ref, value_ref, cos_ref, sin_ref,
    attended_ref, delta_ref,
    flat, source, held, first_out, second_out, far_in, near_in, mid_in, cross_out, final,
    acts, spread_w, packed_a, packed_b, weights, total, low_out, low_in, wide_in, wide_out, queries, kv, permuted,
    run_max, run_sum, run_acc, row_out, row_in, table,
    s_flat, s_plane, r_plane, s_move, r_move, s_acts, r_acts, s_own, s_row, r_row, s_table,
    s_low, r_low, s_keys, r_keys,
):
    group = lax.axis_index("groups")
    ctx = lax.axis_index("ctx")
    lane = ctx % PLANE
    side = lane // 2
    core = lane % 2
    level = ctx // PLANE
    half_of = level // 2
    is_end = (level == 0) | (level == 3)
    is_inner = (level == 1) | (level == 2)
    tokens = x_any.shape[0]
    count = len(items)
    down_items = list(range(DOWN_CHUNKS))
    in_item = DOWN_CHUNKS
    end_items = down_items[:-INNER_CHUNKS]
    inner_items = down_items[-INNER_CHUNKS:]
    order = down_items[:EARLY_CHUNKS] + [in_item] + down_items[EARLY_CHUNKS:]
    out_items = list(range(DOWN_CHUNKS + 1, count))

    def read_piece(i, k):
        first, piece, rows = items[i]
        begin = (first + (group * PLANE + (lane ^ k)) * piece) * LANES
        return pltpu.make_async_copy(
            pool_any.at[:, pl.ds(pl.multiple_of(begin, LANES), rows * LANES)],
            flat[i].at[k],
            s_flat.at[i, k],
        )

    for i in range(count):
        for k in reversed(range(PLANE)):
            read_piece(i, k).start()

    def dense(i, k):
        return flat[i][k].astype(jnp.float32).reshape(-1, LANES).astype(jnp.bfloat16)

    def prepare(i):
        def step(n, carry):
            k = PLANE - 1 - n
            read_piece(i, k).wait()
            source[i][k] = dense(i, k)
            return carry

        lax.fori_loop(0, PLANE - 1, step, 0)
        read_piece(i, 0).wait()
        held[i][lane] = dense(i, 0)

    barrier = pltpu.get_barrier_semaphore()
    greeted = (1, 2, 3, 4, 5, 8, 12)
    for k in greeted:
        pl.semaphore_signal(barrier, inc=1, device_id=(group, ctx ^ k), device_id_type=MESH)
    pl.semaphore_signal(barrier, inc=1, device_id=(group ^ 1, ctx), device_id_type=MESH)
    mine_row = lax.broadcasted_iota(jnp.int32, row_out.shape, 1)
    row_out[...] = jnp.where(mine_row == 0, stretch_ref[0], stretch_ref[1])
    for i in order[:2]:
        prepare(i)
    pl.semaphore_wait(barrier, len(greeted) + 1)

    row_copy = remote(row_out, row_in, s_row, r_row, group ^ 1, ctx)
    row_copy.start()
    own_row = pltpu.make_async_copy(row_out, table.at[0], s_table.at[0])
    own_row.start()

    def plane_copy(i, k):
        return remote(
            source[i].at[k], held[i].at[lane], s_plane.at[i, k], r_plane.at[i, k], group, ctx ^ k
        )

    def scatter(i):
        for k in reversed(range(1, PLANE)):
            plane_copy(i, k).start()

    def slot(which, part):
        return owner_ref[table[which, 0, part]]

    def mine(which, part, where):
        return lax.div(slot(which, part), PLANE) == where

    def own_candidate(i, which, part):
        return held[i][lax.rem(slot(which, part), PLANE)]

    def move(i, kind):
        if kind == FAR:
            src, dst, there = first_out[i], far_in[i], (group, ctx ^ PLANE)
        elif kind == NEAR:
            src, dst, there = second_out[i], near_in[i], (group, ctx ^ PLANE)
        elif kind == MID:
            src, dst, there = first_out[i], mid_in[i], (group, ctx ^ (3 * PLANE))
        elif kind == BACK:
            src, dst, there = second_out[i], far_in[i], (group, ctx ^ PLANE)
        elif kind == CROSS:
            place = final[i].at[side, group] if i < in_item else final[i].at[lane, group]
            src, dst, there = cross_out[i], place, (group ^ 1, ctx)
        elif kind == WIDE:
            src = dst = final[i].at[side if i < in_item else lane]
            there = (group, ctx ^ 2)
        elif kind == PAIR:
            src = dst = final[i].at[lane]
            there = (group, ctx ^ 1)
        else:
            src = dst = final[i].at[lane ^ 2]
            there = (group, ctx ^ 1)
        return remote(src, dst, s_move.at[i, kind], r_move.at[i, kind], *there)

    def landed(i):
        for k in range(1, PLANE):
            plane_copy(i, k).wait_recv()

    def end_far(i):
        landed(i)
        for which in range(2):
            first_out[i][which] = own_candidate(i, which, 1 - half_of)
        move(i, FAR).start()

    def end_near(i):
        for which in range(2):
            second_out[i][which] = own_candidate(i, which, half_of)
        move(i, NEAR).start()

    def end_send(i):
        end_far(i)
        if i not in end_items:
            end_near(i)

    def settle(i, other_value, own_value):
        cross_out[i][...] = other_value
        move(i, CROSS).start()
        if i < in_item:
            final[i][side, group] = own_value
        else:
            final[i][lane, group] = own_value

    def end_settle(i):
        move(i, BACK).wait_recv()

        def value(which):
            return jnp.where(
                mine(which, half_of, level), own_candidate(i, which, half_of), far_in[i][which]
            )

        settle(i, value(1), value(0))

    def inner_across(i):
        landed(i)
        move(i, FAR).wait_recv()
        for which in range(2):
            first_out[i][which] = jnp.where(
                mine(which, 1 - half_of, level),
                own_candidate(i, which, 1 - half_of),
                far_in[i][which],
            )
        move(i, MID).start()

    def inner_back(i):
        move(i, MID).wait_recv()
        for which in range(2):
            second_out[i][which] = jnp.where(
                mine(which, half_of, level),
                own_candidate(i, which, half_of),
                mid_in[i][which],
            )
        if i not in inner_items:
            move(i, BACK).start()

    def inner_settle(i):
        move(i, NEAR).wait_recv()

        def value(which):
            return jnp.where(
                mine(which, half_of, level ^ 1), near_in[i][which], second_out[i][which]
            )

        settle(i, value(1), value(0))

    def gather_wide(i):
        move(i, CROSS).wait_recv()
        move(i, WIDE).start()
        move(i, PAIR).start()

    def gather_pair(i):
        move(i, WIDE).wait_recv()
        move(i, PAIR2).start()

    def gathered(i):
        move(i, PAIR).wait_recv()
        move(i, PAIR2).wait_recv()

    strip = D // (2 * PLANE)
    inner_width = strip * INNER_CHUNKS // DOWN_CHUNKS
    end_width = strip - inner_width

    near_by = (1, PLANE, PLANE + 1)

    def member(k):
        return k // PLANE * 2 + (core ^ (k % 2))

    def acts_copy(n, k, to_end):
        width = end_width if to_end else inner_width
        part, wing = n // 2, n % 2
        begin = (part * PLANE + wing * 2 + (core ^ (k % 2))) * strip + (0 if to_end else end_width)
        src = x_any.at[:, pl.ds(pl.multiple_of(begin, LANES), width)]
        dst = acts.at[n, k // PLANE * 2 + core, :, pl.ds(0, width)]
        if k == 0:
            return pltpu.make_async_copy(src, dst, s_own.at[n])
        return remote(src, dst, s_acts.at[n, k], r_acts.at[n, k], group, ctx ^ k)

    def acts_send():
        @pl.when(is_end)
        def _():
            for k in (PLANE, PLANE + 1, 1, 0):
                for n in range(4):
                    acts_copy(n, k, k < PLANE).start()

        @pl.when(is_inner)
        def _():
            for k in (PLANE, PLANE + 1, 1, 0):
                for n in range(4):
                    acts_copy(n, k, k >= PLANE).start()

    def acts_landed(to_end):
        for n in range(4):
            acts_copy(n, 0, to_end).wait()
            for k in near_by:
                acts_copy(n, k, to_end).wait_recv()

    def widen(i):
        move(i, CROSS).wait_recv()
        move(i, WIDE).start()

    def convert(i):
        move(i, WIDE).wait_recv()
        pairs = 2 * final[i].shape[2] // 3
        third = pairs // 2
        half = LANES // 2
        row = (i - (inner_items[0] if i in inner_items else 0)) * pairs
        for n in range(4):
            part, wing = n // 2, n % 2
            spread_w[...] = final[i][wing, part].astype(jnp.float32)
            first = spread_w[pl.ds(0, third, stride=3), :]
            second = spread_w[pl.ds(1, third, stride=3), :]
            last = spread_w[pl.ds(2, third, stride=3), :]
            packed_a[pl.ds(0, third, stride=2), :] = first
            packed_b[pl.ds(0, third, stride=2), :] = second
            packed_a[pl.ds(1, third, stride=2), :] = jnp.concatenate(
                [second[:, half:], last[:, :half]], axis=1
            )
            packed_b[pl.ds(1, third, stride=2), :] = jnp.concatenate(
                [last[:, half:], last[:, :half]], axis=1
            )
            weights[n, row : row + pairs, 0:LANES] = packed_a[...].astype(jnp.bfloat16)
            weights[n, row : row + pairs, LANES : 2 * LANES] = packed_b[...].astype(jnp.bfloat16)

    def product(width):
        sum_now = None
        for n in range(4):
            chunk = acts[n, :, :, 0:width].reshape(PLANE * tokens, width)
            term = jnp.dot(chunk, weights[n, 0:width, :], preferred_element_type=jnp.float32)
            sum_now = term if sum_now is None else sum_now + term
        total[...] = sum_now.reshape(PLANE, tokens, 2 * LANES)

    acts_send()
    scatter(order[0])
    scatter(order[1])
    for i in order[2:]:
        prepare(i)
        scatter(i)
    row_copy.wait_recv()
    own_row.wait()
    other_row = pltpu.make_async_copy(row_in, table.at[1], s_table.at[1])
    other_row.start()
    other_row.wait()
    for i in out_items:
        prepare(i)
    lag = 4
    steps = len(order)

    def at(n):
        return order[n] if 0 <= n < steps else None

    @pl.when(is_end)
    def _():
        for n in range(steps + lag + 2):
            if at(n) is not None:
                end_send(at(n))
            if at(n - lag) is not None and at(n - lag) not in inner_items:
                end_settle(at(n - lag))
            if at(n - lag - 1) in end_items:
                widen(at(n - lag - 1))
                if at(n - lag - 1) == end_items[-4]:
                    scatter(out_items[0])
            if at(n - lag - 2) in end_items:
                convert(at(n - lag - 2))
        scatter(out_items[1])
        acts_landed(True)
        product(end_width)
        end_far(out_items[0])

    @pl.when(is_inner)
    def _():
        for i in out_items:
            scatter(i)
        for n in range(steps + 4):
            if at(n) is not None:
                inner_across(at(n))
            if at(n - 1) is not None:
                inner_back(at(n - 1))
            if at(n - 2) is not None and at(n - 2) not in end_items:
                inner_settle(at(n - 2))
            if at(n - 3) in inner_items:
                widen(at(n - 3))
            if at(n - 4) in inner_items:
                convert(at(n - 4))
        acts_landed(False)
        product(inner_width)

    def at_inner(step, i):
        @pl.when(is_inner)
        def _():
            step(i)

    def at_end(step, i):
        @pl.when(is_end)
        def _():
            step(i)

    def low_copy(k):
        return remote(
            low_out.at[member(k)], low_in.at[near_by.index(k)],
            s_low.at[k], r_low.at[k], group, ctx ^ k,
        )

    low_out[...] = total[...].astype(jnp.bfloat16)
    for k in near_by[1:] + near_by[:1]:
        low_copy(k).start()

    gather_wide(in_item)
    at_end(end_far, out_items[1])
    at_end(end_near, out_items[0])
    at_inner(inner_across, out_items[0])
    result = total[core]
    gather_pair(in_item)
    for k in near_by:
        low_copy(k).wait_recv()
        result = result + low_in[near_by.index(k)].astype(jnp.float32)
    low = result.astype(jnp.bfloat16)
    gathered(in_item)
    at_inner(inner_back, out_items[0])
    in_rows = items[in_item][2]
    for part in range(2):
        for owner in range(PLANE):
            j = part * PLANE + owner
            wide_in[j * in_rows : (j + 1) * in_rows, :] = final[in_item][owner, part].astype(
                jnp.float32
            )

    half = HEAD_SIZE // 2
    query_rows = ADAPTER_RANK * QH
    kinds = 2 * KEYVALUE_HEADS
    for j in range(kinds):
        first = ADAPTER_RANK * (1 if j < KEYVALUE_HEADS else 2)
        delta = adapter_scale * jnp.dot(
            low[:, first : first + ADAPTER_RANK],
            wide_in[pl.ds(query_rows + j, ADAPTER_RANK, stride=kinds), :].astype(jnp.bfloat16),
            preferred_element_type=jnp.float32
        )
        base_ref = key_ref if j < KEYVALUE_HEADS else value_ref
        head = j % KEYVALUE_HEADS
        if j < KEYVALUE_HEADS:
            swapped = jnp.concatenate([delta[:, half:], delta[:, :half]], axis=1)
            delta = delta * cos_ref[...] + swapped * sin_ref[...]
        base = base_ref[:, head * HEAD_SIZE : (head + 1) * HEAD_SIZE].astype(jnp.float32)
        kv[ctx, :, j * HEAD_SIZE : (j + 1) * HEAD_SIZE] = (base + delta).astype(jnp.bfloat16)

    def query_head(head):
        up = wide_in[pl.ds(head, ADAPTER_RANK, stride=QH), :].astype(jnp.bfloat16)
        delta = adapter_scale * jnp.dot(
            low[:, :ADAPTER_RANK], up, preferred_element_type=jnp.float32
        )
        swapped = jnp.concatenate([delta[:, half:], delta[:, :half]], axis=1)
        delta = delta * cos_ref[...] + swapped * sin_ref[...]
        base = query_ref[:, head * HEAD_SIZE : (head + 1) * HEAD_SIZE].astype(jnp.float32)
        shared = QH // KEYVALUE_HEADS
        queries[
            head // shared, (head % shared) * tokens : (head % shared + 1) * tokens, :
        ] = (base + delta).astype(jnp.bfloat16)

    def keys_up(n):
        place = kv.at[ctx - PLANE * n]
        return remote(place, place, s_keys.at[n, 0], r_keys.at[n + 1, 0], group, ctx + PLANE)

    def keys_copy(n, kind):
        place = kv.at[(ctx ^ (2 if kind == 3 else 0)) - PLANE * n]
        return remote(
            place, place, s_keys.at[n, kind], r_keys.at[n, kind], group, ctx ^ (2 if kind == 1 else 1)
        )

    def keys_kick(n):
        @pl.when(level >= n)
        def _():
            if n > 0:
                place = kv.at[ctx - PLANE * n]
                remote(
                    place, place, s_keys.at[n - 1, 0], r_keys.at[n, 0], group, ctx - PLANE
                ).wait_recv()
            if n < 3:

                @pl.when(level < 3)
                def _():
                    keys_up(n).start()

            keys_copy(n, 1).start()
            keys_copy(n, 2).start()

    def keys_relay(n):
        @pl.when(level >= n)
        def _():
            keys_copy(n, 1).wait_recv()
            keys_copy(n, 3).start()

    def keys_drain(n):
        @pl.when(level >= n)
        def _():
            for kind in (1, 2, 3):
                keys_copy(n, kind).wait_send()
            if n < 3:

                @pl.when(level < 3)
                def _():
                    keys_up(n).wait_send()


    heads = QH // KEYVALUE_HEADS
    rows = heads * tokens
    keys_count = PLANE * tokens
    source_lane = lax.broadcasted_iota(jnp.int32, (HEAD_SIZE, HEAD_SIZE), 0)
    target_lane = lax.broadcasted_iota(jnp.int32, (HEAD_SIZE, HEAD_SIZE), 1)
    wanted = jnp.where(target_lane < half, 2 * target_lane, 2 * (target_lane - half) + 1)
    shuffle = jnp.where(source_lane == wanted, 1.0, 0.0).astype(jnp.bfloat16)
    factor = HEAD_SIZE ** (-0.5) * math.log2(math.e)

    def attend_block(n):
        @pl.when(level >= n)
        def _():
            keys_copy(n, 2).wait_recv()
            keys_copy(n, 3).wait_recv()
            first = PLANE * (level - n)
            for head in range(KEYVALUE_HEADS):
                keys = kv[pl.ds(first, PLANE), :, head * HEAD_SIZE : (head + 1) * HEAD_SIZE]
                value_first = (KEYVALUE_HEADS + head) * HEAD_SIZE
                values = kv[pl.ds(first, PLANE), :, value_first : value_first + HEAD_SIZE]
                keys = keys.reshape(keys_count, HEAD_SIZE)
                values = values.reshape(keys_count, HEAD_SIZE)
                scores = lax.dot_general(
                    queries[head], keys, (((1,), (1,)), ((), ())), preferred_element_type=jnp.float32
                )
                if n == 0:
                    query_pos = lane * tokens + lax.rem(
                        lax.broadcasted_iota(jnp.int32, (rows, keys_count), 0), tokens
                    )
                    key_pos = lax.broadcasted_iota(jnp.int32, (rows, keys_count), 1)
                    scores = jnp.where(query_pos >= key_pos, scores, mask_floor)
                top = jnp.max(scores, axis=1, keepdims=True)
                if n > 0:
                    top = jnp.maximum(top, run_max[head])
                weights = jnp.exp2((scores - top) * factor)
                norm = jnp.sum(weights, axis=1, keepdims=True)
                summed = jnp.dot(
                    weights.astype(jnp.bfloat16), values, preferred_element_type=jnp.float32
                )
                if n > 0:
                    rescale = jnp.exp2((run_max[head] - top) * factor)
                    norm = norm + run_sum[head] * rescale
                    summed = summed + run_acc[head] * rescale
                run_max[head] = top
                run_sum[head] = norm
                run_acc[head] = summed

    keys_kick(0)
    at_end(end_near, out_items[1])
    at_inner(inner_across, out_items[1])
    at_inner(inner_settle, out_items[0])
    for head in range(QH // 4):
        query_head(head)
    keys_relay(0)
    at_end(end_settle, out_items[0])
    keys_kick(1)
    at_inner(inner_back, out_items[1])
    for head in range(QH // 4, QH // 2):
        query_head(head)
    gather_wide(out_items[0])
    keys_relay(1)
    keys_kick(2)
    for head in range(QH // 2, QH):
        query_head(head)
    at_inner(inner_settle, out_items[1])
    at_end(end_settle, out_items[1])
    attend_block(0)
    keys_relay(2)
    keys_kick(3)
    gather_wide(out_items[1])
    gather_pair(out_items[0])
    attend_block(1)
    keys_relay(3)
    attend_block(2)
    gather_pair(out_items[1])
    attend_block(3)
    for head in range(KEYVALUE_HEADS):
        attended = (run_acc[head] / run_sum[head]).astype(jnp.bfloat16)
        mixed = jnp.dot(attended, shuffle, preferred_element_type=jnp.float32).astype(jnp.bfloat16)
        for j in range(heads):
            place = slice((head * heads + j) * HEAD_SIZE, (head * heads + j + 1) * HEAD_SIZE)
            attended_ref[:, place] = attended[j * tokens : (j + 1) * tokens]
            permuted[:, place] = mixed[j * tokens : (j + 1) * tokens]
    gathered(out_items[0])
    gathered(out_items[1])

    unit = items[out_items[0]][2]
    raise_start = QH * half

    def out_unit(n):
        j, chunk = n // OUT_CHUNKS, n % OUT_CHUNKS
        return final[out_items[chunk]].at[j % PLANE, j // PLANE]

    units = 2 * PLANE * OUT_CHUNKS
    for n in range(units):
        low_row = max(n * unit, raise_start)
        high_row = (n + 1) * unit
        if high_row > low_row:
            wide_out[low_row - raise_start : high_row - raise_start, :] = out_unit(n)[
                low_row - n * unit : unit, :
            ].astype(jnp.float32)
    narrow = jnp.zeros((tokens, ADAPTER_RANK), jnp.float32)
    for head in range(QH):
        begin = head * half
        block = out_unit(begin // unit)[begin % unit : begin % unit + half, :]
        weight = jnp.concatenate([block[:, :half], block[:, half:]], axis=0)
        narrow = narrow + jnp.dot(
            permuted[:, head * HEAD_SIZE : (head + 1) * HEAD_SIZE],
            weight,
            preferred_element_type=jnp.float32,
        )
    narrow = narrow.astype(jnp.bfloat16)
    blocks = D // LANES
    for j in range(blocks):
        up = wide_out[pl.ds(j, ADAPTER_RANK, stride=blocks), :].astype(jnp.bfloat16)
        delta_ref[:, j * LANES : (j + 1) * LANES] = (
            adapter_scale * jnp.dot(narrow, up, preferred_element_type=jnp.float32)
        ).astype(jnp.bfloat16)

    row_copy.wait_send()
    for i in range(count):
        for k in range(1, PLANE):
            plane_copy(i, k).wait_send()
        if i >= in_item:
            for kind in (CROSS, WIDE, PAIR, PAIR2):
                move(i, kind).wait_send()
    for k in near_by:
        low_copy(k).wait_send()
    for n in range(4):
        keys_drain(n)

    @pl.when(is_end)
    def _():
        for i in range(count):
            move(i, FAR).wait_send()
            if i not in end_items:
                move(i, NEAR).wait_send()
            if i in end_items:
                move(i, CROSS).wait_send()
                move(i, WIDE).wait_send()
        for k in near_by:
            for n in range(4):
                acts_copy(n, k, k < PLANE).wait_send()

    @pl.when(is_inner)
    def _():
        for i in range(count):
            move(i, MID).wait_send()
            if i not in inner_items:
                move(i, BACK).wait_send()
            if i in inner_items:
                move(i, CROSS).wait_send()
                move(i, WIDE).wait_send()
        for k in near_by:
            for n in range(4):
                acts_copy(n, k, k >= PLANE).wait_send()


def deliver_kernel(attended_ref, delta_ref, attended_out, delta_out, sems):
    copies = [
        pltpu.make_async_copy(attended_ref, attended_out, sems.at[0]),
        pltpu.make_async_copy(delta_ref, delta_out, sems.at[1]),
    ]
    for copy in copies:
        copy.start()
    for copy in copies:
        copy.wait()


def deliver(attended, delta):
    return pl.pallas_call(
        deliver_kernel,
        out_shape=tuple(jax.ShapeDtypeStruct(a.shape, a.dtype) for a in (attended, delta)),
        in_specs=[ON_CHIP, ON_CHIP],
        out_specs=(ANYWHERE, ANYWHERE),
        scratch_shapes=[pltpu.SemaphoreType.DMA((2,))],
        compiler_params=pltpu.CompilerParams(vmem_limit_bytes=56 * 1024 * 1024),
    )(attended, delta)


def fused(owner, stretch, x, pool, query_rows, key_rows, value_rows, cosine, sine):
    items = item_table(2 * PLANE)
    tokens = x.shape[0]
    bf16 = jnp.bfloat16
    f32 = jnp.float32
    dma = pltpu.SemaphoreType.DMA
    vmem = pltpu.VMEM
    count = len(items)
    sizes = [rows for _, _, rows in items]

    def each(*lead):
        return [vmem(lead + (rows, LANES), bf16) for rows in sizes]

    down_rows, in_rows, out_rows = section_rows()
    final = [
        vmem(((2, 2) if i < DOWN_CHUNKS else (PLANE, 2)) + (rows, LANES), bf16)
        for i, rows in enumerate(sizes)
    ]
    end_width = D // (2 * PLANE) * (DOWN_CHUNKS - INNER_CHUNKS) // DOWN_CHUNKS
    heads = QH // KEYVALUE_HEADS
    kv_columns = 2 * KEYVALUE_HEADS * HEAD_SIZE
    devices = 4 * PLANE
    scratch = [
        [vmem((PLANE, 1, rows * LANES), bf16) for rows in sizes],
        each(PLANE),
        each(PLANE),
        each(2),
        each(2),
        each(2),
        each(2),
        each(2),
        each(),
        final,
        vmem((4, PLANE, tokens, end_width), bf16),
        vmem((sizes[0], LANES), f32),
        vmem((2 * sizes[0] // 3, LANES), f32),
        vmem((2 * sizes[0] // 3, LANES), f32),
        vmem((4, end_width, 2 * LANES), bf16),
        vmem((PLANE, tokens, 2 * LANES), f32),
        vmem((PLANE, tokens, 2 * LANES), bf16),
        vmem((3, tokens, 2 * LANES), bf16),
        vmem((in_rows, LANES), f32),
        vmem((ADAPTER_RANK * D // LANES, LANES), f32),
        vmem((KEYVALUE_HEADS, heads * tokens, HEAD_SIZE), bf16),
        vmem((devices, tokens, kv_columns), bf16),
        vmem((tokens, QH * HEAD_SIZE), bf16),
        vmem((KEYVALUE_HEADS, heads * tokens, 1), f32),
        vmem((KEYVALUE_HEADS, heads * tokens, 1), f32),
        vmem((KEYVALUE_HEADS, heads * tokens, HEAD_SIZE), f32),
        vmem((1, LANES), jnp.int32),
        vmem((1, LANES), jnp.int32),
        pltpu.SMEM((2, 1, LANES), jnp.int32),
        dma((count, PLANE)),
        dma((count, PLANE)),
        dma((count, PLANE)),
        dma((count, 8)),
        dma((count, 8)),
        dma((4, 2 * PLANE)),
        dma((4, 2 * PLANE)),
        dma((4,)),
        dma,
        dma,
        dma((2,)),
        dma((2 * PLANE,)),
        dma((2 * PLANE,)),
        dma((4, 4)),
        dma((4, 4)),
    ]
    return pl.pallas_call(
        partial(fused_kernel, items),
        out_shape=(
            jax.ShapeDtypeStruct((tokens, QH * HEAD_SIZE), bf16),
            jax.ShapeDtypeStruct((tokens, D), bf16),
        ),
        in_specs=[SCALARS, SCALARS, ANYWHERE, ANYWHERE] + [ON_CHIP] * 5,
        out_specs=(ON_CHIP, ON_CHIP),
        scratch_shapes=scratch,
        compiler_params=pltpu.CompilerParams(
            collective_id=2, has_side_effects=True, vmem_limit_bytes=60 * 1024 * 1024
        ),
    )(owner, stretch, x, pool, query_rows, key_rows, value_rows, cosine, sine)


def shards(
    normed_input, query_base, key_base, value_base, adapter_pool, stretch_adapter, adapter_owner
):
    cycle_size = lax.axis_size("ctx")
    my_index = lax.axis_index("ctx")
    tok_rows = normed_input.shape[0]
    token_positions = my_index * tok_rows + jnp.arange(tok_rows, dtype=jnp.int32)
    groups = lax.axis_size("groups")
    cube = BLOCK_TOKENS // tok_rows
    cubes = cycle_size // cube
    down_size = 3 * ADAPTER_RANK * D
    half_dim = HEAD_SIZE // 2
    frequency = rope_base ** (-(jnp.arange(half_dim, dtype=jnp.float32) * 2.0) / HEAD_SIZE)
    angle = token_positions.astype(jnp.float32)[:, None] * frequency[None, :]
    cosine = jnp.cos(angle)
    sine = jnp.sin(angle)
    cosine = jnp.concatenate([cosine, cosine], axis=1)
    sine = jnp.concatenate([-sine, sine], axis=1)
    if groups == 2 and cube == 2 * PLANE and cubes == 2:
        return deliver(*fused(
            adapter_owner, stretch_adapter, normed_input, adapter_pool,
            query_base, key_base, value_base, cosine, sine,
        ))
    padding = -stretch_adapter.shape[0] % LANES
    stretch_row = jnp.pad(stretch_adapter, (0, padding))[None]
    moved, down_slice, rest = place_adapter(
        groups, cubes, cube, down_size, adapter_owner, stretch_row, normed_input, adapter_pool
    )
    rest = rest.reshape(-1, LANES)
    queries, gathered = keyval(
        cube,
        cycle_size,
        moved,
        down_slice.reshape(D // cube, 3 * ADAPTER_RANK),
        rest,
        query_base,
        key_base,
        value_base,
        cosine,
        sine,
    )
    gathered = gathered.reshape(cycle_size * tok_rows, -1)
    return attend(queries, gathered, rest)


def solution(mesh):
    placed = (
        P(("groups", "ctx"), None),
        P(("groups", "ctx"), None),
        P(("groups", "ctx"), None),
        P(("groups", "ctx"), None),
        P("ctx", None),
        P("groups"),
        P(),
    )
    return jax.shard_map(
        shards,
        mesh=mesh,
        in_specs=placed,
        out_specs=(P(("groups", "ctx"), None), P(("groups", "ctx"), None)),
        check_vma=False,
    )
```
